32 devices in a mesh: ctx: 8 (over y, x, core), shard: 4 (over z).
Axes of the slice: x: 2, y: 2, z: 4, core: 2. Of those that a mesh axis runs over, the one named last changes fastest.
Arguments:
- hidden_in: bfloat16 [8, 1024, 768], P('shard', 'ctx'), may hold values from -6 to 6
- block_of: int32 [16], replicated, may hold values from 0 to 15, each once
- lengths: int32 [8], replicated, may hold values from 256 to 1024, as said below
- attn_latent: float32 [4, 768, 768], P(None, 'shard'), may hold values from -1.25 to 1.25
- ffn_in_latent: float32 [768, 3072], P('shard'), may hold values from -1.25 to 1.25
- ffn_out_latent: float32 [3072, 768], P('shard'), may hold values from -1.25 to 1.25
- student_vec: float32 [12, 768], replicated
- teacher_attn: bfloat16 [4, 768, 768], P(None, 'shard'), may hold values from -0.3125 to 0.3125
- teacher_ffn_in: bfloat16 [768, 3072], P('shard'), may hold values from -0.21875 to 0.21875
- teacher_ffn_out: bfloat16 [3072, 768], P('shard'), may hold values from -0.109375 to 0.109375
- teacher_vec: float32 [12, 768], replicated
Outputs:
- output: bfloat16 [8, 1024, 768], P('shard', 'ctx')
- statistics: float32 [4], replicated
- grad_hidden: float32 [8, 1024, 768], P('shard', 'ctx')
- grad_attn_latent: float32 [4, 768, 768], P(None, 'shard')
- grad_ffn_in_latent: float32 [768, 3072], P('shard')
- grad_ffn_out_latent: float32 [3072, 768], P('shard')
- grad_student_vec: float32 [11, 768], replicated
- grad_query_bias: float32 [768], replicated
The draws below stay inside these ranges and needn't reach their ends.
Inputs may be any that keep to these rules, and one draw needn't show every extreme that they name: `block_of`: every block of 64 places of a sequence is named once; entry q holds the block that lies at layout places q * 64 to (q + 1) * 64 - 1, the same for every sequence. `lengths`: A token is valid where its place is below its sequence's length; some sequence has length 1024.
All inputs are finite; a program needn't handle non-finite values.
Results may differ from the reference program's by a relative error of at most 0.0097.
Values may be sent and summed in bfloat16 or wider, within the bound.
No kernel may reach another device: no remote copies, remote signals or barrier semaphores. Data moves between devices by JAX's collectives and lax.ppermute only.
A program may use at most 320 MiB of HBM per device.

```python
import jax
import jax.numpy as jnp
from jax import lax

D = 768
HEADS = 12
HEAD_DIM = 64
FF = 3072
BLK = 64
LEN = 1024
SEQS = 8
N_CTX = 8


def vector_table(table_key):
    rows_total = 8 + FF // D
    base_draw = jax.random.normal(table_key, (rows_total, D), jnp.float32)
    row_index = jnp.arange(rows_total)[:, None]
    is_gain = (row_index == 4) | (row_index == 6)
    return jnp.where(is_gain, 1.0 + 0.1 * base_draw, 0.3 * base_draw)


def draw_student_vec(key, part):
    return vector_table(jax.random.fold_in(key, 11))


def draw_teacher_vec(key, part):
    return vector_table(jax.random.fold_in(key, 12))


def draw_lengths(key, part):
    first_key, second_key = jax.random.split(jax.random.fold_in(key, 13))
    drawn = jax.random.randint(first_key, (SEQS,), LEN // 4, LEN + 1, dtype=jnp.int32)
    longest = jax.random.randint(second_key, (), 0, SEQS, dtype=jnp.int32)
    return jnp.where(jnp.arange(SEQS, dtype=jnp.int32) == longest, LEN, drawn).astype(jnp.int32)


def block_levels(stream_key, extent, pieces, least, largest):
    loudness, own = 1.0, jax.random.fold_in(stream_key, 6)
    for dim, blocks in pieces:
        draws = jnp.exp(jax.random.uniform(jax.random.fold_in(own, dim), (blocks,), jnp.float32, least / len(pieces), largest / len(pieces)))
        loudness = loudness * jnp.repeat(draws, extent[dim] // blocks).reshape([-1 if axis == dim else 1 for axis in range(len(extent))])
    return loudness


def noise(own_key, shape, deviation, limit, pieces=(), held_as=jnp.bfloat16):
    level = block_levels(own_key, shape, pieces, -0.22, 0.18) if pieces else 1.0
    result = jax.random.normal(own_key, shape, jnp.float32) * deviation * level
    return jnp.minimum(jnp.maximum(result, -limit), limit).astype(held_as)


def setup_inputs(seed: int = 0) -> dict:
    arg_keys = jax.random.split(jax.random.key(seed), 12)
    hidden_in = noise(arg_keys[0], (SEQS, LEN, D), 1.0, 6.0, ((0, 4), (1, 8)))
    block_of = jax.random.permutation(arg_keys[1], 2 * N_CTX).astype(jnp.int32)
    lengths = draw_lengths(jax.random.fold_in(arg_keys[11], 71), 0)
    attn_latent = jnp.clip(jax.random.uniform(arg_keys[3], (4, D, D), jnp.float32, -1.25, 1.25) * block_levels(arg_keys[3], (4, D, D), ((1, 4),), -0.4, 0.0), -1.25, 1.25)
    ffn_in_latent = jnp.clip(jax.random.uniform(arg_keys[4], (D, FF), jnp.float32, -1.25, 1.25) * block_levels(arg_keys[4], (D, FF), ((0, 4),), -0.4, 0.0), -1.25, 1.25)
    ffn_out_latent = jnp.clip(jax.random.uniform(arg_keys[5], (FF, D), jnp.float32, -1.25, 1.25) * block_levels(arg_keys[5], (FF, D), ((0, 4),), -0.4, 0.0), -1.25, 1.25)
    student_vec = draw_student_vec(jax.random.fold_in(arg_keys[11], 71), 0)
    teacher_attn = noise(arg_keys[7], (4, D, D), (D // 2) ** -0.5, 0.3125, ((1, 4),))
    teacher_ffn_in = noise(arg_keys[8], (D, FF), D ** -0.5, 0.21875, ((0, 4),))
    teacher_ffn_out = noise(arg_keys[9], (FF, D), FF ** -0.5, 0.109375, ((0, 4),))
    teacher_vec = draw_teacher_vec(jax.random.fold_in(arg_keys[11], 71), 0)
    return dict(hidden_in=hidden_in, block_of=block_of, lengths=lengths, attn_latent=attn_latent, ffn_in_latent=ffn_in_latent, ffn_out_latent=ffn_out_latent, student_vec=student_vec, teacher_attn=teacher_attn, teacher_ffn_in=teacher_ffn_in, teacher_ffn_out=teacher_ffn_out, teacher_vec=teacher_vec)


@jax.custom_vjp
def low(v):
    return lax.optimization_barrier(v.astype(jnp.bfloat16)).astype(jnp.float32)

@jax.custom_vjp
def low_back(v):
    return v

def low_keep(v):
    return (low(v), None)

def low_pass(kept, grad):
    return (grad,)

def back_keep(v):
    return (v, None)

def back_low(kept, grad):
    return (low(grad),)
low.defvjp(low_keep, low_pass)
low_back.defvjp(back_keep, back_low)
norm_eps = 1e-05
attn_gains = (2.0, 2.0, 1.0, 4.0)

def product(left_side, right_side):
    return jnp.dot(left_side, right_side, precision=lax.Precision.HIGHEST, preferred_element_type=jnp.float32)

def layer_norm(values, gain, shift):
    middle = lax.optimization_barrier(jnp.mean(values, axis=-1, keepdims=True))
    centred = values - middle
    spread = lax.optimization_barrier(jnp.mean(centred * centred, axis=-1, keepdims=True))
    return centred * lax.rsqrt(spread + norm_eps) * gain + shift

def binarize(latent, gain, fan_in):
    column_mean = lax.optimization_barrier(jnp.mean(jnp.abs(latent), axis=-2, keepdims=True))
    return low(gain * column_mean * jnp.sign(latent) * fan_in ** (-0.5))

def attend_sequence(query_rows, key_rows, value_rows, positions):
    block_rows = min(512, LEN)
    query_blocks = query_rows.reshape(LEN // block_rows, block_rows, HEADS, HEAD_DIM)
    place_blocks = positions.reshape(LEN // block_rows, block_rows)
    key_heads = key_rows.reshape(LEN, HEADS, HEAD_DIM)
    value_heads = value_rows.reshape(LEN, HEADS, HEAD_DIM)

    def one_block(block_item):
        query_block, place_block = block_item
        scores = jnp.einsum('qhd,khd->hqk', query_block, key_heads, precision=lax.Precision.HIGHEST) * HEAD_DIM ** (-0.5)
        scores = low_back(scores)
        allowed = place_block[:, None] >= positions[None, :]
        scores = jnp.where(allowed[None], scores, -1e+30)
        prob_rows = jax.nn.softmax(scores, axis=-1)
        return jnp.einsum('hqk,khd->qhd', low(prob_rows), value_heads, precision=lax.Precision.HIGHEST)
    mixed = lax.map(jax.checkpoint(one_block), (query_blocks, place_blocks))
    return mixed.reshape(LEN, D)

def layer(tokens, weights, vector, positions):
    w_query, w_key, w_value, w_out, w_in, w_down = weights
    query_rows = low(low_back(product(tokens, w_query)) + vector[0])
    key_rows = low(low_back(product(tokens, w_key)))
    value_rows = low(low_back(product(tokens, w_value)) + vector[1])
    mixed = attend_sequence(query_rows, key_rows, value_rows, positions)
    heads_out = low(low_back(mixed))
    branch = low_back(product(heads_out, w_out)) + vector[2]
    first_norm = layer_norm(tokens + branch, vector[4], vector[5])
    inner_pre = low_back(product(low(first_norm), w_in)) + vector[8:].reshape(FF)
    activated = low(jax.nn.gelu(inner_pre, approximate=False))
    feed_out = low_back(product(activated, w_down)) + vector[3]
    second_sum = first_norm + feed_out
    return (layer_norm(second_sum, vector[6], vector[7]), branch, feed_out, second_sum)

def reference(hidden_in, block_of, lengths, attn_latent, ffn_in_latent, ffn_out_latent, student_vec, teacher_attn, teacher_ffn_in, teacher_ffn_out, teacher_vec):
    positions = (block_of[:, None] * BLK + jnp.arange(BLK, dtype=jnp.int32)[None, :]).reshape(LEN).astype(jnp.int32)
    valid_count = jnp.sum(lengths.astype(jnp.float32))
    attn_gain = jnp.asarray(attn_gains, dtype=jnp.float32)[:, None, None]
    bin_attn = binarize(attn_latent, attn_gain, D)
    student = (bin_attn[0], bin_attn[1], bin_attn[2], bin_attn[3], binarize(ffn_in_latent, 1.0, D), binarize(ffn_out_latent, 1.0, FF))
    teach_attn = teacher_attn.astype(jnp.float32)
    teacher = (teach_attn[0], teach_attn[1], teach_attn[2], teach_attn[3], teacher_ffn_in.astype(jnp.float32), teacher_ffn_out.astype(jnp.float32))
    tokens_all = hidden_in.astype(jnp.float32)

    def one_sequence(carry_in, seq_item):
        seq_tokens, seq_length = seq_item
        valid_rows = (positions < seq_length).astype(jnp.float32)[:, None]
        target = layer(seq_tokens, teacher, teacher_vec, positions)[0]

        def objective(tokens, w_query, w_key, w_value, w_out, w_in, w_down, vector):
            output, branch, feed_out, second_sum = layer(tokens, (w_query, w_key, w_value, w_out, w_in, w_down), vector, positions)
            mismatch = output - target
            loss_part = 0.5 * jnp.sum(valid_rows * mismatch * mismatch) / (valid_count * D)
            square_sums = jnp.stack([jnp.sum(valid_rows * branch * branch), jnp.sum(valid_rows * feed_out * feed_out), jnp.sum(valid_rows * second_sum * second_sum)])
            return (loss_part, (output, square_sums))
        loss_part, backward, (output, square_sums) = jax.vjp(objective, seq_tokens, *student, student_vec, has_aux=True)
        gradients = backward(jnp.ones_like(loss_part))
        carry_out = jax.tree.map(jnp.add, carry_in, (tuple(gradients[1:]), loss_part, square_sums))
        return (carry_out, (output, gradients[0]))
    start_grads = tuple((jnp.zeros_like(weight_one) for weight_one in student)) + (jnp.zeros_like(student_vec),)
    start = (start_grads, jnp.zeros((), jnp.float32), jnp.zeros((3,), jnp.float32))
    (weight_grads, loss_total, square_total), (outputs, input_grads) = lax.scan(one_sequence, start, (tokens_all, lengths))
    statistics = jnp.concatenate([loss_total[None], jnp.sqrt(square_total / (valid_count * D))])
    keep_attn = (jnp.abs(attn_latent) <= 1.0).astype(jnp.float32)
    keep_in = (jnp.abs(ffn_in_latent) <= 1.0).astype(jnp.float32)
    keep_out = (jnp.abs(ffn_out_latent) <= 1.0).astype(jnp.float32)
    grad_attn = jnp.stack(weight_grads[0:4]) * keep_attn
    return (outputs.astype(jnp.bfloat16), statistics, input_grads, grad_attn, weight_grads[4] * keep_in, weight_grads[5] * keep_out, weight_grads[6][1:], weight_grads[6][0])
```

```python
import functools

import jax
import jax.numpy as jnp
from jax import lax
from jax.experimental import pallas as pl
from jax.experimental.pallas import tpu as pltpu
from jax.sharding import PartitionSpec as P

D = 768
HEADS = 12
HEAD_DIM = 64
FF = 3072
BLK = 64

CHIPS = 4
CORES = 2
GROUP = CHIPS * CORES
COLS = D // CHIPS
HEADS_HERE = HEADS // CHIPS
UNITS = FF // CHIPS

norm_eps = 1e-05
attn_gains = (2.0, 2.0, 1.0, 4.0)
masked_score = -1e30
score_scale = HEAD_DIM ** (-0.5)
bf16 = jnp.bfloat16
f32 = jnp.float32


def dot(left_side, right_side):
    return jnp.dot(left_side, right_side, preferred_element_type=f32)


def dot_left(left_side, right_side):
    return lax.dot_general(
        left_side, right_side, (((0,), (0,)), ((), ())), preferred_element_type=f32
    )


def dot_right(left_side, right_side):
    return lax.dot_general(
        left_side, right_side, (((1,), (1,)), ((), ())), preferred_element_type=f32
    )


def layer_norm(values, gain, shift):
    middle = jnp.mean(values, axis=-1, keepdims=True)
    centred = values - middle
    spread = jnp.mean(centred * centred, axis=-1, keepdims=True)
    return centred * lax.rsqrt(spread + norm_eps) * gain + shift


def layer_norm_back(values, gain, grad_out):
    middle = jnp.mean(values, axis=-1, keepdims=True)
    centred = values - middle
    spread = jnp.mean(centred * centred, axis=-1, keepdims=True)
    inverse = lax.rsqrt(spread + norm_eps)
    normal = centred * inverse
    scaled = grad_out * gain
    grad_in = (
        scaled
        - jnp.mean(scaled, axis=-1, keepdims=True)
        - normal * jnp.mean(scaled * normal, axis=-1, keepdims=True)
    ) * inverse
    return grad_in, jnp.sum(grad_out * normal, axis=0), jnp.sum(grad_out, axis=0)


def normal_cdf(values):
    return 0.5 * (1.0 + lax.erf(values * 0.7071067811865476))


def tree_sum(items):
    while len(items) > 1:
        items = [items[i] + items[i + 1] for i in range(0, len(items), 2)]
    return items[0]


def attend_kernel(q_ref, k_ref, v_ref, pq_ref, pk_ref, o_ref, lse_ref, *, tile):
    tiles = q_ref.shape[0] // tile
    for head in range(HEADS_HERE):
        span = slice(head * HEAD_DIM, (head + 1) * HEAD_DIM)
        k_head = k_ref[:, span]
        v_turned = v_ref[:, span].T

        def step(t, carry):
            rows = pl.ds(pl.multiple_of(t * tile, tile), tile)
            scores = dot_right(k_head, q_ref[rows, span]) * score_scale
            allowed = pq_ref[:, rows] >= pk_ref[...]
            scores = jnp.where(allowed, scores, masked_score)
            peak = jnp.max(scores, axis=0, keepdims=True)
            powers = jnp.exp(scores - peak)
            total = jnp.sum(powers, axis=0, keepdims=True)
            mixed = dot(v_turned, (powers / total).astype(bf16))
            o_ref[rows, span] = mixed.T.astype(bf16)
            lse_ref[head : head + 1, rows] = peak + jnp.log(total)
            return carry

        lax.fori_loop(0, tiles, step, 0)


def attend(query, key, value, pos_q, pos_k, tile=256):
    return pl.pallas_call(
        functools.partial(attend_kernel, tile=tile),
        out_shape=(
            jax.ShapeDtypeStruct(query.shape, bf16),
            jax.ShapeDtypeStruct((HEADS_HERE, query.shape[0]), f32),
        ),
        name="attend",
    )(query, key, value, pos_q, pos_k)


def attend_back_kernel(
    q_ref, k_ref, v_ref, g_ref, lse_ref, pq_ref, pk_ref, gq_ref, gk_ref, gv_ref, ak_ref, av_ref, *, tile
):
    tiles = q_ref.shape[0] // tile
    for head in range(HEADS_HERE):
        span = slice(head * HEAD_DIM, (head + 1) * HEAD_DIM)
        k_head = k_ref[:, span]
        v_head = v_ref[:, span]
        k_turned = k_head.T
        ak_ref[...] = jnp.zeros_like(ak_ref)
        av_ref[...] = jnp.zeros_like(av_ref)

        def step(t, carry):
            rows = pl.ds(pl.multiple_of(t * tile, tile), tile)
            q_tile = q_ref[rows, span]
            g_tile = g_ref[rows, span]
            scores = dot_right(k_head, q_tile) * score_scale
            allowed = pq_ref[:, rows] >= pk_ref[...]
            scores = jnp.where(allowed, scores, masked_score)
            probs = jnp.exp(scores - lse_ref[head : head + 1, rows])
            grad_probs = dot_right(v_head, g_tile)
            delta = jnp.sum(probs * grad_probs, axis=0, keepdims=True)
            grad_scores = (probs * (grad_probs - delta)).astype(bf16)
            gq_ref[rows, span] = dot(k_turned, grad_scores).T * score_scale
            ak_ref[...] += dot(grad_scores, q_tile)
            av_ref[...] += dot(probs.astype(bf16), g_tile)
            return carry

        lax.fori_loop(0, tiles, step, 0)
        gk_ref[:, span] = ak_ref[...] * score_scale
        gv_ref[:, span] = av_ref[...]


def attend_back(query, key, value, grad_rows, lse, pos_q, pos_k, tile=256):
    return pl.pallas_call(
        functools.partial(attend_back_kernel, tile=tile),
        out_shape=(
            jax.ShapeDtypeStruct(query.shape, f32),
            jax.ShapeDtypeStruct(key.shape, f32),
            jax.ShapeDtypeStruct(value.shape, f32),
        ),
        scratch_shapes=[
            pltpu.VMEM((key.shape[0], HEAD_DIM), f32),
            pltpu.VMEM((key.shape[0], HEAD_DIM), f32),
        ],
        name="attend_back",
    )(query, key, value, grad_rows, lse, pos_q, pos_k)


def body(
    n_ctx,
    n_shard,
    hidden_in,
    block_of,
    lengths,
    attn_latent,
    ffn_in_latent,
    ffn_out_latent,
    student_vec,
    teacher_attn,
    teacher_ffn_in,
    teacher_ffn_out,
    teacher_vec,
):
    seqs, rows, _ = hidden_in.shape
    rest = n_ctx // GROUP
    own = seqs * rows
    ctx = lax.axis_index("ctx")
    z = lax.axis_index("shard")
    k = ctx % CORES
    j = (ctx // CORES) % CHIPS
    r = ctx // GROUP
    units_z = FF // n_shard // CHIPS

    def over_chips(piece, mask):
        return lax.ppermute(piece, "ctx", [(a, a ^ (mask * CORES)) for a in range(n_ctx)])

    def over_cores(piece):
        return lax.ppermute(piece, "ctx", [(a, a ^ 1) for a in range(n_ctx)])

    def over_rest(piece, mask):
        return lax.ppermute(piece, "ctx", [(a, a ^ (mask * GROUP)) for a in range(n_ctx)])

    def over_z(piece, mask):
        return lax.ppermute(piece, "shard", [(a, a ^ mask) for a in range(n_shard)])

    def index(array, place, axis=0):
        return lax.dynamic_index_in_dim(array, place, axis, keepdims=False)

    def reorder(array, place, axis=0):
        return jnp.take(array, jnp.arange(array.shape[axis]) ^ place, axis=axis)

    def gather_z(piece):
        pieces = jnp.stack([piece] + [over_z(piece, m) for m in range(1, n_shard)])
        both = jnp.stack([pieces, over_cores(pieces)], axis=1)
        both = reorder(reorder(both, z, 0), k, 1)
        return both.reshape(n_shard * CORES * piece.shape[0], piece.shape[1])

    def gather_chips(piece):
        return [piece] + [over_chips(piece, m) for m in range(1, CHIPS)]

    def scatter_z(partial):
        part_rows = partial.shape[0] // (n_shard * CORES)
        view = partial.reshape(n_shard, CORES, part_rows, partial.shape[1])
        mine = index(view, k, 1) + over_cores(index(view, 1 - k, 1).astype(bf16)).astype(f32)
        total = tree_sum(
            [index(mine, z)]
            + [over_z(index(mine, z ^ m).astype(bf16), m).astype(f32) for m in range(1, n_shard)]
        )
        if rest > 1:
            total = tree_sum(
                [total]
                + [over_rest(total.astype(bf16), m).astype(f32) for m in range(1, rest)]
            )
        return total.astype(bf16)

    def gather_plane(piece):
        pieces = jnp.stack(gather_chips(piece))
        both = jnp.stack([pieces, over_cores(pieces)], axis=1)
        return reorder(reorder(both, j, 0), k, 1)

    def total_all(values):
        values = values + over_cores(values)
        values = tree_sum(gather_chips(values))
        if rest > 1:
            values = tree_sum([values] + [over_rest(values, m) for m in range(1, rest)])
        return tree_sum([values] + [over_z(values, m) for m in range(1, n_shard)])

    def places_of(chip):
        starts = jnp.stack([(chip * CORES + k) * rows, (chip * CORES + 1 - k) * rows])
        layout = (starts[:, None] + jnp.arange(rows, dtype=jnp.int32)[None, :]).reshape(own)
        hot = (layout[:, None] // BLK) == jnp.arange(block_of.shape[0], dtype=jnp.int32)[None, :]
        return jnp.sum(jnp.where(hot, block_of[None, :], 0), axis=1) * BLK + layout % BLK

    pos_q = jnp.concatenate([places_of(r * CHIPS + (j ^ m)) for m in range(CHIPS)])
    pos_k = jnp.concatenate(
        [places_of((r ^ n) * CHIPS + (j ^ m)) for n in range(rest) for m in range(CHIPS)]
    )
    pos_q_row = pos_q[None, :]
    pos_k_col = pos_k[:, None]

    mine_in = jnp.concatenate([index(hidden_in, k), over_cores(index(hidden_in, 1 - k))])
    own_rows = mine_in.astype(f32)
    own_length = index(lengths, z * seqs + k)
    valid = (pos_q[:own] < own_length).astype(f32)[:, None]
    count = jnp.sum(lengths.astype(f32))
    loss_scale = count * D

    x_all = jnp.concatenate(gather_chips(mine_in))

    def pieces_of(attn, w_in, w_down):
        half = attn.shape[1] // CORES
        mine = lax.dynamic_slice_in_dim(attn, k * half, half, 1)
        qkv = index(mine[:3].reshape(3, half, CHIPS, COLS), j, 2)
        qkv = jnp.concatenate([qkv[0], qkv[1], qkv[2]], axis=1)
        few = attn.shape[1] // GROUP
        out = lax.dynamic_slice_in_dim(attn[3], (j * CORES + k) * few, few, 0)
        inner = lax.dynamic_slice_in_dim(w_in, k * half, half, 0)
        inner = index(inner.reshape(half, n_shard, CHIPS, units_z), j, 2).reshape(half, UNITS)
        down = lax.dynamic_slice_in_dim(
            w_down, (j * CORES + k) * (units_z // CORES), units_z // CORES, 0
        )
        return qkv, out, inner, down

    def gather_out(piece):
        pieces = jnp.stack([piece] + [over_z(piece, m) for m in range(1, n_shard)])
        chips = jnp.stack(gather_chips(pieces), axis=1)
        both = jnp.stack([chips, over_cores(chips)], axis=2)
        both = reorder(reorder(reorder(both, z, 0), j, 1), k, 2)
        return reorder(both.reshape(CHIPS, COLS, D), j, 0).reshape(D, D)

    def weights_of(pieces):
        qkv, out, inner, down = pieces
        return gather_z(qkv), gather_out(out), gather_z(inner), gather_z(down)

    t_weights = weights_of(pieces_of(teacher_attn, teacher_ffn_in, teacher_ffn_out))

    sums = jnp.concatenate(
        [
            jnp.sum(jnp.abs(attn_latent), axis=1).reshape(-1),
            jnp.sum(jnp.abs(ffn_in_latent), axis=0),
            jnp.sum(jnp.abs(ffn_out_latent), axis=0),
        ]
    )
    sums = tree_sum([sums] + [over_z(sums, m) for m in range(1, n_shard)])
    gains = jnp.asarray(attn_gains, dtype=f32)[:, None, None]
    scale_attn = gains * (sums[: 4 * D].reshape(4, 1, D) / D)
    scale_in = sums[4 * D : 4 * D + FF][None] / D
    scale_down = sums[4 * D + FF :][None] / FF
    s_weights = weights_of(
        pieces_of(
            (scale_attn * jnp.sign(attn_latent) * D ** (-0.5)).astype(bf16),
            (scale_in * jnp.sign(ffn_in_latent) * D ** (-0.5)).astype(bf16),
            (scale_down * jnp.sign(ffn_out_latent) * FF ** (-0.5)).astype(bf16),
        )
    )

    def chunk_cols(vector):
        return index(vector.reshape(CHIPS, COLS), j)

    def rest_gather(values):
        if rest == 1:
            return values
        return jnp.concatenate([values] + [over_rest(values, m) for m in range(1, rest)])

    def rest_scatter(partial):
        if rest == 1:
            return partial
        view = partial.reshape(rest, -1, partial.shape[1])
        return tree_sum(
            [view[0]] + [over_rest(view[m].astype(bf16), m).astype(f32) for m in range(1, rest)]
        )

    def scatter_chips(pieces):
        return tree_sum(
            [pieces[0]]
            + [over_chips(pieces[m].astype(bf16), m).astype(f32) for m in range(1, CHIPS)]
        )

    def forward(weights, vector):
        w_qkv, w_out, w_in, w_down = weights
        bias = jnp.concatenate(
            [chunk_cols(vector[0]), jnp.zeros((COLS,), f32), chunk_cols(vector[1])]
        )
        qkv = (dot(x_all, w_qkv) + bias).astype(bf16)
        query = qkv[:, :COLS]
        key = rest_gather(qkv[:, COLS : 2 * COLS])
        value = rest_gather(qkv[:, 2 * COLS :])
        heads, lse = attend(query, key, value, pos_q_row, pos_k_col)
        pieces = heads.reshape(CHIPS, own, COLS)
        heads_own = jnp.concatenate(
            [pieces[0]] + [over_chips(pieces[m], m) for m in range(1, CHIPS)], axis=1
        )
        branch = dot(heads_own, w_out) + vector[2]
        residual = own_rows + branch
        first = layer_norm(residual, vector[4], vector[5])
        firsts = gather_chips(first.astype(bf16))
        b1 = index(vector[8:].reshape(n_shard, CHIPS, units_z), j, 1).reshape(UNITS)
        inners, acts, parts = [], [], []
        for piece in firsts:
            inner = dot(piece, w_in) + b1
            act = (inner * normal_cdf(inner)).astype(bf16)
            inners.append(inner)
            acts.append(act)
            parts.append(dot(act, w_down))
        feed = scatter_chips(parts) + vector[3]
        second = first + feed
        out = layer_norm(second, vector[6], vector[7])
        return dict(
            query=query,
            key=key,
            value=value,
            lse=lse,
            heads_own=heads_own,
            branch=branch,
            residual=residual,
            first=first,
            firsts=firsts,
            inners=inners,
            acts=acts,
            feed=feed,
            second=second,
            out=out,
        )

    target = forward(t_weights, teacher_vec)["out"]
    s = forward(s_weights, student_vec)
    w_qkv, w_out, w_in, w_down = s_weights
    out = s["out"]
    mismatch = out - target
    grad_second, grad_g2, grad_c2 = layer_norm_back(
        s["second"], student_vec[6], valid * mismatch / loss_scale
    )
    grad_b2 = jnp.sum(grad_second, axis=0)
    feeds = gather_chips(grad_second.astype(bf16))
    grad_inners, parts, grad_b1 = [], [], 0.0
    for feed, inner in zip(feeds, s["inners"]):
        slope = normal_cdf(inner) + inner * jnp.exp(-0.5 * inner * inner) * 0.3989422804014327
        grad_inner = dot_right(feed, w_down) * slope
        grad_b1 = grad_b1 + jnp.sum(grad_inner, axis=0)
        grad_inner = grad_inner.astype(bf16)
        grad_inners.append(grad_inner)
        parts.append(dot_right(grad_inner, w_in))
    grad_first = grad_second + scatter_chips(parts)
    grad_res, grad_g1, grad_c1 = layer_norm_back(s["residual"], student_vec[4], grad_first)
    grad_bo = jnp.sum(grad_res, axis=0)
    grad_branch = grad_res.astype(bf16)
    grad_heads_own = dot_right(grad_branch, w_out).astype(bf16)
    grad_heads = jnp.concatenate(
        [grad_heads_own[:, :COLS]]
        + [
            over_chips(grad_heads_own[:, m * COLS : (m + 1) * COLS], m)
            for m in range(1, CHIPS)
        ]
    )
    grad_query, grad_key, grad_value = attend_back(
        s["query"], s["key"], s["value"], grad_heads, s["lse"], pos_q_row, pos_k_col
    )
    grad_key, grad_value = rest_scatter(grad_key), rest_scatter(grad_value)
    grad_bq = jnp.sum(grad_query, axis=0)
    grad_bv = jnp.sum(grad_value, axis=0)
    grad_qkv = jnp.concatenate([grad_query, grad_key, grad_value], axis=1).astype(bf16)
    parts = dot_right(grad_qkv, w_qkv).reshape(CHIPS, own, D)
    grad_own = grad_res + scatter_chips([parts[m] for m in range(CHIPS)])

    acts = jnp.concatenate(s["acts"])
    down_grad = gather_plane(scatter_z(dot_left(acts, jnp.concatenate(feeds))))
    down_grad = down_grad.reshape(ffn_out_latent.shape)
    in_grad = scatter_z(dot_left(jnp.concatenate(s["firsts"]), jnp.concatenate(grad_inners)))
    in_grad = gather_plane(in_grad).reshape(CHIPS, ffn_in_latent.shape[0], n_shard, units_z)
    in_grad = in_grad.transpose(1, 2, 0, 3).reshape(ffn_in_latent.shape)
    rel_cols = reorder(grad_branch.reshape(own, CHIPS, COLS), j, 1)
    out_parts = reorder(
        dot_left(s["heads_own"], rel_cols.reshape(own, D)).reshape(CHIPS, COLS, D), j, 0
    ).reshape(D, CHIPS, COLS)
    out_grad = scatter_z(scatter_chips([out_parts[:, m] for m in range(CHIPS)]))
    qkv_grad = scatter_z(dot_left(x_all, grad_qkv))

    def columns(piece):
        full = gather_plane(piece)
        return full.reshape(CHIPS, attn_latent.shape[1], -1)

    out_grad = columns(out_grad).transpose(1, 0, 2).reshape(1, -1, D)
    qkv_grad = columns(qkv_grad).reshape(CHIPS, -1, 3, COLS).transpose(2, 1, 0, 3)
    attn_grad = jnp.concatenate([qkv_grad.reshape(3, -1, D), out_grad])

    def keep(latent, grad):
        return jnp.where(jnp.abs(latent) <= 1.0, grad.astype(f32), 0.0)

    def spread(chunk):
        hot = (jnp.arange(CHIPS) == j).astype(f32)[:, None]
        return (hot * chunk[None]).reshape(D)

    hot = (jnp.arange(CHIPS) == j).astype(f32)[None, :, None]
    b1_rows = (grad_b1.reshape(n_shard, 1, units_z) * hot).reshape(FF // D, D)
    stats = jnp.stack(
        [
            0.5 * jnp.sum(valid * mismatch * mismatch),
            jnp.sum(valid * s["branch"] * s["branch"]),
            jnp.sum(valid * s["feed"] * s["feed"]),
            jnp.sum(valid * s["second"] * s["second"]),
        ]
    )
    early = jnp.concatenate(
        [
            jnp.stack([grad_bo, grad_b2, grad_g1, grad_c1, grad_g2, grad_c2]),
            b1_rows,
            jnp.pad(stats, (0, D - 4))[None],
        ]
    )
    early = total_all(early)
    late = total_all(jnp.stack([spread(grad_bq), spread(grad_bv)]))
    stats = early[-1, :4]
    statistics = jnp.concatenate([stats[:1] / loss_scale, jnp.sqrt(stats[1:] / loss_scale)])

    def to_owners(values):
        here, there = values[:rows], over_cores(values[rows:])
        return jnp.where(k == 0, jnp.stack([here, there]), jnp.stack([there, here]))

    return (
        to_owners(out.astype(bf16)),
        statistics,
        to_owners(grad_own),
        keep(attn_latent, attn_grad),
        keep(ffn_in_latent, in_grad),
        keep(ffn_out_latent, down_grad),
        jnp.concatenate([late[1:], early[:-1]]),
        late[0],
    )


def solution(mesh):
    n_ctx, n_shard = mesh.shape["ctx"], mesh.shape["shard"]
    in_specs = (
        P("shard", "ctx", None),
        P(),
        P(),
        P(None, "shard", None),
        P("shard", None),
        P("shard", None),
        P(),
        P(None, "shard", None),
        P("shard", None),
        P("shard", None),
        P(),
    )
    out_specs = (
        P("shard", "ctx", None),
        P(),
        P("shard", "ctx", None),
        P(None, "shard", None),
        P("shard", None),
        P("shard", None),
        P(),
        P(),
    )
    return jax.shard_map(
        functools.partial(body, n_ctx, n_shard),
        mesh=mesh,
        in_specs=in_specs,
        out_specs=out_specs,
        check_vma=False,
    )
```

```python
import functools

import jax
import jax.numpy as jnp
from jax import lax
from jax.experimental import pallas as pl
from jax.experimental.pallas import tpu as pltpu
from jax.sharding import PartitionSpec as P

D = 768
HEADS = 12
HEAD_DIM = 64
FF = 3072
BLK = 64

CHIPS = 4
CORES = 2
GROUP = CHIPS * CORES
COLS = D // CHIPS
HEADS_HERE = HEADS // CHIPS
UNITS = FF // CHIPS
HALF = UNITS // CORES
QKV = 3 * COLS

norm_eps = 1e-05
attn_gains = (2.0, 2.0, 1.0, 4.0)
masked_score = -1e30
score_scale = HEAD_DIM ** (-0.5)
bf16 = jnp.bfloat16
f32 = jnp.float32

IZ, IK, IJ, IR = 0, 1, 2, 3
ROW_BO, ROW_B2, ROW_G1, ROW_C1, ROW_G2, ROW_C2, ROW_STATS, ROW_B1, ROW_QV = range(9)
VEC_ROWS = 16

SMEM_SPEC = pl.BlockSpec(memory_space=pltpu.SMEM)
VMEM_SPEC = pl.BlockSpec(memory_space=pltpu.VMEM)


def dot(left_side, right_side):
    return jnp.dot(left_side, right_side, preferred_element_type=f32)


def dot_left(left_side, right_side):
    return lax.dot_general(
        left_side, right_side, (((0,), (0,)), ((), ())), preferred_element_type=f32
    )


def dot_right(left_side, right_side):
    return lax.dot_general(
        left_side, right_side, (((1,), (1,)), ((), ())), preferred_element_type=f32
    )


def normal_cdf(values):
    return 0.5 * (1.0 + lax.erf(values * 0.7071067811865476))


def tree_sum(items):
    items = list(items)
    while len(items) > 1:
        items = [items[i] + items[i + 1] for i in range(0, len(items), 2)]
    return items[0]


def aligned(start, size):
    return pl.ds(pl.multiple_of(start, size), size)


def shape(dims, kind=bf16):
    return jax.ShapeDtypeStruct(dims, kind)


def call(kernel, name, outs, scalars, arrays, scratch=()):
    return pl.pallas_call(
        kernel,
        out_shape=outs,
        in_specs=[SMEM_SPEC] * len(scalars) + [VMEM_SPEC] * len(arrays),
        out_specs=jax.tree.map(lambda _: VMEM_SPEC, outs),
        scratch_shapes=list(scratch),
        name=name,
    )(*scalars, *arrays)


def pick(place, options):
    value = options[0]
    for number, option in enumerate(options[1:], 1):
        value = jnp.where(place == number, option, value)
    return value


def sums_kernel(attn_ref, in_ref, out_ref, sums_ref):
    @pl.when(pl.program_id(0) == 0)
    def _():
        sums_ref[...] = jnp.zeros_like(sums_ref)

    for number in range(4):
        sums_ref[number : number + 1, :] += jnp.sum(
            jnp.abs(attn_ref[number]), axis=0, keepdims=True
        )
    for number in range(FF // D):
        sums_ref[4 + number : 5 + number, :] += jnp.sum(
            jnp.abs(in_ref[:, number * D : (number + 1) * D]), axis=0, keepdims=True
        )
    last = 4 + FF // D
    sums_ref[last : last + 1, :] += jnp.sum(jnp.abs(out_ref[...]), axis=0, keepdims=True)


def column_sums(attn, w_in, w_down, steps=4):
    return pl.pallas_call(
        sums_kernel,
        out_shape=shape((16, D), f32),
        grid=(steps,),
        in_specs=[
            pl.BlockSpec((4, attn.shape[1] // steps, D), lambda i: (0, i, 0)),
            pl.BlockSpec((w_in.shape[0] // steps, FF), lambda i: (i, 0)),
            pl.BlockSpec((w_down.shape[0] // steps, D), lambda i: (i, 0)),
        ],
        out_specs=pl.BlockSpec((16, D), lambda i: (0, 0)),
        name="column_sums",
    )(attn, w_in, w_down)


def sign_of(values):
    return jnp.where(values > 0, 1.0, jnp.where(values < 0, -1.0, 0.0))


def choose(size, count, start):
    place = lax.broadcasted_iota(jnp.int32, (size, count), 0)
    goal = lax.broadcasted_iota(jnp.int32, (size, count), 1) + start
    return jnp.where(place == goal, 1.0, 0.0).astype(bf16)


def pieces_kernel(n_shard, student, ids_ref, *refs):
    if student:
        attn_ref, in_ref, down_ref, sums_ref, early_ref, late_ref = refs
    else:
        attn_ref, in_ref, down_ref, early_ref, late_ref = refs
    k, j = ids_ref[IK], ids_ref[IJ]
    units = FF // n_shard
    few = units // GROUP
    rows_z = in_ref.shape[0]

    def binary(values, row, gain, fan_in):
        if not student:
            return values
        scale = gain * (sums_ref[row : row + 1, :] / fan_in) * fan_in ** (-0.5)
        return (sign_of(values) * scale).astype(bf16)

    chosen = choose(D, COLS, j * COLS)
    for number in range(4):
        full = binary(attn_ref[number], number, attn_gains[number], D)
        early_ref[:, number * COLS : (number + 1) * COLS] = dot(full, chosen).astype(bf16)
    chosen = choose(units, few, (j * CORES + k) * few)
    for number in range(FF // D):
        full = binary(in_ref[:, number * D : (number + 1) * D], 4 + number, 1.0, D)
        for part in range(D // units):
            place = (number * (D // units) + part) * few
            late_ref[0:rows_z, place : place + few] = dot(
                full[:, part * units : (part + 1) * units], chosen
            ).astype(bf16)
    full = binary(down_ref[...], 4 + FF // D, 1.0, FF)
    late_ref[rows_z : rows_z + few, :] = full[:, :HALF]
    late_ref[rows_z + few : rows_z + 2 * few, :] = full[:, HALF:]


def weight_pieces(n_shard, ids, attn, w_in, w_down, sums=None):
    half = attn.shape[1] // CORES
    few = FF // n_shard // GROUP
    rows_z = w_in.shape[0]
    specs = [
        pl.BlockSpec((4, half, D), lambda i, ids: (0, ids[IK], 0)),
        pl.BlockSpec((rows_z, FF), lambda i, ids: (0, 0)),
        pl.BlockSpec((few, D), lambda i, ids: (CORES * ids[IJ] + ids[IK], 0)),
    ]
    args = [attn, w_in, w_down]
    if sums is not None:
        specs.append(pl.BlockSpec((16, D), lambda i, ids: (0, 0)))
        args.append(sums)
    return pl.pallas_call(
        functools.partial(pieces_kernel, n_shard, sums is not None),
        out_shape=(shape((half, D)), shape((rows_z + 2 * few, HALF))),
        grid_spec=pltpu.PrefetchScalarGridSpec(
            num_scalar_prefetch=1,
            grid=(1,),
            in_specs=specs,
            out_specs=(
                pl.BlockSpec((half, D), lambda i, ids: (0, 0)),
                pl.BlockSpec((rows_z + 2 * few, HALF), lambda i, ids: (0, 0)),
            ),
        ),
        name="student_pieces" if sums is not None else "teacher_pieces",
    )(ids, *args)


def early_kernel(n_shard, ids_ref, *refs):
    t_refs, s_refs = refs[:n_shard], refs[n_shard : 2 * n_shard]
    qkv_ref, out_ref = refs[2 * n_shard :]
    z = ids_ref[IZ]
    half = t_refs[0].shape[0]
    span = n_shard * half
    for model, group in enumerate((t_refs, s_refs)):
        for mask, ref in enumerate(group):
            place = z ^ mask
            rows = pl.ds(pl.multiple_of(model * span + place * half, half), half)
            qkv_ref[rows, :] = ref[:, :QKV]
            fold = n_shard // 2
            low = pl.ds(
                pl.multiple_of(model * (span // 2) + lax.rem(place, fold) * half, half), half
            )

            @pl.when(place < fold)
            def _():
                out_ref[low, 0:COLS] = ref[:, QKV:]

            @pl.when(place >= fold)
            def _():
                out_ref[low, COLS:] = ref[:, QKV:]


def out_weight_kernel(n_shard, ids_ref, *refs):
    z, k, j = ids_ref[IZ], ids_ref[IK], ids_ref[IJ]
    t_ref, s_ref = refs[2 * CHIPS :]
    half = D // n_shard // CORES
    span = n_shard * half // 2
    for core in range(CORES):
        for mask in range(CHIPS):
            ref = refs[core * CHIPS + mask]
            for model, goal in enumerate((t_ref, s_ref)):
                for place in range(n_shard):
                    fold = n_shard // 2
                    low = model * span + (place % fold) * half
                    lanes = slice(0, COLS) if place < fold else slice(COLS, 2 * COLS)
                    rows = pl.ds(
                        pl.multiple_of((place * CORES + (k ^ core)) * half, half), half
                    )
                    goal[j ^ mask, rows, :] = ref[low : low + half, lanes]


def late_kernel(n_shard, ids_ref, *refs):
    z, k, j = ids_ref[IZ], ids_ref[IK], ids_ref[IJ]
    vec_ref, in_ref, down_ref, b1_ref = refs[CORES * n_shard :]
    units = FF // n_shard
    few = units // GROUP
    rows_z = D // n_shard
    for core in range(CORES):
        lanes = aligned((k ^ core) * HALF, HALF)
        for mask in range(n_shard):
            ref = refs[core * n_shard + mask]
            place = z ^ mask
            in_ref[aligned(place * rows_z, rows_z), lanes] = ref[0:rows_z, :]
            rows = pl.ds(pl.multiple_of((k ^ core) * HALF + place * few, few), few)
            down_ref[rows, 0:HALF] = ref[rows_z : rows_z + few, :]
            down_ref[rows, HALF:] = ref[rows_z + few : rows_z + 2 * few, :]
    for core in range(CORES):
        for place in range(n_shard):
            options = []
            for chip in range(CHIPS):
                start = place * units + (chip * CORES + core) * few
                row, lane = 8 + start // D, start % D
                options.append(vec_ref[row : row + 1, lane : lane + few])
            goal = core * HALF + place * few
            b1_ref[0:1, goal : goal + few] = pick(j, options)


def places_kernel(rest, ids_ref, block_ref, lengths_ref, row_ref, col_ref, valid_ref, *, seqs, rows):
    z, k, j, r = ids_ref[IZ], ids_ref[IK], ids_ref[IJ], ids_ref[IR]
    length = lengths_ref[z * seqs + k]
    per = rows // BLK
    number = 0
    for far in range(rest):
        for mask in range(CHIPS):
            for half in range(CORES):
                for part in range(per):
                    block = ((((r ^ far) * CHIPS + (j ^ mask)) * CORES + (k ^ half)) * per) + part
                    base = block_ref[block] * BLK
                    goal = slice(number * BLK, (number + 1) * BLK)
                    col = base + lax.broadcasted_iota(jnp.int32, (BLK, 1), 0)
                    col_ref[goal, :] = col
                    if far == 0:
                        row_ref[:, goal] = base + lax.broadcasted_iota(jnp.int32, (1, BLK), 1)
                    if far == 0 and mask == 0:
                        valid_ref[goal, :] = jnp.where(col < length, 1.0, 0.0)
                    number += 1


def input_kernel(ids_ref, *refs):
    k = ids_ref[IK]
    own_ref, send_ref = refs[CHIPS:]
    rows = refs[0].shape[1]
    for mask in range(CHIPS):
        goal = slice(mask * rows, (mask + 1) * rows)
        own_ref[goal, :] = refs[mask][k]
        send_ref[goal, :] = refs[mask][1 - k]


def qkv_kernel(n_shard, model, ids_ref, own_ref, oth_ref, half_ref, peer_ref, vec_ref, *outs):
    k, j = ids_ref[IK], ids_ref[IJ]
    q_ref, k_ref, v_ref, w_ref = outs
    half = D // n_shard // CORES
    base = model * n_shard * half
    for core, ref in enumerate((half_ref, peer_ref)):
        for place in range(n_shard):
            rows = pl.ds(pl.multiple_of((place * CORES + (k ^ core)) * half, half), half)
            w_ref[rows, :] = ref[base + place * half : base + (place + 1) * half, :]
    weight = w_ref[...]
    chips = [slice(chip * COLS, (chip + 1) * COLS) for chip in range(CHIPS)]
    q_bias = pick(j, [vec_ref[0:1, chip] for chip in chips])
    v_bias = pick(j, [vec_ref[1:2, chip] for chip in chips])
    rows = own_ref.shape[0] // CHIPS
    for core, ref in enumerate((own_ref, oth_ref)):
        for mask in range(CHIPS):
            result = dot(ref[mask * rows : (mask + 1) * rows, :], weight)
            goal = slice((mask * CORES + core) * rows, (mask * CORES + core + 1) * rows)
            q_ref[goal, :] = (result[:, :COLS] + q_bias).astype(bf16)
            k_ref[goal, :] = result[:, COLS : 2 * COLS].astype(bf16)
            v_ref[goal, :] = (result[:, 2 * COLS :] + v_bias).astype(bf16)


def attend_kernel(q_ref, k_ref, v_ref, pq_ref, pk_ref, *outs, tile):
    o_refs, lse_ref = outs[:CHIPS], outs[CHIPS]
    own = q_ref.shape[0] // CHIPS
    for head in range(HEADS_HERE):
        span = slice(head * HEAD_DIM, (head + 1) * HEAD_DIM)
        k_head = k_ref[:, span]
        v_turned = v_ref[:, span].T
        for t in range(q_ref.shape[0] // tile):
            rows = slice(t * tile, (t + 1) * tile)
            scores = dot_right(k_head, q_ref[rows, span]) * score_scale
            allowed = pq_ref[:, rows] >= pk_ref[...]
            scores = jnp.where(allowed, scores, masked_score)
            peak = jnp.max(scores, axis=0, keepdims=True)
            powers = jnp.exp(scores - peak)
            total = jnp.sum(powers, axis=0, keepdims=True)
            mixed = dot(v_turned, powers.astype(bf16)) / total
            low = t * tile % own
            o_refs[t * tile // own][low : low + tile, span] = mixed.T.astype(bf16)
            lse_ref[head : head + 1, rows] = peak + jnp.log(total)


def norm_parts(values):
    middle = jnp.mean(values, axis=-1, keepdims=True)
    centred = values - middle
    spread = jnp.mean(centred * centred, axis=-1, keepdims=True)
    inverse = lax.rsqrt(spread + norm_eps)
    return centred * inverse, inverse


def norm_back(values, gain, grad_out):
    normal, inverse = norm_parts(values)
    scaled = grad_out * gain
    grad_in = (
        scaled
        - jnp.mean(scaled, axis=-1, keepdims=True)
        - normal * jnp.mean(scaled * normal, axis=-1, keepdims=True)
    ) * inverse
    return grad_in, normal


def column_total(values):
    return jnp.sum(values, axis=0, keepdims=True)


def branch_kernel(student, ids_ref, *refs):
    j = ids_ref[IJ]
    h_refs, (w_ref, own_ref, oth_ref, vec_ref, valid_ref) = refs[:CHIPS], refs[CHIPS : CHIPS + 5]
    outs = refs[CHIPS + 5 :]
    first_ref, sent_ref = outs[:2]
    rows = own_ref.shape[0] // CHIPS
    if student:
        residual_ref, sums_ref = outs[2:]
        sums_ref[...] = jnp.zeros_like(sums_ref)
    for core, x_ref in enumerate((own_ref, oth_ref)):
        goal = slice(core * rows, (core + 1) * rows)
        parts = []
        for chip in range(CHIPS):
            parts.append(
                tree_sum(
                    dot(
                        h_refs[mask][goal, :],
                        w_ref[chip, aligned((j ^ mask) * COLS, COLS), :],
                    )
                    for mask in range(CHIPS)
                )
            )
        branch = jnp.concatenate(parts, axis=1) + vec_ref[2:3, :]
        residual = x_ref[0:rows, :].astype(f32) + branch
        normal, _ = norm_parts(residual)
        first = normal * vec_ref[4:5, :] + vec_ref[5:6, :]
        first_ref[goal, :] = first
        sent_ref[goal, :] = first.astype(bf16)
        if student:
            residual_ref[goal, :] = residual
            sums_ref[0:1, :] += column_total(valid_ref[goal, :] * branch * branch)


def feed_kernel(student, piece_ref, in_ref, down_ref, b1_ref, part_ref, *outs):
    inner = dot(piece_ref[...], in_ref[...]) + b1_ref[0:1, :]
    act = (inner * normal_cdf(inner)).astype(bf16)
    if student:
        outs[0][...] = inner
        outs[1][...] = act
    part_ref[...] = dot(act, down_ref[...]).astype(part_ref.dtype)


def target_kernel(*refs):
    parts, (first_ref, vec_ref, target_ref) = refs[:CHIPS], refs[CHIPS:]
    feed = tree_sum(ref[...].astype(f32) for ref in parts) + vec_ref[3:4, :]
    normal, _ = norm_parts(first_ref[...] + feed)
    target_ref[...] = normal * vec_ref[6:7, :] + vec_ref[7:8, :]


def loss_kernel(lengths_ref, *refs):
    parts, rest = refs[:CHIPS], refs[CHIPS:]
    first_ref, vec_ref, target_ref, valid_ref, out_ref, grad_ref, sent_ref, sums_ref = rest
    count = lengths_ref[0]
    for number in range(1, lengths_ref.shape[0]):
        count = count + lengths_ref[number]
    share = 1.0 / (count.astype(f32) * D)
    feed = tree_sum(ref[...].astype(f32) for ref in parts) + vec_ref[3:4, :]
    second = first_ref[...] + feed
    normal, inverse = norm_parts(second)
    out = normal * vec_ref[6:7, :] + vec_ref[7:8, :]
    out_ref[...] = out.astype(bf16)
    valid = valid_ref[...]
    mismatch = valid * (out - target_ref[...])
    grad_out = mismatch * share
    scaled = grad_out * vec_ref[6:7, :]
    grad = (
        scaled
        - jnp.mean(scaled, axis=-1, keepdims=True)
        - normal * jnp.mean(scaled * normal, axis=-1, keepdims=True)
    ) * inverse
    grad_ref[...] = grad
    sent_ref[...] = grad.astype(bf16)
    sums_ref[...] = jnp.concatenate(
        [
            column_total(grad),
            column_total(grad_out * normal),
            column_total(grad_out),
            0.5 * column_total(mismatch * mismatch),
            column_total(valid * feed * feed),
            column_total(valid * second * second),
            jnp.zeros((2, D), f32),
        ]
    )


def feed_back_kernel(piece_ref, inner_ref, in_ref, down_ref, part_ref, grad_ref, sum_ref):
    inner = inner_ref[...]
    slope = normal_cdf(inner) + inner * jnp.exp(-0.5 * inner * inner) * 0.3989422804014327
    grad = dot_right(piece_ref[...], down_ref[...]) * slope
    sum_ref[...] = jnp.broadcast_to(column_total(grad), sum_ref.shape)
    grad = grad.astype(bf16)
    grad_ref[...] = grad
    part_ref[...] = dot_right(grad, in_ref[...]).astype(part_ref.dtype)


def branch_back_kernel(ids_ref, *refs):
    j = ids_ref[IJ]
    parts, rest = refs[:CHIPS], refs[CHIPS:]
    second_ref, residual_ref, vec_ref, w_ref = rest[:4]
    grad_ref, sent_ref = rest[4:6]
    h_refs, (sums_ref,) = rest[6 : 6 + CHIPS], rest[6 + CHIPS :]
    grad_first = second_ref[...] + tree_sum(ref[...].astype(f32) for ref in parts)
    grad, normal = norm_back(residual_ref[...], vec_ref[4:5, :], grad_first)
    grad_ref[...] = grad
    sums_ref[...] = jnp.concatenate(
        [
            column_total(grad),
            column_total(grad_first * normal),
            column_total(grad_first),
            jnp.zeros((5, D), f32),
        ]
    )
    grad = grad.astype(bf16)
    sent_ref[...] = grad
    chips = [grad[:, chip * COLS : (chip + 1) * COLS] for chip in range(CHIPS)]
    for mask in range(CHIPS):
        rows = aligned((j ^ mask) * COLS, COLS)
        h_refs[mask][...] = tree_sum(
            dot_right(chips[chip], w_ref[chip, rows, :]) for chip in range(CHIPS)
        ).astype(bf16)


def attend_back_kernel(*refs, tile):
    q_ref, k_ref, v_ref = refs[:3]
    g_refs = refs[3 : 3 + CHIPS]
    lse_ref, pq_ref, pk_ref, gq_ref, gk_ref, gv_ref, sums_ref, ak_ref, av_ref = refs[3 + CHIPS :]
    own = q_ref.shape[0] // CHIPS
    sums_ref[...] = jnp.zeros_like(sums_ref)
    for head in range(HEADS_HERE):
        span = slice(head * HEAD_DIM, (head + 1) * HEAD_DIM)
        k_head = k_ref[:, span]
        v_head = v_ref[:, span]
        k_turned = k_head.T
        for t in range(q_ref.shape[0] // tile):
            rows = slice(t * tile, (t + 1) * tile)
            low = t * tile % own
            q_tile = q_ref[rows, span]
            g_tile = g_refs[t * tile // own][low : low + tile, span]
            scores = dot_right(k_head, q_tile) * score_scale
            allowed = pq_ref[:, rows] >= pk_ref[...]
            scores = jnp.where(allowed, scores, masked_score)
            probs = jnp.exp(scores - lse_ref[head : head + 1, rows])
            grad_probs = dot_right(v_head, g_tile)
            delta = jnp.sum(probs * grad_probs, axis=0, keepdims=True)
            grad_scores = (probs * (grad_probs - delta)).astype(bf16)
            grad_query = dot(k_turned, grad_scores).T * score_scale
            gq_ref[rows, span] = grad_query.astype(bf16)
            sums_ref[0:1, span] += column_total(grad_query)
            if t == 0:
                ak_ref[...] = dot(grad_scores, q_tile)
                av_ref[...] = dot(probs.astype(bf16), g_tile)
            else:
                ak_ref[...] += dot(grad_scores, q_tile)
                av_ref[...] += dot(probs.astype(bf16), g_tile)
        gk_ref[:, span] = (ak_ref[...] * score_scale).astype(gk_ref.dtype)
        gv_ref[:, span] = av_ref[...].astype(gv_ref.dtype)
        sums_ref[1:2, span] = column_total(av_ref[...])


def qkv_back_kernel(gq_ref, gk_ref, gv_ref, w_ref, *part_refs):
    own = gq_ref.shape[0] // CHIPS
    for mask in range(CHIPS):
        rows = slice(mask * own, (mask + 1) * own)
        part_refs[mask][...] = (
            dot_right(gq_ref[rows, :], w_ref[:, :COLS])
            + dot_right(gk_ref[rows, :], w_ref[:, COLS : 2 * COLS])
            + dot_right(gv_ref[rows, :], w_ref[:, 2 * COLS :])
        ).astype(part_refs[mask].dtype)


def hidden_kernel(res_ref, *refs):
    parts, (own_ref, send_ref) = refs[:CHIPS], refs[CHIPS:]
    total = res_ref[...] + tree_sum(ref[...].astype(f32) for ref in parts)
    rows = own_ref.shape[0]
    own_ref[...] = total[:rows, :]
    send_ref[...] = total[rows:, :]


def late_grad_kernel(n_shard, ids_ref, *refs):
    k = ids_ref[IK]
    acts, feeds, firsts, inners = (refs[i * CHIPS : (i + 1) * CHIPS] for i in range(4))
    own_ref, send_ref, down_ref, in_ref = refs[4 * CHIPS :]
    down_ref[...] = tree_sum(dot_left(a[...], g[...]) for a, g in zip(acts, feeds))
    in_ref[...] = tree_sum(dot_left(a[...], g[...]) for a, g in zip(firsts, inners))
    few = FF // n_shard // GROUP
    rows_z = D // n_shard
    each = rows_z + 2 * few
    for goal_ref, half in ((own_ref, k), (send_ref, 1 - k)):
        lanes = aligned(half * HALF, HALF)
        for place in range(n_shard):
            base = place * each
            kind = goal_ref.dtype
            goal_ref[base : base + rows_z, :] = in_ref[
                place * rows_z : (place + 1) * rows_z, lanes
            ].astype(kind)
            rows = pl.ds(pl.multiple_of(half * HALF + place * few, few), few)
            goal_ref[base + rows_z : base + rows_z + few, :] = down_ref[rows, :HALF].astype(kind)
            goal_ref[base + rows_z + few : base + each, :] = down_ref[rows, HALF:].astype(kind)


def split_z_kernel(n_shard, ids_ref, own_ref, got_ref, *outs):
    z = ids_ref[IZ]
    each = outs[0].shape[0]
    for mask in range(n_shard):
        rows = aligned((z ^ mask) * each, each)
        outs[mask][...] = (own_ref[rows, :] + got_ref[rows, :].astype(f32)).astype(
            outs[mask].dtype
        )


def sum_kernel(*refs):
    refs[-1][...] = tree_sum(ref[...].astype(f32) for ref in refs[:-1]).astype(bf16)


def late_final_kernel(n_shard, ids_ref, *refs):
    k, j = ids_ref[IK], ids_ref[IJ]
    pieces = refs[:GROUP]
    in_latent_ref, down_latent_ref, in_ref, down_ref, all_ref = refs[GROUP:]
    few = FF // n_shard // GROUP
    rows_z = D // n_shard
    for core in range(CORES):
        for mask in range(CHIPS):
            ref = pieces[core * CHIPS + mask]
            all_ref[(j ^ mask) * CORES + (k ^ core)] = ref[...]
    for number in range(GROUP):
        for place in range(n_shard):
            goal = (place * GROUP + number) * few
            lanes = slice(goal, goal + few)
            grad = all_ref[number, 0:rows_z, place * few : (place + 1) * few].astype(f32)
            keep = jnp.abs(in_latent_ref[:, lanes]) <= 1.0
            in_ref[:, lanes] = jnp.where(keep, grad, 0.0)
        rows = slice(number * few, (number + 1) * few)
        for part in range(2):
            lanes = slice(part * HALF, (part + 1) * HALF)
            low = rows_z + part * few
            grad = all_ref[number, low : low + few, :].astype(f32)
            keep = jnp.abs(down_latent_ref[rows, lanes]) <= 1.0
            down_ref[rows, lanes] = jnp.where(keep, grad, 0.0)


def out_grad_kernel(n_shard, ids_ref, *refs):
    j = ids_ref[IJ]
    h_refs, grad_ref = refs[:CHIPS], refs[CHIPS]
    outs, (cols_ref, full_ref) = refs[CHIPS + 1 : CHIPS + 1 + CHIPS], refs[CHIPS + 1 + CHIPS :]
    half = D // n_shard // CORES
    for chip in range(CHIPS):
        cols_ref[chip] = grad_ref[:, chip * COLS : (chip + 1) * COLS]
    for goal in range(CHIPS):
        cols = cols_ref[j ^ goal]
        for mask in range(CHIPS):
            full_ref[aligned((j ^ mask) * COLS, COLS), :] = dot_left(h_refs[mask][...], cols)
        for core in range(CORES):
            for place in range(n_shard):
                low = (place * CORES + core) * half
                outs[goal][place * half : (place + 1) * half, core * COLS : (core + 1) * COLS] = (
                    full_ref[low : low + half, :].astype(outs[goal].dtype)
                )


def split_hi_lo(values):
    high = values.astype(bf16)
    low = (values - high.astype(f32)).astype(bf16)
    return high, low


def early_grad_kernel(n_shard, ids_ref, *refs):
    k = ids_ref[IK]
    own_x, oth_x, gq_ref, gk_ref, gv_ref = refs[:5]
    outs, refs = refs[5 : 5 + CHIPS], refs[5 + CHIPS :]
    branch_sums, loss_sums, res_sums = refs[:3]
    b1_sums, refs = refs[3 : 3 + CHIPS], refs[3 + CHIPS :]
    qv_sums, own_ref, vec_ref, send_ref, full_ref = refs
    half = D // n_shard // CORES
    rows = own_x.shape[0] // CHIPS
    for number, g_ref in enumerate((gq_ref, gk_ref, gv_ref)):
        parts = []
        for core, x_ref in enumerate((own_x, oth_x)):
            for mask in range(CHIPS):
                goal = slice((mask * CORES + core) * rows, (mask * CORES + core + 1) * rows)
                parts.append(dot_left(x_ref[mask * rows : (mask + 1) * rows, :], g_ref[goal, :]))
        full_ref[:, number * COLS : (number + 1) * COLS] = tree_sum(parts)
    total = tree_sum(ref[...].astype(f32) for ref in outs)
    for place in range(n_shard):
        for core in range(CORES):
            low = (place * CORES + core) * half
            full_ref[low : low + half, QKV:] = total[
                place * half : (place + 1) * half, core * COLS : (core + 1) * COLS
            ]
    for place in range(n_shard):
        goal = slice(place * half, (place + 1) * half)
        mine = pl.ds(pl.multiple_of((place * CORES + k) * half, half), half)
        theirs = pl.ds(pl.multiple_of((place * CORES + 1 - k) * half, half), half)
        own_ref[goal, :] = full_ref[mine, :]
        send_ref[goal, :] = full_ref[theirs, :].astype(bf16)
    lane = lax.broadcasted_iota(jnp.int32, (1, D), 1)
    stats = jnp.zeros((1, D), f32)
    for number, row in enumerate(
        (loss_sums[3:4, :], branch_sums[0:1, :], loss_sums[4:5, :], loss_sums[5:6, :])
    ):
        stats = stats + jnp.where(lane == number, jnp.sum(row, axis=1, keepdims=True), 0.0)
    table = jnp.concatenate(
        [
            res_sums[0:1, :],
            loss_sums[0:1, :],
            res_sums[1:3, :],
            loss_sums[1:3, :],
            stats,
            tree_sum(ref[0:1, :] for ref in b1_sums),
            jnp.concatenate(
                [qv_sums[0:1, :], qv_sums[1:2, :], jnp.zeros((1, D - 2 * COLS), f32)], axis=1
            ),
            jnp.zeros((VEC_ROWS - 9, D), f32),
        ]
    )
    high, low = split_hi_lo(table)
    base = n_shard * half
    send_ref[base : base + VEC_ROWS, :] = high
    send_ref[base + VEC_ROWS : base + 2 * VEC_ROWS, :] = low
    vec_ref[...] = high.astype(f32) + low.astype(f32)


def early_split_kernel(n_shard, ids_ref, own_ref, vec_ref, got_ref, *outs):
    z = ids_ref[IZ]
    half = D // n_shard // CORES
    base = n_shard * half
    table = vec_ref[...] + (
        got_ref[base : base + VEC_ROWS, :].astype(f32)
        + got_ref[base + VEC_ROWS : base + 2 * VEC_ROWS, :].astype(f32)
    )
    high, low = split_hi_lo(table)
    for mask in range(n_shard):
        rows = aligned((z ^ mask) * half, half)
        kind = outs[mask].dtype
        outs[mask][0:half, :] = (own_ref[rows, :] + got_ref[rows, :].astype(f32)).astype(kind)
        outs[mask][half : half + VEC_ROWS, :] = high.astype(kind)
        outs[mask][half + VEC_ROWS : half + 2 * VEC_ROWS, :] = low.astype(kind)


def early_sum_kernel(*refs):
    ins, out_ref = refs[:-1], refs[-1]
    half = out_ref.shape[0] - 2 * VEC_ROWS
    out_ref[0:half, :] = tree_sum(ref[0:half, :].astype(f32) for ref in ins).astype(bf16)
    table = tree_sum(
        ref[half : half + VEC_ROWS, :].astype(f32)
        + ref[half + VEC_ROWS : half + 2 * VEC_ROWS, :].astype(f32)
        for ref in ins
    )
    high, low = split_hi_lo(table)
    out_ref[half : half + VEC_ROWS, :] = high
    out_ref[half + VEC_ROWS : half + 2 * VEC_ROWS, :] = low


def early_final_kernel(n_shard, ids_ref, lengths_ref, *refs):
    k, j = ids_ref[IK], ids_ref[IJ]
    pieces = refs[:GROUP]
    latent_ref, attn_ref, vec_ref, query_ref, stats_ref, all_ref, rows_ref, flat_ref = refs[GROUP:]
    half = D // n_shard // CORES
    few = FF // n_shard // GROUP
    units = FF // n_shard
    for core in range(CORES):
        for mask in range(CHIPS):
            ref = pieces[core * CHIPS + mask]
            all_ref[(j ^ mask) * CORES + (k ^ core)] = ref[0:half, :]
    for chip in range(CHIPS):
        for core in range(CORES):
            for number in range(4):
                lanes = slice(chip * COLS, (chip + 1) * COLS)
                rows = slice(core * half, (core + 1) * half)
                grad = all_ref[
                    chip * CORES + core, :, number * COLS : (number + 1) * COLS
                ].astype(f32)
                keep = jnp.abs(latent_ref[number, rows, lanes]) <= 1.0
                attn_ref[number, rows, lanes] = jnp.where(keep, grad, 0.0)
    tables = [
        pieces[mask][half : half + VEC_ROWS, :].astype(f32)
        + pieces[mask][half + VEC_ROWS : half + 2 * VEC_ROWS, :].astype(f32)
        for mask in range(CHIPS)
    ]
    total = tree_sum(tables)
    for mask in range(CHIPS):
        rows_ref[j ^ mask] = tables[mask]
    count = lengths_ref[0]
    for number in range(1, lengths_ref.shape[0]):
        count = count + lengths_ref[number]
    scale = count.astype(f32) * D
    stats = total[ROW_STATS : ROW_STATS + 1, 0:128] / scale
    lane = lax.broadcasted_iota(jnp.int32, (1, 128), 1)
    stats_ref[...] = jnp.where(lane == 0, stats, jnp.sqrt(stats))
    vec_ref[1:7, :] = total[0:6, :]
    for chip in range(CHIPS):
        lanes = slice(chip * COLS, (chip + 1) * COLS)
        query_ref[:, lanes] = rows_ref[chip, ROW_QV : ROW_QV + 1, 0:COLS]
        vec_ref[0:1, lanes] = rows_ref[chip, ROW_QV : ROW_QV + 1, COLS : 2 * COLS]
        for core in range(CORES):
            for place in range(n_shard):
                start = place * units + (chip * CORES + core) * few
                row, lane = 7 + start // D, start % D
                vec_ref[row : row + 1, lane : lane + few] = rows_ref[
                    chip, ROW_B1 : ROW_B1 + 1, core * HALF + place * few : core * HALF + (place + 1) * few
                ]


def owners_kernel(ids_ref, here_ref, there_ref, out_ref):
    k = ids_ref[IK]
    out_ref[k] = here_ref[...]
    out_ref[1 - k] = there_ref[...]


def body(
    n_ctx,
    n_shard,
    hidden_in,
    block_of,
    lengths,
    attn_latent,
    ffn_in_latent,
    ffn_out_latent,
    student_vec,
    teacher_attn,
    teacher_ffn_in,
    teacher_ffn_out,
    teacher_vec,
):
    seqs, rows, _ = hidden_in.shape
    rest = n_ctx // GROUP
    own = seqs * rows
    tokens = CHIPS * own
    keys = rest * tokens
    ctx = lax.axis_index("ctx")
    z = lax.axis_index("shard")
    ids = jnp.stack([z, ctx % CORES, (ctx // CORES) % CHIPS, ctx // GROUP]).astype(jnp.int32)
    half = D // n_shard // CORES
    few = FF // n_shard // GROUP
    rows_z = D // n_shard
    each = rows_z + 2 * few

    def over_chips(piece, mask):
        return lax.ppermute(piece, "ctx", [(a, a ^ (mask * CORES)) for a in range(n_ctx)])

    def over_cores(piece):
        return lax.ppermute(piece, "ctx", [(a, a ^ 1) for a in range(n_ctx)])

    def over_rest(piece, mask):
        return lax.ppermute(piece, "ctx", [(a, a ^ (mask * GROUP)) for a in range(n_ctx)])

    def over_z(piece, mask):
        return lax.ppermute(piece, "shard", [(a, a ^ mask) for a in range(n_shard)])

    def gather_z(piece):
        return [piece] + [over_z(piece, m) for m in range(1, n_shard)]

    def gather_chips(piece):
        return [piece] + [over_chips(piece, m) for m in range(1, CHIPS)]

    def exchange_chips(pieces):
        return [pieces[0]] + [over_chips(pieces[m], m) for m in range(1, CHIPS)]

    def exchange_z(pieces):
        return [pieces[0]] + [over_z(pieces[m], m) for m in range(1, n_shard)]

    def both_cores(pieces):
        return list(pieces) + [over_cores(piece) for piece in pieces]

    pos_row, pos_col, valid = call(
        functools.partial(places_kernel, rest, seqs=seqs, rows=rows),
        "places",
        (
            shape((1, tokens), jnp.int32),
            shape((keys, 1), jnp.int32),
            shape((own, 1), f32),
        ),
        (ids, block_of, lengths),
        (),
    )
    sums = column_sums(attn_latent, ffn_in_latent, ffn_out_latent)
    sums = tree_sum(gather_z(sums))
    x_own, x_send = call(
        input_kernel,
        "input",
        (shape((tokens // CORES, D)), shape((tokens // CORES, D))),
        (ids,),
        gather_chips(hidden_in),
    )
    x_oth = over_cores(x_send)

    t_early, t_late = weight_pieces(n_shard, ids, teacher_attn, teacher_ffn_in, teacher_ffn_out)
    s_early, s_late = weight_pieces(
        n_shard, ids, attn_latent, ffn_in_latent, ffn_out_latent, sums
    )
    qkv_half, out_half = call(
        functools.partial(early_kernel, n_shard),
        "early_weights",
        (shape((2 * n_shard * half, QKV)), shape((n_shard * half, 2 * COLS))),
        (ids,),
        gather_z(t_early) + gather_z(s_early),
    )
    qkv_peer = over_cores(qkv_half)
    t_out, s_out = call(
        functools.partial(out_weight_kernel, n_shard),
        "out_weights",
        (shape((CHIPS, D, COLS)), shape((CHIPS, D, COLS))),
        (ids,),
        both_cores(gather_chips(out_half)),
    )

    def late_weights(piece, vector):
        return call(
            functools.partial(late_kernel, n_shard),
            "late_weights",
            (shape((D, UNITS)), shape((UNITS, D)), shape((8, UNITS), f32)),
            (ids,),
            both_cores(gather_z(piece)) + [vector],
        )

    t_late = late_weights(t_late, teacher_vec)
    s_late = late_weights(s_late, student_vec)

    def rest_gather(values):
        if rest == 1:
            return values
        return jnp.concatenate([values] + [over_rest(values, m) for m in range(1, rest)])

    def rest_scatter(partial):
        if rest == 1:
            return partial
        view = partial.reshape(rest, tokens, partial.shape[1])
        return tree_sum(
            [view[0]] + [over_rest(view[m].astype(bf16), m).astype(f32) for m in range(1, rest)]
        ).astype(bf16)

    def rest_total(piece):
        if rest == 1:
            return piece
        return call(
            early_sum_kernel if piece.shape[1] == D else sum_kernel,
            "rest_sum",
            shape(piece.shape),
            (),
            [piece] + [over_rest(piece, m) for m in range(1, rest)],
        )

    def attention(model, vector):
        query, key, value, w_qkv = call(
            functools.partial(qkv_kernel, n_shard, model),
            "qkv",
            (
                shape((tokens, COLS)),
                shape((tokens, COLS)),
                shape((tokens, COLS)),
                shape((D, QKV)),
            ),
            (ids,),
            (x_own, x_oth, qkv_half, qkv_peer, vector),
        )
        key, value = rest_gather(key), rest_gather(value)
        *heads, lse = call(
            functools.partial(attend_kernel, tile=own),
            "attend",
            tuple([shape((own, COLS))] * CHIPS + [shape((HEADS_HERE, tokens), f32)]),
            (),
            (query, key, value, pos_row, pos_col),
        )
        return query, key, value, w_qkv, lse, exchange_chips(heads)

    def branch(student, heads, w_out, vector):
        outs = [shape((own, D), f32), shape((own, D))]
        if student:
            outs += [shape((own, D), f32), shape((8, D), f32)]
        return call(
            functools.partial(branch_kernel, student),
            "branch",
            tuple(outs),
            (ids,),
            (*heads, w_out, x_own, x_oth, vector, valid),
        )

    def feed(student, piece, mask, late):
        outs = [shape((own, D), f32 if mask == 0 else bf16)]
        if student:
            outs += [shape((own, UNITS), f32), shape((own, UNITS))]
        return call(
            functools.partial(feed_kernel, student), "feed", tuple(outs), (), (piece, *late)
        )

    t_heads = attention(0, teacher_vec)[-1]
    query, key, value, w_qkv, lse, heads = attention(1, student_vec)

    t_first, sent = branch(False, t_heads, t_out, teacher_vec)
    parts = [feed(False, p, m, t_late)[0] for m, p in enumerate(gather_chips(sent))]
    target = call(
        target_kernel,
        "target",
        shape((own, D), f32),
        (),
        (*exchange_chips(parts), t_first, teacher_vec),
    )

    first, sent, residual, branch_sums = branch(True, heads, s_out, student_vec)
    firsts = gather_chips(sent)
    w_in, w_down, _ = s_late
    fed = [feed(True, p, m, s_late) for m, p in enumerate(firsts)]
    parts, inners, acts = ([f[i] for f in fed] for i in range(3))
    out, grad_second, sent, loss_sums = call(
        loss_kernel,
        "loss",
        (shape((own, D)), shape((own, D), f32), shape((own, D)), shape((8, D), f32)),
        (lengths,),
        (*exchange_chips(parts), first, student_vec, target, valid),
    )

    feeds = gather_chips(sent)
    backs = [
        call(
            feed_back_kernel,
            "feed_back",
            (
                shape((own, D), f32 if m == 0 else bf16),
                shape((own, UNITS)),
                shape((8, UNITS), f32),
            ),
            (),
            (feeds[m], inners[m], w_in, w_down),
        )
        for m in range(CHIPS)
    ]
    parts, grad_inners, b1_sums = ([b[i] for b in backs] for i in range(3))
    grad_res, grad_branch, *rest_outs = call(
        branch_back_kernel,
        "branch_back",
        tuple(
            [shape((own, D), f32), shape((own, D))]
            + [shape((own, COLS))] * CHIPS
            + [shape((8, D), f32)]
        ),
        (ids,),
        (*exchange_chips(parts), grad_second, residual, student_vec, s_out),
    )
    grad_heads, res_sums = exchange_chips(rest_outs[:CHIPS]), rest_outs[CHIPS]

    kind = bf16 if rest == 1 else f32
    grad_query, grad_key, grad_value, qv_sums = call(
        functools.partial(attend_back_kernel, tile=own),
        "attend_back",
        (
            shape((tokens, COLS)),
            shape((keys, COLS), kind),
            shape((keys, COLS), kind),
            shape((8, COLS), f32),
        ),
        (),
        (query, key, value, *grad_heads, lse, pos_row, pos_col),
        (pltpu.VMEM((keys, HEAD_DIM), f32), pltpu.VMEM((keys, HEAD_DIM), f32)),
    )
    grad_key, grad_value = rest_scatter(grad_key), rest_scatter(grad_value)
    parts = call(
        qkv_back_kernel,
        "qkv_back",
        tuple(shape((own, D), f32 if m == 0 else bf16) for m in range(CHIPS)),
        (),
        (grad_query, grad_key, grad_value, w_qkv),
    )
    here, there = call(
        hidden_kernel,
        "hidden",
        (shape((rows, D), f32), shape((rows, D), f32)),
        (),
        (grad_res, *exchange_chips(parts)),
    )

    def to_owners(here, there):
        return call(
            owners_kernel,
            "owners",
            shape((CORES, *here.shape), here.dtype),
            (ids,),
            (here, over_cores(there)),
        )

    grad_hidden = to_owners(here, there)
    output = to_owners(out[:rows], out[rows:])

    mine, send = call(
        functools.partial(late_grad_kernel, n_shard),
        "late_grad",
        (shape((n_shard * each, HALF), f32), shape((n_shard * each, HALF))),
        (ids,),
        (*acts, *feeds, *firsts, *grad_inners),
        (pltpu.VMEM((UNITS, D), f32), pltpu.VMEM((D, UNITS), f32)),
    )
    pieces = call(
        functools.partial(split_z_kernel, n_shard),
        "late_split",
        tuple(shape((each, HALF), f32 if m == 0 else bf16) for m in range(n_shard)),
        (ids,),
        (mine, over_cores(send)),
    )
    piece = call(sum_kernel, "late_sum", shape((each, HALF)), (), exchange_z(pieces))
    in_grad, down_grad = call(
        functools.partial(late_final_kernel, n_shard),
        "late_final",
        (shape(ffn_in_latent.shape, f32), shape(ffn_out_latent.shape, f32)),
        (ids,),
        (*both_cores(gather_chips(rest_total(piece))), ffn_in_latent, ffn_out_latent),
        (pltpu.VMEM((GROUP, each, HALF), bf16),),
    )

    pieces = call(
        functools.partial(out_grad_kernel, n_shard),
        "out_grad",
        tuple(
            shape((n_shard * half, 2 * COLS), f32 if m == 0 else bf16) for m in range(CHIPS)
        ),
        (ids,),
        (*heads, grad_branch),
        (pltpu.VMEM((CHIPS, own, COLS), bf16), pltpu.VMEM((D, COLS), f32)),
    )
    mine, table, send = call(
        functools.partial(early_grad_kernel, n_shard),
        "early_grad",
        (
            shape((n_shard * half, D), f32),
            shape((VEC_ROWS, D), f32),
            shape((n_shard * half + 2 * VEC_ROWS, D)),
        ),
        (ids,),
        (
            x_own,
            x_oth,
            grad_query,
            grad_key,
            grad_value,
            *exchange_chips(pieces),
            branch_sums,
            loss_sums,
            res_sums,
            *b1_sums,
            qv_sums,
        ),
        (pltpu.VMEM((D, D), f32),),
    )
    pieces = call(
        functools.partial(early_split_kernel, n_shard),
        "early_split",
        tuple(
            shape((half + 2 * VEC_ROWS, D), f32 if m == 0 else bf16) for m in range(n_shard)
        ),
        (ids,),
        (mine, table, over_cores(send)),
    )
    piece = call(
        early_sum_kernel, "early_sum", shape((half + 2 * VEC_ROWS, D)), (), exchange_z(pieces)
    )
    attn_grad, vec_grad, query_grad, stats = call(
        functools.partial(early_final_kernel, n_shard),
        "early_final",
        (
            shape(attn_latent.shape, f32),
            shape((7 + FF // D, D), f32),
            shape((1, D), f32),
            shape((1, 128), f32),
        ),
        (ids, lengths),
        (*both_cores(gather_chips(rest_total(piece))), attn_latent),
        (
            pltpu.VMEM((GROUP, half, D), bf16),
            pltpu.VMEM((CHIPS, VEC_ROWS, D), f32),
            pltpu.VMEM((8, D), f32),
        ),
    )
    return (
        output,
        stats[0, :4],
        grad_hidden,
        attn_grad,
        in_grad,
        down_grad,
        vec_grad,
        query_grad[0],
    )


def solution(mesh):
    n_ctx, n_shard = mesh.shape["ctx"], mesh.shape["shard"]
    in_specs = (
        P("shard", "ctx", None),
        P(),
        P(),
        P(None, "shard", None),
        P("shard", None),
        P("shard", None),
        P(),
        P(None, "shard", None),
        P("shard", None),
        P("shard", None),
        P(),
    )
    out_specs = (
        P("shard", "ctx", None),
        P(),
        P("shard", "ctx", None),
        P(None, "shard", None),
        P("shard", None),
        P("shard", None),
        P(),
        P(),
    )
    return jax.shard_map(
        functools.partial(body, n_ctx, n_shard),
        mesh=mesh,
        in_specs=in_specs,
        out_specs=out_specs,
        check_vma=False,
    )
```

```python
import functools

import jax
import jax.numpy as jnp
from jax import lax
from jax.experimental import pallas as pl
from jax.experimental.pallas import tpu as pltpu
from jax.sharding import Mesh
from jax.sharding import PartitionSpec as P

D = 768
HEADS = 12
HEAD_DIM = 64
FF = 3072
BLK = 64

CHIPS = 4
CORES = 2
GROUP = CHIPS * CORES
COLS = D // CHIPS
HEADS_HERE = HEADS // CHIPS
UNITS = FF // CHIPS
HALF = UNITS // CORES
QKV = 3 * COLS

norm_eps = 1e-05
attn_gains = (2.0, 2.0, 1.0, 4.0)
masked_score = -1e30
score_scale = HEAD_DIM ** (-0.5)
log2_e = 1.4426950408889634
bf16 = jnp.bfloat16
f32 = jnp.float32

IZ, IK, IJ, IR = 0, 1, 2, 3
ROW_BO, ROW_B2, ROW_G1, ROW_C1, ROW_G2, ROW_C2, ROW_STATS, ROW_B1, ROW_QV = range(9)
VEC_ROWS = 16

SMEM_SPEC = pl.BlockSpec(memory_space=pltpu.SMEM)
VMEM_SPEC = pl.BlockSpec(memory_space=pltpu.VMEM)


def dot(left_side, right_side):
    return jnp.dot(left_side, right_side, preferred_element_type=f32)


def dot_left(left_side, right_side):
    return lax.dot_general(
        left_side, right_side, (((0,), (0,)), ((), ())), preferred_element_type=f32
    )


def dot_right(left_side, right_side):
    return lax.dot_general(
        left_side, right_side, (((1,), (1,)), ((), ())), preferred_element_type=f32
    )


def normal_cdf(values):
    return 0.5 * (1.0 + lax.erf(values * 0.7071067811865476))


def tree_sum(items):
    items = list(items)
    while len(items) > 1:
        items = [items[i] + items[i + 1] for i in range(0, len(items), 2)]
    return items[0]


def aligned(start, size):
    return pl.ds(pl.multiple_of(start, size), size)


def shape(dims, kind=bf16):
    return jax.ShapeDtypeStruct(dims, kind)


def call(kernel, name, outs, scalars, arrays, scratch=(), limit=16):
    return pl.pallas_call(
        kernel,
        out_shape=outs,
        in_specs=[SMEM_SPEC] * len(scalars) + [VMEM_SPEC] * len(arrays),
        out_specs=jax.tree.map(lambda _: VMEM_SPEC, outs),
        scratch_shapes=list(scratch),
        compiler_params=pltpu.CompilerParams(vmem_limit_bytes=limit * 2**20),
        name=name,
    )(*scalars, *arrays)


def without_ids(kernel, ids_ref, *refs):
    kernel(*refs)


class Line:
    def __init__(self, ids):
        self.ids = ids

    def wait(self, *values):
        self.ids = lax.optimization_barrier((self.ids, *values))[0]

    def behind(self, *values):
        return lax.optimization_barrier((self.ids, *values))[1:]

    def __call__(self, kernel, name, outs, scalars, arrays, scratch=(), limit=16, bare=False):
        if bare:
            kernel = functools.partial(without_ids, kernel)
        result = call(kernel, name, outs, (self.ids, *scalars), arrays, scratch, limit)
        self.wait(jax.tree.leaves(result)[0])
        return result


def pick(place, options):
    value = options[0]
    for number, option in enumerate(options[1:], 1):
        value = jnp.where(place == number, option, value)
    return value


def sums_kernel(ids_ref, attn_ref, in_ref, out_ref, sums_ref):
    @pl.when(pl.program_id(0) == 0)
    def _():
        sums_ref[...] = jnp.zeros_like(sums_ref)

    for number in range(4):
        sums_ref[number : number + 1, :] += jnp.sum(
            jnp.abs(attn_ref[number]), axis=0, keepdims=True
        )
    for number in range(FF // D):
        sums_ref[4 + number : 5 + number, :] += jnp.sum(
            jnp.abs(in_ref[:, number * D : (number + 1) * D]), axis=0, keepdims=True
        )
    last = 4 + FF // D
    sums_ref[last : last + 1, :] += jnp.sum(jnp.abs(out_ref[...]), axis=0, keepdims=True)


def column_sums(ids, attn, w_in, w_down, steps=4):
    return pl.pallas_call(
        sums_kernel,
        out_shape=shape((16, D), f32),
        grid_spec=pltpu.PrefetchScalarGridSpec(
            num_scalar_prefetch=1,
            grid=(steps,),
            in_specs=[
                pl.BlockSpec((4, attn.shape[1] // steps, D), lambda i, ids: (0, i, 0)),
                pl.BlockSpec((w_in.shape[0] // steps, FF), lambda i, ids: (i, 0)),
                pl.BlockSpec((w_down.shape[0] // steps, D), lambda i, ids: (i, 0)),
            ],
            out_specs=pl.BlockSpec((16, D), lambda i, ids: (0, 0)),
        ),
        compiler_params=pltpu.CompilerParams(vmem_limit_bytes=16 * 2**20),
        name="column_sums",
    )(ids, attn, w_in, w_down)


def sign_of(values):
    return jnp.where(values > 0, 1.0, jnp.where(values < 0, -1.0, 0.0))


def choose(size, count, start):
    place = lax.broadcasted_iota(jnp.int32, (size, count), 0)
    goal = lax.broadcasted_iota(jnp.int32, (size, count), 1) + start
    return jnp.where(place == goal, 1.0, 0.0).astype(bf16)


def pieces_kernel(n_shard, student, ids_ref, attn_ref, in_ref, down_ref, early_ref, late_ref):
    k, j = ids_ref[IK], ids_ref[IJ]
    units = FF // n_shard
    few = units // GROUP
    rows_z = in_ref.shape[0]

    def travels(values):
        return sign_of(values).astype(bf16) if student else values

    chosen = choose(D, COLS, j * COLS)
    for number in range(4):
        early_ref[:, number * COLS : (number + 1) * COLS] = dot(
            travels(attn_ref[number]), chosen
        ).astype(bf16)
    chosen = choose(units, few, (j * CORES + k) * few)
    for place in range(n_shard):
        late_ref[0:rows_z, place * few : (place + 1) * few] = dot(
            travels(in_ref[:, place * units : (place + 1) * units]), chosen
        ).astype(bf16)
    full = travels(down_ref[...])
    late_ref[rows_z : rows_z + few, :] = full[:, :HALF]
    late_ref[rows_z + few : rows_z + 2 * few, :] = full[:, HALF:]


def weight_pieces(n_shard, student, ids, attn, w_in, w_down):
    half = attn.shape[1] // CORES
    few = FF // n_shard // GROUP
    rows_z = w_in.shape[0]
    return pl.pallas_call(
        functools.partial(pieces_kernel, n_shard, student),
        out_shape=(shape((half, D)), shape((rows_z + 2 * few, HALF))),
        grid_spec=pltpu.PrefetchScalarGridSpec(
            num_scalar_prefetch=1,
            grid=(1,),
            in_specs=[
                pl.BlockSpec((4, half, D), lambda i, ids: (0, ids[IK], 0)),
                pl.BlockSpec((rows_z, FF), lambda i, ids: (0, 0)),
                pl.BlockSpec((few, D), lambda i, ids: (CORES * ids[IJ] + ids[IK], 0)),
            ],
            out_specs=(
                pl.BlockSpec((half, D), lambda i, ids: (0, 0)),
                pl.BlockSpec((rows_z + 2 * few, HALF), lambda i, ids: (0, 0)),
            ),
        ),
        compiler_params=pltpu.CompilerParams(vmem_limit_bytes=24 * 2**20),
        name="student_pieces" if student else "teacher_pieces",
    )(ids, attn, w_in, w_down)


def scale_row(sums_ref, row, gain, fan_in):
    return gain * (sums_ref[row : row + 1, :] / fan_in) * fan_in ** (-0.5)


def scaled(values, scale):
    return (values.astype(f32) * scale).astype(bf16)


def early_kernel(n_shard, model, ids_ref, *refs):
    group, refs = refs[:n_shard], refs[n_shard:]
    qkv_ref, out_ref = refs[-2:]
    z = ids_ref[IZ]
    half = group[0].shape[0]
    fold = n_shard // 2
    base = model * fold * half
    if model:
        out_ref[0:base, :] = refs[0][...]
    for mask, ref in enumerate(group):
        place = z ^ mask
        qkv_ref[aligned(place * half, half), :] = ref[:, :QKV]
        low = pl.ds(pl.multiple_of(base + lax.rem(place, fold) * half, half), half)

        @pl.when(place < fold)
        def _():
            out_ref[low, 0:COLS] = ref[:, QKV:]

        @pl.when(place >= fold)
        def _():
            out_ref[low, COLS:] = ref[:, QKV:]


def out_weight_kernel(n_shard, ids_ref, *refs):
    k, j = ids_ref[IK], ids_ref[IJ]
    sums_ref, t_ref, s_ref, scale_ref = refs[2 * CHIPS :]
    scale = scale_row(sums_ref, 3, attn_gains[3], D)
    for chip in range(CHIPS):
        scale_ref[chip] = scale[:, chip * COLS : (chip + 1) * COLS]
    half = D // n_shard // CORES
    span = n_shard * half // 2
    for core in range(CORES):
        for mask in range(CHIPS):
            ref = refs[core * CHIPS + mask]
            for model, goal in enumerate((t_ref, s_ref)):
                for place in range(n_shard):
                    fold = n_shard // 2
                    low = model * span + (place % fold) * half
                    lanes = slice(0, COLS) if place < fold else slice(COLS, 2 * COLS)
                    rows = pl.ds(
                        pl.multiple_of((place * CORES + (k ^ core)) * half, half), half
                    )
                    piece = ref[low : low + half, lanes]
                    if model:
                        piece = scaled(piece, scale_ref[j ^ mask])
                    goal[j ^ mask, rows, :] = piece


def late_kernel(n_shard, student, ids_ref, all_ref, vec_ref, *refs):
    if student:
        sums_ref, in_ref, down_ref, b1_ref = refs
        down_scale = scale_row(sums_ref, 4 + FF // D, 1.0, FF)
    else:
        in_ref, down_ref, b1_ref = refs
    j = ids_ref[IJ]
    units = FF // n_shard
    few = units // GROUP
    rows_z = D // n_shard
    each = rows_z + 2 * few

    def mine(ref, row, core, place):
        options = []
        for chip in range(CHIPS):
            start = place * units + (chip * CORES + core) * few
            low, lane = row + start // D, start % D
            options.append(ref[low : low + 1, lane : lane + few])
        return pick(j, options)

    for core in range(CORES):
        lanes = slice(core * HALF, (core + 1) * HALF)
        if student:
            scale = jnp.concatenate(
                [mine(sums_ref, 4, core, place) for place in range(n_shard)], axis=1
            )
            scale = (scale / D) * D ** (-0.5)
        for place in range(n_shard):
            base = (place * CORES + core) * each
            piece = all_ref[base : base + rows_z, :]
            rows = slice(core * HALF + place * few, core * HALF + (place + 1) * few)
            left = all_ref[base + rows_z : base + rows_z + few, :]
            right = all_ref[base + rows_z + few : base + each, :]
            if student:
                piece = scaled(piece, scale)
                left = scaled(left, down_scale[:, :HALF])
                right = scaled(right, down_scale[:, HALF:])
            in_ref[place * rows_z : (place + 1) * rows_z, lanes] = piece
            down_ref[rows, 0:HALF] = left
            down_ref[rows, HALF:] = right
            b1_ref[0:1, rows] = mine(vec_ref, 8, core, place)


def places_kernel(rest, ids_ref, block_ref, lengths_ref, row_ref, col_ref, valid_ref, *, seqs, rows):
    z, k, j, r = ids_ref[IZ], ids_ref[IK], ids_ref[IJ], ids_ref[IR]
    length = lengths_ref[z * seqs + k]
    per = rows // BLK
    number = 0
    for far in range(rest):
        for mask in range(CHIPS):
            for half in range(CORES):
                for part in range(per):
                    block = ((((r ^ far) * CHIPS + (j ^ mask)) * CORES + (k ^ half)) * per) + part
                    base = block_ref[block] * BLK
                    goal = slice(number * BLK, (number + 1) * BLK)
                    col = base + lax.broadcasted_iota(jnp.int32, (BLK, 1), 0)
                    col_ref[goal, :] = col
                    if far == 0:
                        row_ref[:, goal] = base + lax.broadcasted_iota(jnp.int32, (1, BLK), 1)
                    if far == 0 and mask == 0:
                        valid_ref[goal, :] = jnp.where(col < length, 1.0, 0.0)
                    number += 1


def input_kernel(ids_ref, *refs):
    k = ids_ref[IK]
    own_ref, send_ref = refs[CHIPS:]
    rows = refs[0].shape[1]
    for mask in range(CHIPS):
        goal = slice(mask * rows, (mask + 1) * rows)
        own_ref[goal, :] = refs[mask][k]
        send_ref[goal, :] = refs[mask][1 - k]


def qkv_kernel(n_shard, student, ids_ref, own_ref, oth_ref, half_ref, peer_ref, vec_ref, *outs):
    k, j = ids_ref[IK], ids_ref[IJ]
    if student:
        sums_ref, outs = outs[0], outs[1:]
        scale = jnp.concatenate(
            [
                pick(
                    j,
                    [
                        scale_row(sums_ref, number, attn_gains[number], D)[
                            :, chip * COLS : (chip + 1) * COLS
                        ]
                        for chip in range(CHIPS)
                    ],
                )
                for number in range(3)
            ],
            axis=1,
        )
    q_ref, k_ref, v_ref, w_ref = outs
    half = D // n_shard // CORES
    for core, ref in enumerate((half_ref, peer_ref)):
        for place in range(n_shard):
            rows = pl.ds(pl.multiple_of((place * CORES + (k ^ core)) * half, half), half)
            piece = ref[place * half : (place + 1) * half, :]
            w_ref[rows, :] = scaled(piece, scale) if student else piece
    weight = w_ref[...]
    chips = [slice(chip * COLS, (chip + 1) * COLS) for chip in range(CHIPS)]
    q_bias = pick(j, [vec_ref[0:1, chip] for chip in chips])
    v_bias = pick(j, [vec_ref[1:2, chip] for chip in chips])
    rows = own_ref.shape[0] // CHIPS
    for core, ref in enumerate((own_ref, oth_ref)):
        for mask in range(CHIPS):
            result = dot(ref[mask * rows : (mask + 1) * rows, :], weight)
            goal = slice((mask * CORES + core) * rows, (mask * CORES + core + 1) * rows)
            sets = (
                (q_ref, result[:, :COLS] + q_bias),
                (k_ref, result[:, COLS : 2 * COLS]),
                (v_ref, result[:, 2 * COLS :] + v_bias),
            )
            for goal_ref, values in sets:
                for head in range(HEADS_HERE):
                    span = slice(head * HEAD_DIM, (head + 1) * HEAD_DIM)
                    goal_ref[head, goal, :] = values[:, span].astype(bf16)


def attend_kernel(q_ref, k_ref, v_ref, pq_ref, pk_ref, *outs, tile):
    o_refs, lse_ref, all_ref = outs[:CHIPS], outs[CHIPS], outs[CHIPS + 1]
    tokens = q_ref.shape[1]
    own = tokens // CHIPS

    def one_head(head, carry):
        k_head = k_ref[head]
        v_turned = v_ref[head].T
        for t in range(tokens // tile):
            rows = slice(t * tile, (t + 1) * tile)
            scores = dot_right(k_head, q_ref[head, rows, :]) * (score_scale * log2_e)
            allowed = pq_ref[:, rows] >= pk_ref[...]
            scores = jnp.where(allowed, scores, masked_score)
            peak = jnp.max(scores, axis=0, keepdims=True)
            powers = jnp.exp2(scores - peak)
            total = jnp.sum(powers, axis=0, keepdims=True)
            mixed = dot(v_turned, powers.astype(bf16)) / total
            all_ref[head, rows, :] = mixed.T.astype(bf16)
            lse_ref[head, :, rows] = peak + jnp.log2(total)
        return carry

    lax.fori_loop(0, HEADS_HERE, one_head, 0)
    for head in range(HEADS_HERE):
        span = slice(head * HEAD_DIM, (head + 1) * HEAD_DIM)
        for mask in range(CHIPS):
            o_refs[mask][:, span] = all_ref[head, mask * own : (mask + 1) * own, :]


def norm_parts(values):
    middle = jnp.mean(values, axis=-1, keepdims=True)
    centred = values - middle
    spread = jnp.mean(centred * centred, axis=-1, keepdims=True)
    inverse = lax.rsqrt(spread + norm_eps)
    return centred * inverse, inverse


def norm_back(values, gain, grad_out):
    normal, inverse = norm_parts(values)
    scaled = grad_out * gain
    grad_in = (
        scaled
        - jnp.mean(scaled, axis=-1, keepdims=True)
        - normal * jnp.mean(scaled * normal, axis=-1, keepdims=True)
    ) * inverse
    return grad_in, normal


def column_total(values):
    return jnp.sum(values, axis=0, keepdims=True)


def branch_kernel(student, ids_ref, *refs):
    j = ids_ref[IJ]
    h_refs, (w_ref, own_ref, oth_ref, vec_ref, valid_ref) = refs[:CHIPS], refs[CHIPS : CHIPS + 5]
    outs = refs[CHIPS + 5 :]
    first_ref, sent_ref = outs[:2]
    rows = own_ref.shape[0] // CHIPS
    if student:
        residual_ref, sums_ref = outs[2:]
        sums_ref[...] = jnp.zeros_like(sums_ref)
    for core, x_ref in enumerate((own_ref, oth_ref)):
        goal = slice(core * rows, (core + 1) * rows)
        parts = []
        for chip in range(CHIPS):
            parts.append(
                tree_sum(
                    dot(
                        h_refs[mask][goal, :],
                        w_ref[chip, aligned((j ^ mask) * COLS, COLS), :],
                    )
                    for mask in range(CHIPS)
                )
            )
        branch = jnp.concatenate(parts, axis=1) + vec_ref[2:3, :]
        residual = x_ref[0:rows, :].astype(f32) + branch
        normal, _ = norm_parts(residual)
        first = normal * vec_ref[4:5, :] + vec_ref[5:6, :]
        first_ref[goal, :] = first
        sent_ref[goal, :] = first.astype(bf16)
        if student:
            residual_ref[goal, :] = residual
            sums_ref[0:1, :] += column_total(valid_ref[goal, :] * branch * branch)


def feed_kernel(student, piece_ref, in_ref, down_ref, b1_ref, part_ref, *outs):
    inner = dot(piece_ref[...], in_ref[...]) + b1_ref[0:1, :]
    act = (inner * normal_cdf(inner)).astype(bf16)
    if student:
        outs[0][...] = inner
        outs[1][...] = act
    part_ref[...] = dot(act, down_ref[...]).astype(part_ref.dtype)


def target_kernel(*refs):
    parts, (first_ref, vec_ref, target_ref) = refs[:CHIPS], refs[CHIPS:]
    feed = tree_sum(ref[...].astype(f32) for ref in parts) + vec_ref[3:4, :]
    normal, _ = norm_parts(first_ref[...] + feed)
    target_ref[...] = normal * vec_ref[6:7, :] + vec_ref[7:8, :]


def loss_kernel(ids_ref, lengths_ref, *refs):
    parts, rest = refs[:CHIPS], refs[CHIPS:]
    first_ref, vec_ref, target_ref, valid_ref, out_ref, grad_ref, sent_ref, sums_ref = rest
    count = lengths_ref[0]
    for number in range(1, lengths_ref.shape[0]):
        count = count + lengths_ref[number]
    share = 1.0 / (count.astype(f32) * D)
    feed = tree_sum(ref[...].astype(f32) for ref in parts) + vec_ref[3:4, :]
    second = first_ref[...] + feed
    normal, inverse = norm_parts(second)
    out = normal * vec_ref[6:7, :] + vec_ref[7:8, :]
    out_ref[...] = out.astype(bf16)
    valid = valid_ref[...]
    mismatch = valid * (out - target_ref[...])
    grad_out = mismatch * share
    scaled = grad_out * vec_ref[6:7, :]
    grad = (
        scaled
        - jnp.mean(scaled, axis=-1, keepdims=True)
        - normal * jnp.mean(scaled * normal, axis=-1, keepdims=True)
    ) * inverse
    grad_ref[...] = grad
    sent_ref[...] = grad.astype(bf16)
    sums_ref[...] = jnp.concatenate(
        [
            column_total(grad),
            column_total(grad_out * normal),
            column_total(grad_out),
            0.5 * column_total(mismatch * mismatch),
            column_total(valid * feed * feed),
            column_total(valid * second * second),
            jnp.zeros((2, D), f32),
        ]
    )


def feed_back_kernel(piece_ref, inner_ref, in_ref, down_ref, part_ref, grad_ref, sum_ref):
    inner = inner_ref[...]
    slope = normal_cdf(inner) + inner * jnp.exp(-0.5 * inner * inner) * 0.3989422804014327
    grad = dot_right(piece_ref[...], down_ref[...]) * slope
    sum_ref[...] = jnp.broadcast_to(column_total(grad), sum_ref.shape)
    grad = grad.astype(bf16)
    grad_ref[...] = grad
    part_ref[...] = dot_right(grad, in_ref[...]).astype(part_ref.dtype)


def branch_back_kernel(ids_ref, *refs):
    j = ids_ref[IJ]
    parts, rest = refs[:CHIPS], refs[CHIPS:]
    second_ref, residual_ref, vec_ref, w_ref = rest[:4]
    grad_ref, sent_ref = rest[4:6]
    h_refs, (sums_ref,) = rest[6 : 6 + CHIPS], rest[6 + CHIPS :]
    grad_first = second_ref[...] + tree_sum(ref[...].astype(f32) for ref in parts)
    grad, normal = norm_back(residual_ref[...], vec_ref[4:5, :], grad_first)
    grad_ref[...] = grad
    sums_ref[...] = jnp.concatenate(
        [
            column_total(grad),
            column_total(grad_first * normal),
            column_total(grad_first),
            jnp.zeros((5, D), f32),
        ]
    )
    grad = grad.astype(bf16)
    sent_ref[...] = grad
    chips = [grad[:, chip * COLS : (chip + 1) * COLS] for chip in range(CHIPS)]
    for mask in range(CHIPS):
        rows = aligned((j ^ mask) * COLS, COLS)
        h_refs[mask][...] = tree_sum(
            dot_right(chips[chip], w_ref[chip, rows, :]) for chip in range(CHIPS)
        ).astype(bf16)


def attend_back_kernel(*refs, tile):
    q_ref, k_ref, v_ref = refs[:3]
    g_refs, refs = refs[3 : 3 + CHIPS], refs[3 + CHIPS :]
    lse_ref, pq_ref, pk_ref, gq_ref, gk_ref, gv_ref, sums_ref = refs[:7]
    g_all, aq_ref, ak_ref, av_ref = refs[7:]
    tokens = q_ref.shape[1]
    own = tokens // CHIPS
    for head in range(HEADS_HERE):
        span = slice(head * HEAD_DIM, (head + 1) * HEAD_DIM)
        for mask in range(CHIPS):
            g_all[head, mask * own : (mask + 1) * own, :] = g_refs[mask][:, span]

    def one_head(head, carry):
        k_head = k_ref[head]
        v_head = v_ref[head]
        k_turned = k_head.T
        for t in range(tokens // tile):
            rows = slice(t * tile, (t + 1) * tile)
            q_tile = q_ref[head, rows, :]
            g_tile = g_all[head, rows, :]
            scores = dot_right(k_head, q_tile) * (score_scale * log2_e)
            allowed = pq_ref[:, rows] >= pk_ref[...]
            scores = jnp.where(allowed, scores, masked_score)
            probs = jnp.exp2(scores - lse_ref[head, :, rows])
            grad_probs = dot_right(v_head, g_tile)
            delta = jnp.sum(probs * grad_probs, axis=0, keepdims=True)
            grad_scores = (probs * (grad_probs - delta)).astype(bf16)
            aq_ref[head, rows, :] = dot(k_turned, grad_scores).T * score_scale
            if t == 0:
                ak_ref[head] = dot(grad_scores, q_tile)
                av_ref[head] = dot(probs.astype(bf16), g_tile)
            else:
                ak_ref[head] += dot(grad_scores, q_tile)
                av_ref[head] += dot(probs.astype(bf16), g_tile)
        return carry

    lax.fori_loop(0, HEADS_HERE, one_head, 0)
    sums_ref[...] = jnp.zeros_like(sums_ref)
    for head in range(HEADS_HERE):
        span = slice(head * HEAD_DIM, (head + 1) * HEAD_DIM)
        grad_query = aq_ref[head]
        grad_value = av_ref[head]
        gq_ref[:, span] = grad_query.astype(bf16)
        gk_ref[:, span] = (ak_ref[head] * score_scale).astype(gk_ref.dtype)
        gv_ref[:, span] = grad_value.astype(gv_ref.dtype)
        sums_ref[0:1, span] = column_total(grad_query)
        sums_ref[1:2, span] = column_total(grad_value)


def qkv_back_kernel(gq_ref, gk_ref, gv_ref, w_ref, *part_refs):
    own = gq_ref.shape[0] // CHIPS
    for mask in range(CHIPS):
        rows = slice(mask * own, (mask + 1) * own)
        part_refs[mask][...] = (
            dot_right(gq_ref[rows, :], w_ref[:, :COLS])
            + dot_right(gk_ref[rows, :], w_ref[:, COLS : 2 * COLS])
            + dot_right(gv_ref[rows, :], w_ref[:, 2 * COLS :])
        ).astype(part_refs[mask].dtype)


def hidden_kernel(res_ref, *refs):
    parts, (own_ref, send_ref) = refs[:CHIPS], refs[CHIPS:]
    total = res_ref[...] + tree_sum(ref[...].astype(f32) for ref in parts)
    rows = own_ref.shape[0]
    own_ref[...] = total[:rows, :]
    send_ref[...] = total[rows:, :]


def late_grad_kernel(n_shard, *refs):
    acts, feeds, firsts, inners = (refs[i * CHIPS : (i + 1) * CHIPS] for i in range(4))
    all_ref, down_ref, in_ref = refs[4 * CHIPS :]
    down_ref[...] = tree_sum(dot_left(a[...], g[...]) for a, g in zip(acts, feeds)).astype(bf16)
    in_ref[...] = tree_sum(dot_left(a[...], g[...]) for a, g in zip(firsts, inners)).astype(bf16)
    few = FF // n_shard // GROUP
    rows_z = D // n_shard
    each = rows_z + 2 * few
    for core in range(CORES):
        lanes = slice(core * HALF, (core + 1) * HALF)
        for place in range(n_shard):
            base = (place * CORES + core) * each
            all_ref[base : base + rows_z, :] = in_ref[place * rows_z : (place + 1) * rows_z, lanes]
            rows = slice(core * HALF + place * few, core * HALF + (place + 1) * few)
            all_ref[base + rows_z : base + rows_z + few, :] = down_ref[rows, :HALF]
            all_ref[base + rows_z + few : base + each, :] = down_ref[rows, HALF:]


def late_final_kernel(n_shard, all_ref, in_latent_ref, down_latent_ref, in_ref, down_ref):
    few = FF // n_shard // GROUP
    rows_z = D // n_shard
    each = rows_z + 2 * few
    for number in range(GROUP):
        base = number * each
        for place in range(n_shard):
            goal = (place * GROUP + number) * few
            lanes = slice(goal, goal + few)
            grad = all_ref[base : base + rows_z, place * few : (place + 1) * few].astype(f32)
            keep = jnp.abs(in_latent_ref[:, lanes]) <= 1.0
            in_ref[:, lanes] = jnp.where(keep, grad, 0.0)
        rows = slice(number * few, (number + 1) * few)
        for part in range(2):
            lanes = slice(part * HALF, (part + 1) * HALF)
            low = base + rows_z + part * few
            grad = all_ref[low : low + few, :].astype(f32)
            keep = jnp.abs(down_latent_ref[rows, lanes]) <= 1.0
            down_ref[rows, lanes] = jnp.where(keep, grad, 0.0)


def out_grad_kernel(n_shard, ids_ref, *refs):
    j = ids_ref[IJ]
    h_refs, grad_ref = refs[:CHIPS], refs[CHIPS]
    outs, (cols_ref, full_ref) = refs[CHIPS + 1 : CHIPS + 1 + CHIPS], refs[CHIPS + 1 + CHIPS :]
    half = D // n_shard // CORES
    for chip in range(CHIPS):
        cols_ref[chip] = grad_ref[:, chip * COLS : (chip + 1) * COLS]
    for goal in range(CHIPS):
        cols = cols_ref[j ^ goal]
        for mask in range(CHIPS):
            full_ref[aligned((j ^ mask) * COLS, COLS), :] = dot_left(h_refs[mask][...], cols)
        for core in range(CORES):
            for place in range(n_shard):
                low = (place * CORES + core) * half
                outs[goal][place * half : (place + 1) * half, core * COLS : (core + 1) * COLS] = (
                    full_ref[low : low + half, :].astype(outs[goal].dtype)
                )


def split_hi_lo(values):
    high = values.astype(bf16)
    low = (values - high.astype(f32)).astype(bf16)
    return high, low


def early_grad_kernel(n_shard, ids_ref, *refs):
    k = ids_ref[IK]
    own_x, oth_x, gq_ref, gk_ref, gv_ref = refs[:5]
    outs, refs = refs[5 : 5 + CHIPS], refs[5 + CHIPS :]
    branch_sums, loss_sums, res_sums = refs[:3]
    b1_sums, refs = refs[3 : 3 + CHIPS], refs[3 + CHIPS :]
    qv_sums, own_ref, vec_ref, send_ref, full_ref = refs
    half = D // n_shard // CORES
    rows = own_x.shape[0] // CHIPS
    for number, g_ref in enumerate((gq_ref, gk_ref, gv_ref)):
        parts = []
        for core, x_ref in enumerate((own_x, oth_x)):
            for mask in range(CHIPS):
                goal = slice((mask * CORES + core) * rows, (mask * CORES + core + 1) * rows)
                parts.append(dot_left(x_ref[mask * rows : (mask + 1) * rows, :], g_ref[goal, :]))
        full_ref[:, number * COLS : (number + 1) * COLS] = tree_sum(parts)
    total = tree_sum(ref[...].astype(f32) for ref in outs)
    for place in range(n_shard):
        for core in range(CORES):
            low = (place * CORES + core) * half
            full_ref[low : low + half, QKV:] = total[
                place * half : (place + 1) * half, core * COLS : (core + 1) * COLS
            ]
    for place in range(n_shard):
        goal = slice(place * half, (place + 1) * half)
        mine = pl.ds(pl.multiple_of((place * CORES + k) * half, half), half)
        theirs = pl.ds(pl.multiple_of((place * CORES + 1 - k) * half, half), half)
        own_ref[goal, :] = full_ref[mine, :]
        send_ref[goal, :] = full_ref[theirs, :].astype(bf16)
    lane = lax.broadcasted_iota(jnp.int32, (1, D), 1)
    stats = jnp.zeros((1, D), f32)
    for number, row in enumerate(
        (loss_sums[3:4, :], branch_sums[0:1, :], loss_sums[4:5, :], loss_sums[5:6, :])
    ):
        stats = stats + jnp.where(lane == number, jnp.sum(row, axis=1, keepdims=True), 0.0)
    table = jnp.concatenate(
        [
            res_sums[0:1, :],
            loss_sums[0:1, :],
            res_sums[1:3, :],
            loss_sums[1:3, :],
            stats,
            tree_sum(ref[0:1, :] for ref in b1_sums),
            jnp.concatenate(
                [qv_sums[0:1, :], qv_sums[1:2, :], jnp.zeros((1, D - 2 * COLS), f32)], axis=1
            ),
            jnp.zeros((VEC_ROWS - 9, D), f32),
        ]
    )
    high, low = split_hi_lo(table)
    base = n_shard * half
    send_ref[base : base + VEC_ROWS, :] = high
    send_ref[base + VEC_ROWS : base + 2 * VEC_ROWS, :] = low
    vec_ref[...] = high.astype(f32) + low.astype(f32)


def early_split_kernel(n_shard, ids_ref, own_ref, vec_ref, got_ref, *outs):
    z = ids_ref[IZ]
    half = D // n_shard // CORES
    base = n_shard * half
    table = vec_ref[...] + (
        got_ref[base : base + VEC_ROWS, :].astype(f32)
        + got_ref[base + VEC_ROWS : base + 2 * VEC_ROWS, :].astype(f32)
    )
    high, low = split_hi_lo(table)
    for mask in range(n_shard):
        rows = aligned((z ^ mask) * half, half)
        kind = outs[mask].dtype
        outs[mask][0:half, :] = (own_ref[rows, :] + got_ref[rows, :].astype(f32)).astype(kind)
        outs[mask][half : half + VEC_ROWS, :] = high.astype(kind)
        outs[mask][half + VEC_ROWS : half + 2 * VEC_ROWS, :] = low.astype(kind)


def early_sum_kernel(*refs):
    ins, out_ref = refs[:-1], refs[-1]
    half = out_ref.shape[0] - 2 * VEC_ROWS
    out_ref[0:half, :] = tree_sum(ref[0:half, :].astype(f32) for ref in ins).astype(bf16)
    table = tree_sum(
        ref[half : half + VEC_ROWS, :].astype(f32)
        + ref[half + VEC_ROWS : half + 2 * VEC_ROWS, :].astype(f32)
        for ref in ins
    )
    high, low = split_hi_lo(table)
    out_ref[half : half + VEC_ROWS, :] = high
    out_ref[half + VEC_ROWS : half + 2 * VEC_ROWS, :] = low


def early_final_kernel(n_shard, ids_ref, lengths_ref, *refs):
    k, j = ids_ref[IK], ids_ref[IJ]
    pieces = refs[:GROUP]
    latent_ref, attn_ref, vec_ref, query_ref, stats_ref, all_ref, rows_ref, flat_ref = refs[GROUP:]
    half = D // n_shard // CORES
    few = FF // n_shard // GROUP
    units = FF // n_shard
    for core in range(CORES):
        for mask in range(CHIPS):
            ref = pieces[core * CHIPS + mask]
            all_ref[(j ^ mask) * CORES + (k ^ core)] = ref[0:half, :]
    for chip in range(CHIPS):
        for core in range(CORES):
            for number in range(4):
                lanes = slice(chip * COLS, (chip + 1) * COLS)
                rows = slice(core * half, (core + 1) * half)
                grad = all_ref[
                    chip * CORES + core, :, number * COLS : (number + 1) * COLS
                ].astype(f32)
                keep = jnp.abs(latent_ref[number, rows, lanes]) <= 1.0
                attn_ref[number, rows, lanes] = jnp.where(keep, grad, 0.0)
    tables = [
        pieces[mask][half : half + VEC_ROWS, :].astype(f32)
        + pieces[mask][half + VEC_ROWS : half + 2 * VEC_ROWS, :].astype(f32)
        for mask in range(CHIPS)
    ]
    total = tree_sum(tables)
    for mask in range(CHIPS):
        rows_ref[j ^ mask] = tables[mask]
    count = lengths_ref[0]
    for number in range(1, lengths_ref.shape[0]):
        count = count + lengths_ref[number]
    scale = count.astype(f32) * D
    stats = total[ROW_STATS : ROW_STATS + 1, 0:128] / scale
    lane = lax.broadcasted_iota(jnp.int32, (1, 128), 1)
    stats_ref[...] = jnp.where(lane == 0, stats, jnp.sqrt(stats))
    vec_ref[1:7, :] = total[0:6, :]
    for chip in range(CHIPS):
        lanes = slice(chip * COLS, (chip + 1) * COLS)
        query_ref[:, lanes] = rows_ref[chip, ROW_QV : ROW_QV + 1, 0:COLS]
        vec_ref[0:1, lanes] = rows_ref[chip, ROW_QV : ROW_QV + 1, COLS : 2 * COLS]
        for core in range(CORES):
            for place in range(n_shard):
                start = place * units + (chip * CORES + core) * few
                row, lane = 7 + start // D, start % D
                vec_ref[row : row + 1, lane : lane + few] = rows_ref[
                    chip, ROW_B1 : ROW_B1 + 1, core * HALF + place * few : core * HALF + (place + 1) * few
                ]


def owners_kernel(ids_ref, here_ref, there_ref, out_ref):
    k = ids_ref[IK]
    out_ref[k] = here_ref[...]
    out_ref[1 - k] = there_ref[...]


def body(
    hidden_in,
    block_of,
    lengths,
    attn_latent,
    ffn_in_latent,
    ffn_out_latent,
    student_vec,
    teacher_attn,
    teacher_ffn_in,
    teacher_ffn_out,
    teacher_vec,
):
    seqs, rows, _ = hidden_in.shape
    rest = lax.axis_size("rest")
    n_shard = lax.axis_size("shard")
    own = seqs * rows
    tokens = CHIPS * own
    keys = rest * tokens
    ids = jnp.stack([lax.axis_index(name) for name in ("shard", "core", "chip", "rest")])
    half = D // n_shard // CORES
    few = FF // n_shard // GROUP
    rows_z = D // n_shard
    each = rows_z + 2 * few
    line = Line(ids.astype(jnp.int32))

    def flip(piece, axis, mask):
        size = lax.axis_size(axis)
        return lax.ppermute(piece, axis, [(a, a ^ mask) for a in range(size)])

    def gather(piece, axis):
        return [piece] + [flip(piece, axis, m) for m in range(1, lax.axis_size(axis))]

    def exchange(pieces, axis):
        return [pieces[0]] + [flip(pieces[m], axis, m) for m in range(1, len(pieces))]

    def swap(piece):
        return flip(piece, "core", 1)

    t_early, t_late = weight_pieces(
        n_shard, False, line.ids, teacher_attn, teacher_ffn_in, teacher_ffn_out
    )
    line.wait(t_early)
    s_early, s_late = weight_pieces(
        n_shard, True, line.ids, attn_latent, ffn_in_latent, ffn_out_latent
    )
    line.wait(s_early)
    sums = column_sums(line.ids, attn_latent, ffn_in_latent, ffn_out_latent)
    line.wait(sums)
    pos_row, pos_col, valid = line(
        functools.partial(places_kernel, rest, seqs=seqs, rows=rows),
        "places",
        (
            shape((1, tokens), jnp.int32),
            shape((keys, 1), jnp.int32),
            shape((own, 1), f32),
        ),
        (block_of, lengths),
        (),
    )
    for mask in (1 << bit for bit in range(n_shard.bit_length() - 1)):
        sums = sums + flip(sums, "shard", mask)
    t_late = lax.all_gather(t_late, ("shard", "core"), axis=0, tiled=True)
    s_late = lax.all_gather(s_late, ("shard", "core"), axis=0, tiled=True)

    t_qkv_half, t_out_half = line(
        functools.partial(early_kernel, n_shard, 0),
        "early_weights",
        (shape((n_shard * half, QKV)), shape((n_shard * half // 2, 2 * COLS))),
        (),
        gather(t_early, "shard"),
    )
    x_own, x_send = line(
        input_kernel,
        "input",
        (shape((tokens // CORES, D)), shape((tokens // CORES, D))),
        (),
        gather(hidden_in, "chip"),
    )
    x_oth = swap(x_send)

    def rest_gather(values):
        if rest == 1:
            return values
        return jnp.concatenate(gather(values, "rest"), axis=1)

    def rest_scatter(partial):
        if rest == 1:
            return partial
        view = partial.reshape(rest, tokens, COLS)
        return tree_sum(
            [view[0]]
            + [flip(view[m].astype(bf16), "rest", m).astype(f32) for m in range(1, rest)]
        ).astype(bf16)

    def project(student, qkv_half, vector):
        heads = shape((HEADS_HERE, tokens, HEAD_DIM))
        query, key, value, w_qkv = line(
            functools.partial(qkv_kernel, n_shard, student),
            "qkv",
            (heads, heads, heads, shape((D, QKV))),
            (),
            [x_own, x_oth, qkv_half, swap(qkv_half), vector] + [sums] * student,
        )
        return query, rest_gather(key), rest_gather(value), w_qkv

    def attend(query, key, value):
        *heads, lse = line(
            functools.partial(attend_kernel, tile=own),
            "attend",
            tuple([shape((own, COLS))] * CHIPS + [shape((HEADS_HERE, 1, tokens), f32)]),
            (),
            (query, key, value, pos_row, pos_col),
            (pltpu.VMEM((HEADS_HERE, tokens, HEAD_DIM), bf16),),
            limit=20 if rest == 1 else 48,
            bare=True,
        )
        return exchange(heads, "chip"), lse

    def branch(student, heads, w_out, vector):
        outs = [shape((own, D), f32), shape((own, D))]
        if student:
            outs += [shape((own, D), f32), shape((8, D), f32)]
        return line(
            functools.partial(branch_kernel, student),
            "branch",
            tuple(outs),
            (),
            (*heads, w_out, x_own, x_oth, vector, valid),
        )

    def late_weights(student, gathered, vector):
        return line(
            functools.partial(late_kernel, n_shard, student),
            "late_weights",
            (shape((D, UNITS)), shape((UNITS, D)), shape((8, UNITS), f32)),
            (),
            [gathered, vector] + [sums] * student,
        )

    def feed(student, piece, mask, late):
        outs = [shape((own, D), f32 if mask == 0 else bf16)]
        if student:
            outs += [shape((own, UNITS), f32), shape((own, UNITS))]
        return line(
            functools.partial(feed_kernel, student),
            "feed",
            tuple(outs),
            (),
            (piece, *late),
            bare=True,
        )

    t_query, t_key, t_value, _ = project(False, t_qkv_half, teacher_vec)
    s_qkv_half, out_half = line(
        functools.partial(early_kernel, n_shard, 1),
        "early_weights",
        (shape((n_shard * half, QKV)), shape((n_shard * half, 2 * COLS))),
        (),
        gather(s_early, "shard") + [t_out_half],
    )
    t_heads, _ = attend(t_query, t_key, t_value)
    query, key, value, w_qkv = project(True, s_qkv_half, student_vec)
    out_all = list(line.behind(*gather(out_half, "chip")))
    t_out, s_out = line(
        functools.partial(out_weight_kernel, n_shard),
        "out_weights",
        (shape((CHIPS, D, COLS)), shape((CHIPS, D, COLS))),
        (),
        out_all + [swap(piece) for piece in out_all] + [sums],
        (pltpu.VMEM((CHIPS, 1, COLS), f32),),
    )
    t_first, t_sent = branch(False, t_heads, t_out, teacher_vec)
    t_firsts = gather(t_sent, "chip")
    heads, lse = attend(query, key, value)
    t_late = late_weights(False, t_late, teacher_vec)
    t_parts = [feed(False, t_firsts[0], 0, t_late)[0]]
    first, sent, residual, branch_sums = branch(True, heads, s_out, student_vec)
    firsts = gather(sent, "chip")
    t_parts += [feed(False, t_firsts[m], m, t_late)[0] for m in range(1, CHIPS)]
    t_parts = exchange(t_parts, "chip")
    s_late = late_weights(True, s_late, student_vec)
    w_in, w_down, _ = s_late
    fed = [feed(True, firsts[m], m, s_late) for m in range(CHIPS)]
    parts, inners, acts = ([f[i] for f in fed] for i in range(3))
    target = line(
        target_kernel,
        "target",
        shape((own, D), f32),
        (),
        (*t_parts, t_first, teacher_vec),
        bare=True,
    )
    out, grad_second, sent, loss_sums = line(
        loss_kernel,
        "loss",
        (shape((own, D)), shape((own, D), f32), shape((own, D)), shape((8, D), f32)),
        (lengths,),
        (*exchange(parts, "chip"), first, student_vec, target, valid),
    )

    feeds = gather(sent, "chip")

    def to_owners(here, there):
        return line(
            owners_kernel,
            "owners",
            shape((CORES, *here.shape), here.dtype),
            (),
            (here, swap(there)),
        )

    output = to_owners(out[:rows], out[rows:])
    backs = [
        line(
            feed_back_kernel,
            "feed_back",
            (
                shape((own, D), f32 if m == 0 else bf16),
                shape((own, UNITS)),
                shape((8, UNITS), f32),
            ),
            (),
            (feeds[m], inners[m], w_in, w_down),
            bare=True,
        )
        for m in range(CHIPS)
    ]
    parts, grad_inners, b1_sums = ([b[i] for b in backs] for i in range(3))
    late_grad = line(
        functools.partial(late_grad_kernel, n_shard),
        "late_grad",
        shape((n_shard * CORES * each, HALF)),
        (),
        (*acts, *feeds, *firsts, *grad_inners),
        (pltpu.VMEM((UNITS, D), bf16), pltpu.VMEM((D, UNITS), bf16)),
        limit=24,
        bare=True,
    )
    grad_res, grad_branch, *rest_outs = line(
        branch_back_kernel,
        "branch_back",
        tuple(
            [shape((own, D), f32), shape((own, D))]
            + [shape((own, COLS))] * CHIPS
            + [shape((8, D), f32)]
        ),
        (),
        (*exchange(parts, "chip"), grad_second, residual, student_vec, s_out),
    )
    grad_heads, res_sums = exchange(rest_outs[:CHIPS], "chip"), rest_outs[CHIPS]
    line.wait(*grad_heads)
    out_parts = line(
        functools.partial(out_grad_kernel, n_shard),
        "out_grad",
        tuple(
            shape((n_shard * half, 2 * COLS), f32 if m == 0 else bf16) for m in range(CHIPS)
        ),
        (),
        (*heads, grad_branch),
        (pltpu.VMEM((CHIPS, own, COLS), bf16), pltpu.VMEM((D, COLS), f32)),
    )
    late = lax.psum_scatter(late_grad, ("shard", "core"), scatter_dimension=0, tiled=True)
    (late,) = line.behind(late)
    if rest > 1:
        late = lax.psum(late, "rest")
    late = lax.all_gather(late, ("chip", "core"), axis=0, tiled=True)
    kind = bf16 if rest == 1 else f32
    grad_query, grad_key, grad_value, qv_sums = line(
        functools.partial(attend_back_kernel, tile=own),
        "attend_back",
        (
            shape((tokens, COLS)),
            shape((keys, COLS), kind),
            shape((keys, COLS), kind),
            shape((8, COLS), f32),
        ),
        (),
        (query, key, value, *grad_heads, lse, pos_row, pos_col),
        (
            pltpu.VMEM((HEADS_HERE, tokens, HEAD_DIM), bf16),
            pltpu.VMEM((HEADS_HERE, tokens, HEAD_DIM), f32),
            pltpu.VMEM((HEADS_HERE, keys, HEAD_DIM), f32),
            pltpu.VMEM((HEADS_HERE, keys, HEAD_DIM), f32),
        ),
        limit=28 if rest == 1 else 56,
        bare=True,
    )
    grad_key, grad_value = rest_scatter(grad_key), rest_scatter(grad_value)
    mine, table, send = line(
        functools.partial(early_grad_kernel, n_shard),
        "early_grad",
        (
            shape((n_shard * half, D), f32),
            shape((VEC_ROWS, D), f32),
            shape((n_shard * half + 2 * VEC_ROWS, D)),
        ),
        (),
        (
            x_own,
            x_oth,
            grad_query,
            grad_key,
            grad_value,
            *exchange(out_parts, "chip"),
            branch_sums,
            loss_sums,
            res_sums,
            *b1_sums,
            qv_sums,
        ),
        (pltpu.VMEM((D, D), f32),),
        limit=20,
    )
    parts = line(
        qkv_back_kernel,
        "qkv_back",
        tuple(shape((own, D), f32 if m == 0 else bf16) for m in range(CHIPS)),
        (),
        (grad_query, grad_key, grad_value, w_qkv),
        bare=True,
    )
    pieces = line(
        functools.partial(early_split_kernel, n_shard),
        "early_split",
        tuple(
            shape((half + 2 * VEC_ROWS, D), f32 if m == 0 else bf16) for m in range(n_shard)
        ),
        (),
        (mine, table, swap(send)),
    )
    here, there = line(
        hidden_kernel,
        "hidden",
        (shape((rows, D), f32), shape((rows, D), f32)),
        (),
        (grad_res, *exchange(parts, "chip")),
        bare=True,
    )
    early = line(
        early_sum_kernel,
        "early_sum",
        shape((half + 2 * VEC_ROWS, D)),
        (),
        exchange(pieces, "shard"),
        bare=True,
    )
    if rest > 1:
        early = line(
            early_sum_kernel, "rest_sum", shape(early.shape), (), gather(early, "rest"), bare=True
        )
    early = gather(early, "chip")
    grad_hidden = to_owners(here, there)
    in_grad, down_grad = line(
        functools.partial(late_final_kernel, n_shard),
        "late_final",
        (shape(ffn_in_latent.shape, f32), shape(ffn_out_latent.shape, f32)),
        (),
        (late, ffn_in_latent, ffn_out_latent),
        bare=True,
    )
    early = list(line.behind(*early))
    attn_grad, vec_grad, query_grad, stats = line(
        functools.partial(early_final_kernel, n_shard),
        "early_final",
        (
            shape(attn_latent.shape, f32),
            shape((7 + FF // D, D), f32),
            shape((1, D), f32),
            shape((1, 128), f32),
        ),
        (lengths,),
        (*early, *[swap(piece) for piece in early], attn_latent),
        (
            pltpu.VMEM((GROUP, half, D), bf16),
            pltpu.VMEM((CHIPS, VEC_ROWS, D), f32),
            pltpu.VMEM((8, D), f32),
        ),
    )
    return (
        output,
        stats[0, :4],
        grad_hidden,
        attn_grad,
        in_grad,
        down_grad,
        vec_grad,
        query_grad[0],
    )


def solution(mesh):
    n_ctx, n_shard = mesh.shape["ctx"], mesh.shape["shard"]
    places = mesh.devices.reshape(n_ctx // GROUP, CHIPS, CORES, n_shard)
    inner = Mesh(places, ("rest", "chip", "core", "shard"))
    ctx = ("rest", "chip", "core")
    in_specs = (
        P("shard", ctx, None),
        P(),
        P(),
        P(None, "shard", None),
        P("shard", None),
        P("shard", None),
        P(),
        P(None, "shard", None),
        P("shard", None),
        P("shard", None),
        P(),
    )
    out_specs = (
        P("shard", ctx, None),
        P(),
        P("shard", ctx, None),
        P(None, "shard", None),
        P("shard", None),
        P("shard", None),
        P(),
        P(),
    )
    return jax.shard_map(
        body, mesh=inner, in_specs=in_specs, out_specs=out_specs, check_vma=False
    )
```

```python
import functools

import jax
import jax.numpy as jnp
from jax import lax
from jax.experimental import pallas as pl
from jax.experimental.pallas import tpu as pltpu
from jax.sharding import Mesh
from jax.sharding import PartitionSpec as P

D = 768
HEADS = 12
HEAD_DIM = 64
FF = 3072
BLK = 64

CHIPS = 4
CORES = 2
GROUP = CHIPS * CORES
COLS = D // CHIPS
HEADS_HERE = HEADS // CHIPS
UNITS = FF // CHIPS
HALF = UNITS // CORES
QKV = 3 * COLS

norm_eps = 1e-05
attn_gains = (2.0, 2.0, 1.0, 4.0)
masked_score = -1e30
score_scale = HEAD_DIM ** (-0.5)
log2_e = 1.4426950408889634
bf16 = jnp.bfloat16
f32 = jnp.float32

IZ, IK, IJ, IR = 0, 1, 2, 3
ROW_BO, ROW_B2, ROW_G1, ROW_C1, ROW_G2, ROW_C2, ROW_B1, ROW_QV = range(8)
VEC_ROWS = 8
EXTRA = 16

SMEM_SPEC = pl.BlockSpec(memory_space=pltpu.SMEM)
HBM_SPEC = pl.BlockSpec(memory_space=pltpu.HBM)
VMEM_SPEC = pl.BlockSpec(memory_space=pltpu.VMEM)


def dot(left_side, right_side):
    return jnp.dot(left_side, right_side, preferred_element_type=f32)


def dot_left(left_side, right_side):
    return lax.dot_general(
        left_side, right_side, (((0,), (0,)), ((), ())), preferred_element_type=f32
    )


def dot_right(left_side, right_side):
    return lax.dot_general(
        left_side, right_side, (((1,), (1,)), ((), ())), preferred_element_type=f32
    )


def normal_cdf(values):
    return 0.5 * (1.0 + lax.erf(values * 0.7071067811865476))


def tree_sum(items):
    items = list(items)
    while len(items) > 1:
        items = [items[i] + items[i + 1] for i in range(0, len(items), 2)]
    return items[0]


def aligned(start, size):
    return pl.ds(pl.multiple_of(start, size), size)


def shape(dims, kind=bf16):
    return jax.ShapeDtypeStruct(dims, kind)


def call(kernel, name, outs, scalars, arrays, scratch=(), limit=16):
    return pl.pallas_call(
        kernel,
        out_shape=outs,
        in_specs=[SMEM_SPEC] * len(scalars) + [VMEM_SPEC] * len(arrays),
        out_specs=jax.tree.map(lambda _: VMEM_SPEC, outs),
        scratch_shapes=list(scratch),
        compiler_params=pltpu.CompilerParams(vmem_limit_bytes=limit * 2**20),
        name=name,
    )(*scalars, *arrays)


def without_ids(kernel, ids_ref, *refs):
    kernel(*refs)


class Line:
    def __init__(self, ids):
        self.ids = ids

    def wait(self, *values):
        self.ids = lax.optimization_barrier((self.ids, *values))[0]

    def behind(self, *values):
        return lax.optimization_barrier((self.ids, *values))[1:]

    def __call__(self, kernel, name, outs, scalars, arrays, scratch=(), limit=16, bare=False):
        if bare:
            kernel = functools.partial(without_ids, kernel)
        result = call(kernel, name, outs, (self.ids, *scalars), arrays, scratch, limit)
        self.wait(jax.tree.leaves(result)[0])
        return result


def pick(place, options):
    value = options[0]
    for number, option in enumerate(options[1:], 1):
        value = jnp.where(place == number, option, value)
    return value


def split_three(values):
    high = values.astype(bf16)
    rest = values - high.astype(f32)
    middle = rest.astype(bf16)
    return high, middle, (rest - middle.astype(f32)).astype(bf16)


def join_three(ref, row, *index):
    return tree_sum(
        [ref[(*index, slice(row + part, row + part + 1))].astype(f32) for part in range(3)]
        + [0.0]
    )


def sign_of(values):
    return jnp.where(values > 0, 1.0, jnp.where(values < 0, -1.0, 0.0))


def choose(size, count, start):
    place = lax.broadcasted_iota(jnp.int32, (size, count), 0)
    goal = lax.broadcasted_iota(jnp.int32, (size, count), 1) + start
    return jnp.where(place == goal, 1.0, 0.0).astype(bf16)


def early_pieces_kernel(student, ids_ref, attn_hbm, early_ref, attn_ref, sem):
    k, j = ids_ref[IK], ids_ref[IJ]
    rows_z = attn_hbm.shape[1]
    half = rows_z // CORES
    if student:
        copy = pltpu.make_async_copy(attn_hbm, attn_ref, sem)
    else:
        copy = pltpu.make_async_copy(attn_hbm.at[:, aligned(k * half, half), :], attn_ref, sem)
    copy.start()
    chosen = choose(D, COLS, j * COLS)
    if student:
        early_ref[half:, :] = jnp.zeros((EXTRA, D), bf16)
    copy.wait()
    for number in range(4):
        lanes = slice(number * COLS, (number + 1) * COLS)
        if student:
            full = sign_of(attn_ref[number, aligned(k * half, half), :]).astype(bf16)
            sums = column_total(jnp.abs(attn_ref[number]))
            sums = pick(j, [sums[:, chip * COLS : (chip + 1) * COLS] for chip in range(CHIPS)])
            for part, row in enumerate(split_three(sums)):
                early_ref[half + part : half + part + 1, lanes] = row
        else:
            full = attn_ref[number]
        early_ref[0:half, lanes] = dot(full, chosen).astype(bf16)


def early_pieces(line, student, attn):
    half = attn.shape[1] // CORES
    result = pl.pallas_call(
        functools.partial(early_pieces_kernel, student),
        out_shape=shape((half + EXTRA * student, D)),
        in_specs=[SMEM_SPEC, HBM_SPEC],
        out_specs=VMEM_SPEC,
        scratch_shapes=[
            pltpu.VMEM((4, attn.shape[1] if student else half, D), attn.dtype),
            pltpu.SemaphoreType.DMA,
        ],
        compiler_params=pltpu.CompilerParams(vmem_limit_bytes=12 * 2**20),
        name="early_pieces",
    )(line.ids, attn)
    line.wait(result)
    return result


def late_pieces_kernel(
    n_shard, student, ids_ref, in_hbm, down_hbm, late_ref, in_ref, down_ref, sems
):
    k, j = ids_ref[IK], ids_ref[IJ]
    units = FF // n_shard
    few = units // GROUP
    rows_z = in_ref.shape[0]
    each = rows_z + 2 * few
    number = j * CORES + k
    mine = aligned(number * few, few)
    down_hbm = down_hbm if student else down_hbm.at[mine, :]
    copies = [
        pltpu.make_async_copy(in_hbm, in_ref, sems.at[0]),
        pltpu.make_async_copy(down_hbm, down_ref, sems.at[1]),
    ]
    for copy in copies:
        copy.start()
    chosen = choose(units, few, number * few)
    copies[1].wait()
    if student:
        full = sign_of(down_ref[mine, :]).astype(bf16)
        late_ref[each:, :] = jnp.zeros((EXTRA, HALF), bf16)
        for part, row in enumerate(split_three(column_total(jnp.abs(down_ref[...])))):
            low = each + 3 + part
            late_ref[low : low + 1, :] = row[:, :HALF]
            late_ref[low + 3 : low + 4, :] = row[:, HALF:]
    else:
        full = down_ref[...]
    late_ref[rows_z : rows_z + few, :] = full[:, :HALF]
    late_ref[rows_z + few : each, :] = full[:, HALF:]
    copies[0].wait()
    for place in range(n_shard):
        lanes = slice(place * few, (place + 1) * few)
        full = in_ref[:, place * units : (place + 1) * units]
        if student:
            sums = column_total(jnp.abs(full))
            sums = pick(number, [sums[:, n * few : (n + 1) * few] for n in range(GROUP)])
            for part, row in enumerate(split_three(sums)):
                late_ref[each + part : each + part + 1, lanes] = row
            full = sign_of(full).astype(bf16)
        late_ref[0:rows_z, lanes] = dot(full, chosen).astype(bf16)


def late_pieces(line, n_shard, student, w_in, w_down):
    few = FF // n_shard // GROUP
    rows_z = w_in.shape[0]
    result = pl.pallas_call(
        functools.partial(late_pieces_kernel, n_shard, student),
        out_shape=shape((rows_z + 2 * few + EXTRA * student, HALF)),
        in_specs=[SMEM_SPEC, HBM_SPEC, HBM_SPEC],
        out_specs=VMEM_SPEC,
        scratch_shapes=[
            pltpu.VMEM((rows_z, FF), w_in.dtype),
            pltpu.VMEM((w_down.shape[0] if student else few, D), w_down.dtype),
            pltpu.SemaphoreType.DMA((2,)),
        ],
        compiler_params=pltpu.CompilerParams(vmem_limit_bytes=20 * 2**20),
        name="late_pieces",
    )(line.ids, w_in, w_down)
    line.wait(result)
    return result


def scale_row(sums, gain, fan_in):
    return gain * (sums / fan_in) * fan_in ** (-0.5)


def scaled(values, scale):
    return (values.astype(f32) * scale).astype(bf16)


def early_kernel(n_shard, model, ids_ref, *refs):
    group, refs = refs[:n_shard], refs[n_shard:]
    qkv_ref, out_ref = refs[-2:]
    z = ids_ref[IZ]
    half = D // n_shard // CORES
    fold = n_shard // 2
    base = model * fold * half
    if model:
        out_ref[0:base, :] = refs[0][...]
        sums = tree_sum(join_three(ref, half) for ref in group)
        scale = jnp.concatenate(
            [
                scale_row(sums[:, number * COLS : (number + 1) * COLS], attn_gains[number], D)
                for number in range(4)
            ],
            axis=1,
        )
    for mask, ref in enumerate(group):
        place = z ^ mask
        piece = ref[0:half, :]
        if model:
            piece = scaled(piece, scale)
        qkv_ref[aligned(place * half, half), :] = piece[:, :QKV]
        low = pl.ds(pl.multiple_of(base + lax.rem(place, fold) * half, half), half)

        @pl.when(place < fold)
        def _():
            out_ref[low, 0:COLS] = piece[:, QKV:]

        @pl.when(place >= fold)
        def _():
            out_ref[low, COLS:] = piece[:, QKV:]


def out_weight_kernel(n_shard, ids_ref, *refs):
    k, j = ids_ref[IK], ids_ref[IJ]
    t_ref, s_ref = refs[2 * CHIPS :]
    half = D // n_shard // CORES
    span = n_shard * half // 2
    for core in range(CORES):
        for mask in range(CHIPS):
            ref = refs[core * CHIPS + mask]
            for model, goal in enumerate((t_ref, s_ref)):
                for place in range(n_shard):
                    fold = n_shard // 2
                    low = model * span + (place % fold) * half
                    lanes = slice(0, COLS) if place < fold else slice(COLS, 2 * COLS)
                    rows = pl.ds(
                        pl.multiple_of((place * CORES + (k ^ core)) * half, half), half
                    )
                    goal[j ^ mask, rows, :] = ref[low : low + half, lanes]


def merge_kernel(bit, ids_ref, own_ref, got_ref, both_ref):
    size = own_ref.shape[0]
    mine = (ids_ref[IZ] >> bit) & 1
    both_ref[pl.ds(mine * size, size)] = own_ref[...]
    both_ref[pl.ds((1 - mine) * size, size)] = got_ref[...]


def late_kernel(n_shard, student, ids_ref, *refs):
    groups, vec_ref, refs = refs[:4], refs[4], refs[5:]
    in_ref, down_ref, b1_ref = refs
    z, k, j = ids_ref[IZ], ids_ref[IK], ids_ref[IJ]
    units = FF // n_shard
    few = units // GROUP
    rows_z = D // n_shard
    each = rows_z + 2 * few
    fold = n_shard // 2
    side = lax.div(z, fold)

    def mine(ref, row, core, place):
        options = []
        for chip in range(CHIPS):
            start = place * units + (chip * CORES + core) * few
            low, lane = row + start // D, start % D
            options.append(ref[low : low + 1, lane : lane + few])
        return pick(j, options)

    for core in range(CORES):
        for place in range(n_shard):
            goal = slice(core * HALF + place * few, core * HALF + (place + 1) * few)
            b1_ref[0:1, goal] = mine(vec_ref, 8, core, place)
    if student:
        sums = [
            tree_sum(
                join_three(groups[far], each + 3 * part, number)
                for far in range(2)
                for number in range(fold)
            )
            for part in (1, 2)
        ]
        left_scale, right_scale = (scale_row(row, 1.0, FF) for row in sums)
    for core in range(CORES):
        which = k ^ core
        lanes = aligned(which * HALF, HALF)
        if student:
            scale = tree_sum(
                join_three(groups[core * 2 + far], each, number)
                for far in range(2)
                for number in range(fold)
            )
            scale = scale_row(scale, 1.0, D)
        for far in range(2):
            ref = groups[core * 2 + far]
            for number in range(fold):
                place = (side ^ far) * fold + number
                piece = ref[number, 0:rows_z, :]
                left = ref[number, rows_z : rows_z + few, :]
                right = ref[number, rows_z + few : each, :]
                if student:
                    piece = scaled(piece, scale)
                    left = scaled(left, left_scale)
                    right = scaled(right, right_scale)
                in_ref[aligned(place * rows_z, rows_z), lanes] = piece
                rows = pl.ds(pl.multiple_of(which * HALF + place * few, few), few)
                down_ref[rows, 0:HALF] = left
                down_ref[rows, HALF:] = right


def block_place(rest, per, ids_ref, block_ref, far, mask, core, part):
    k, j, r = ids_ref[IK], ids_ref[IJ], ids_ref[IR]
    chip = (r ^ far) * CHIPS + (j ^ mask)
    return block_ref[(chip * CORES + (k ^ core)) * per + part]


def places_kernel(rest, ids_ref, block_ref, lengths_ref, valid_ref, *outs, seqs, rows):
    length = lengths_ref[ids_ref[IZ] * seqs + ids_ref[IK]]
    per = rows // BLK
    number = 0
    for far in range(rest):
        for mask in range(CHIPS):
            for core in range(CORES):
                for part in range(per):
                    goal = slice(number * BLK, (number + 1) * BLK)
                    number += 1
                    if not outs and mask:
                        continue
                    base = block_place(rest, per, ids_ref, block_ref, far, mask, core, part) * BLK
                    col = base + lax.broadcasted_iota(jnp.int32, (BLK, 1), 0)
                    if far == 0 and mask == 0:
                        valid_ref[goal, :] = jnp.where(col < length, 1.0, 0.0)
                    if outs:
                        outs[1][goal, :] = col
                        if far == 0:
                            row = lax.broadcasted_iota(jnp.int32, (1, BLK), 1)
                            outs[0][:, goal] = base + row


def input_kernel(ids_ref, here_ref, x_ref, y_ref, xy0_ref, xy1_ref, own_ref, send_ref):
    k = ids_ref[IK]
    rows = here_ref.shape[1]
    for mask, ref in enumerate((here_ref, x_ref, y_ref)):
        goal = slice(mask * rows, (mask + 1) * rows)
        own_ref[goal, :] = ref[k]
        send_ref[goal, :] = ref[1 - k]
    goal = slice(3 * rows, 4 * rows)

    @pl.when(k == 0)
    def _():
        own_ref[goal, :] = xy0_ref[...]
        send_ref[goal, :] = xy1_ref[...]

    @pl.when(k == 1)
    def _():
        own_ref[goal, :] = xy1_ref[...]
        send_ref[goal, :] = xy0_ref[...]


def qkv_kernel(n_shard, rest, ids_ref, block_ref, own_ref, oth_ref, half_ref, peer_ref, vec_ref, *outs):
    k, j = ids_ref[IK], ids_ref[IJ]
    q_ref, k_ref, v_ref, w_ref = outs
    half = D // n_shard // CORES
    for core, ref in enumerate((half_ref, peer_ref)):
        for place in range(n_shard):
            rows = pl.ds(pl.multiple_of((place * CORES + (k ^ core)) * half, half), half)
            w_ref[rows, :] = ref[place * half : (place + 1) * half, :]
    weight = w_ref[...]
    chips = [slice(chip * COLS, (chip + 1) * COLS) for chip in range(CHIPS)]
    q_bias = pick(j, [vec_ref[0:1, chip] for chip in chips])
    v_bias = pick(j, [vec_ref[1:2, chip] for chip in chips])
    rows = own_ref.shape[0] // CHIPS
    per = rows // BLK
    for core, ref in enumerate((own_ref, oth_ref)):
        for mask in range(CHIPS):
            result = dot(ref[mask * rows : (mask + 1) * rows, :], weight)
            goal = slice((mask * CORES + core) * rows, (mask * CORES + core + 1) * rows)
            sets = (
                (q_ref, result[:, :COLS] + q_bias),
                (k_ref, result[:, COLS : 2 * COLS]),
                (v_ref, result[:, 2 * COLS :] + v_bias),
            )
            for goal_ref, values in sets:
                values = values.astype(bf16)
                for head in range(HEADS_HERE):
                    span = slice(head * HEAD_DIM, (head + 1) * HEAD_DIM)
                    if rest > 1:
                        goal_ref[head, goal, :] = values[:, span]
                        continue
                    for part in range(per):
                        place = block_place(rest, per, ids_ref, block_ref, 0, mask, core, part)
                        goal_ref[head, aligned(place * BLK, BLK), :] = values[
                            part * BLK : (part + 1) * BLK, span
                        ]


def attend_kernel(q_ref, k_ref, v_ref, pq_ref, pk_ref, *outs, tile):
    o_refs, lse_ref, all_ref = outs[:CHIPS], outs[CHIPS], outs[CHIPS + 1]
    tokens = q_ref.shape[1]
    own = tokens // CHIPS

    def one_head(head, carry):
        k_head = k_ref[head]
        v_turned = v_ref[head].T
        for t in range(tokens // tile):
            rows = slice(t * tile, (t + 1) * tile)
            scores = dot_right(k_head, q_ref[head, rows, :]) * (score_scale * log2_e)
            allowed = pq_ref[:, rows] >= pk_ref[...]
            scores = jnp.where(allowed, scores, masked_score)
            peak = jnp.max(scores, axis=0, keepdims=True)
            powers = jnp.exp2(scores - peak)
            total = jnp.sum(powers, axis=0, keepdims=True)
            mixed = dot(v_turned, powers.astype(bf16)) / total
            all_ref[head, rows, :] = mixed.T.astype(bf16)
            lse_ref[head, :, rows] = peak + jnp.log2(total)
        return carry

    lax.fori_loop(0, HEADS_HERE, one_head, 0)
    for head in range(HEADS_HERE):
        span = slice(head * HEAD_DIM, (head + 1) * HEAD_DIM)
        for mask in range(CHIPS):
            o_refs[mask][:, span] = all_ref[head, mask * own : (mask + 1) * own, :]


def sorted_blocks(ids_ref, block_ref, rows):
    per = rows // BLK
    for mask in range(CHIPS):
        for core in range(CORES):
            for part in range(per):
                place = block_place(1, per, ids_ref, block_ref, 0, mask, core, part)
                yield mask, core * rows + part * BLK, aligned(place * BLK, BLK)


def below_diagonal(tile):
    key = lax.broadcasted_iota(jnp.int32, (tile, tile), 0)
    query = lax.broadcasted_iota(jnp.int32, (tile, tile), 1)
    return key <= query


def causal_kernel(ids_ref, block_ref, q_ref, k_ref, v_ref, *outs, tile):
    o_refs, lse_ref, all_ref = outs[:CHIPS], outs[CHIPS], outs[CHIPS + 1]
    tokens = q_ref.shape[1]
    rows = tokens // GROUP
    allowed = below_diagonal(tile)

    def one_head(head, carry):
        v_turned = v_ref[head].T
        for t in range(tokens // tile):
            here = slice(t * tile, (t + 1) * tile)
            q_tile = q_ref[head, here, :]
            scores = dot_right(k_ref[head, here, :], q_tile) * (score_scale * log2_e)
            scores = jnp.where(allowed, scores, masked_score)
            peak = jnp.max(scores, axis=0, keepdims=True)
            if t:
                before = slice(0, t * tile)
                earlier = dot_right(k_ref[head, before, :], q_tile) * (score_scale * log2_e)
                peak = jnp.maximum(peak, jnp.max(earlier, axis=0, keepdims=True))
            powers = jnp.exp2(scores - peak)
            total = jnp.sum(powers, axis=0, keepdims=True)
            mixed = dot(v_turned[:, here], powers.astype(bf16))
            if t:
                powers = jnp.exp2(earlier - peak)
                total = total + jnp.sum(powers, axis=0, keepdims=True)
                mixed = mixed + dot(v_turned[:, before], powers.astype(bf16))
            all_ref[head, here, :] = (mixed / total).T.astype(bf16)
            lse_ref[head, :, here] = peak + jnp.log2(total)
        return carry

    lax.fori_loop(0, HEADS_HERE, one_head, 0)
    for head in range(HEADS_HERE):
        span = slice(head * HEAD_DIM, (head + 1) * HEAD_DIM)
        for mask, low, place in sorted_blocks(ids_ref, block_ref, rows):
            o_refs[mask][low : low + BLK, span] = all_ref[head, place, :]


def norm_parts(values):
    middle = jnp.mean(values, axis=-1, keepdims=True)
    centred = values - middle
    spread = jnp.mean(centred * centred, axis=-1, keepdims=True)
    inverse = lax.rsqrt(spread + norm_eps)
    return centred * inverse, inverse


def norm_back(values, gain, grad_out):
    normal, inverse = norm_parts(values)
    scaled = grad_out * gain
    grad_in = (
        scaled
        - jnp.mean(scaled, axis=-1, keepdims=True)
        - normal * jnp.mean(scaled * normal, axis=-1, keepdims=True)
    ) * inverse
    return grad_in, normal


def column_total(values):
    return jnp.sum(values, axis=0, keepdims=True)


def branch_kernel(student, ids_ref, *refs):
    j = ids_ref[IJ]
    h_refs, (w_ref, own_ref, oth_ref, vec_ref, valid_ref) = refs[:CHIPS], refs[CHIPS : CHIPS + 5]
    outs = refs[CHIPS + 5 :]
    first_ref, sent_ref = outs[:2]
    rows = own_ref.shape[0] // CHIPS
    if student:
        residual_ref, sums_ref = outs[2:]
        sums_ref[...] = jnp.zeros_like(sums_ref)
    for core, x_ref in enumerate((own_ref, oth_ref)):
        goal = slice(core * rows, (core + 1) * rows)
        parts = []
        for chip in range(CHIPS):
            parts.append(
                tree_sum(
                    dot(
                        h_refs[mask][goal, :],
                        w_ref[chip, aligned((j ^ mask) * COLS, COLS), :],
                    )
                    for mask in range(CHIPS)
                )
            )
        branch = jnp.concatenate(parts, axis=1) + vec_ref[2:3, :]
        residual = x_ref[0:rows, :].astype(f32) + branch
        normal, _ = norm_parts(residual)
        first = normal * vec_ref[4:5, :] + vec_ref[5:6, :]
        first_ref[goal, :] = first
        sent_ref[goal, :] = first.astype(bf16)
        if student:
            residual_ref[goal, :] = residual
            sums_ref[0:1, :] += column_total(valid_ref[goal, :] * branch * branch)


def whole(refs):
    if len(refs) == 1:
        return refs[0][...]
    return jnp.concatenate([ref[...] for ref in refs])


def feed_kernel(student, count, *refs):
    pieces, (in_ref, down_ref, b1_ref, part_ref, *outs) = refs[:count], refs[count:]
    inner = dot(whole(pieces), in_ref[...]) + b1_ref[0:1, :]
    act = (inner * normal_cdf(inner)).astype(bf16)
    if student:
        outs[0][...] = inner
        outs[1][...] = act
    part_ref[...] = dot(act, down_ref[...]).astype(part_ref.dtype)


def target_kernel(*refs):
    parts, (first_ref, vec_ref, target_ref) = refs[:CHIPS], refs[CHIPS:]
    feed = tree_sum(ref[...].astype(f32) for ref in parts) + vec_ref[3:4, :]
    normal, _ = norm_parts(first_ref[...] + feed)
    target_ref[...] = normal * vec_ref[6:7, :] + vec_ref[7:8, :]


def loss_kernel(ids_ref, lengths_ref, *refs):
    parts, rest = refs[:CHIPS], refs[CHIPS:]
    first_ref, vec_ref, target_ref, valid_ref, out_ref, grad_ref, sent_ref, sums_ref = rest
    count = lengths_ref[0]
    for number in range(1, lengths_ref.shape[0]):
        count = count + lengths_ref[number]
    share = 1.0 / (count.astype(f32) * D)
    feed = tree_sum(ref[...].astype(f32) for ref in parts) + vec_ref[3:4, :]
    second = first_ref[...] + feed
    normal, inverse = norm_parts(second)
    out = normal * vec_ref[6:7, :] + vec_ref[7:8, :]
    out_ref[...] = out.astype(bf16)
    valid = valid_ref[...]
    mismatch = valid * (out - target_ref[...])
    grad_out = mismatch * share
    scaled = grad_out * vec_ref[6:7, :]
    grad = (
        scaled
        - jnp.mean(scaled, axis=-1, keepdims=True)
        - normal * jnp.mean(scaled * normal, axis=-1, keepdims=True)
    ) * inverse
    grad_ref[...] = grad
    sent_ref[...] = grad.astype(bf16)
    sums_ref[...] = jnp.concatenate(
        [
            column_total(grad),
            column_total(grad_out * normal),
            column_total(grad_out),
            0.5 * column_total(mismatch * mismatch),
            column_total(valid * feed * feed),
            column_total(valid * second * second),
            jnp.zeros((2, D), f32),
        ]
    )


def feed_back_kernel(count, *refs):
    pieces, refs = refs[:count], refs[count:]
    inner_ref, in_ref, down_ref, part_ref, grad_ref, sum_ref = refs
    inner = inner_ref[...]
    slope = normal_cdf(inner) + inner * jnp.exp(-0.5 * inner * inner) * 0.3989422804014327
    grad = dot_right(whole(pieces), down_ref[...]) * slope
    sum_ref[...] = jnp.broadcast_to(column_total(grad), sum_ref.shape)
    grad = grad.astype(bf16)
    grad_ref[...] = grad
    part_ref[...] = dot_right(grad, in_ref[...]).astype(part_ref.dtype)


def branch_back_kernel(ids_ref, *refs):
    j = ids_ref[IJ]
    parts, rest = refs[:CHIPS], refs[CHIPS:]
    second_ref, residual_ref, vec_ref, w_ref = rest[:4]
    grad_ref, sent_ref = rest[4:6]
    h_refs, (sums_ref,) = rest[6 : 6 + CHIPS], rest[6 + CHIPS :]
    grad_first = second_ref[...] + tree_sum(ref[...].astype(f32) for ref in parts)
    grad, normal = norm_back(residual_ref[...], vec_ref[4:5, :], grad_first)
    grad_ref[...] = grad
    sums_ref[...] = jnp.concatenate(
        [
            column_total(grad),
            column_total(grad_first * normal),
            column_total(grad_first),
            jnp.zeros((5, D), f32),
        ]
    )
    grad = grad.astype(bf16)
    sent_ref[...] = grad
    chips = [grad[:, chip * COLS : (chip + 1) * COLS] for chip in range(CHIPS)]
    for mask in range(CHIPS):
        rows = aligned((j ^ mask) * COLS, COLS)
        h_refs[mask][...] = tree_sum(
            dot_right(chips[chip], w_ref[chip, rows, :]) for chip in range(CHIPS)
        ).astype(bf16)


def attend_back_kernel(*refs, tile):
    q_ref, k_ref, v_ref = refs[:3]
    g_refs, refs = refs[3 : 3 + CHIPS], refs[3 + CHIPS :]
    lse_ref, pq_ref, pk_ref, gq_ref, gk_ref, gv_ref, sums_ref = refs[:7]
    g_all, aq_ref, ak_ref, av_ref = refs[7:]
    tokens = q_ref.shape[1]
    own = tokens // CHIPS
    for head in range(HEADS_HERE):
        span = slice(head * HEAD_DIM, (head + 1) * HEAD_DIM)
        for mask in range(CHIPS):
            g_all[head, mask * own : (mask + 1) * own, :] = g_refs[mask][:, span]

    def one_head(head, carry):
        k_head = k_ref[head]
        v_head = v_ref[head]
        k_turned = k_head.T
        for t in range(tokens // tile):
            rows = slice(t * tile, (t + 1) * tile)
            q_tile = q_ref[head, rows, :]
            g_tile = g_all[head, rows, :]
            scores = dot_right(k_head, q_tile) * (score_scale * log2_e)
            allowed = pq_ref[:, rows] >= pk_ref[...]
            scores = jnp.where(allowed, scores, masked_score)
            probs = jnp.exp2(scores - lse_ref[head, :, rows])
            grad_probs = dot_right(v_head, g_tile)
            delta = jnp.sum(probs * grad_probs, axis=0, keepdims=True)
            grad_scores = (probs * (grad_probs - delta)).astype(bf16)
            aq_ref[head, rows, :] = dot(k_turned, grad_scores).T * score_scale
            if t == 0:
                ak_ref[head] = dot(grad_scores, q_tile)
                av_ref[head] = dot(probs.astype(bf16), g_tile)
            else:
                ak_ref[head] += dot(grad_scores, q_tile)
                av_ref[head] += dot(probs.astype(bf16), g_tile)
        return carry

    lax.fori_loop(0, HEADS_HERE, one_head, 0)
    sums_ref[...] = jnp.zeros_like(sums_ref)
    for head in range(HEADS_HERE):
        span = slice(head * HEAD_DIM, (head + 1) * HEAD_DIM)
        grad_query = aq_ref[head]
        grad_value = av_ref[head]
        gq_ref[:, span] = grad_query.astype(bf16)
        gk_ref[:, span] = (ak_ref[head] * score_scale).astype(gk_ref.dtype)
        gv_ref[:, span] = grad_value.astype(gv_ref.dtype)
        sums_ref[0:1, span] = column_total(grad_query)
        sums_ref[1:2, span] = column_total(grad_value)


def causal_back_kernel(ids_ref, block_ref, *refs, tile):
    q_ref, k_ref, v_ref = refs[:3]
    g_refs, refs = refs[3 : 3 + CHIPS], refs[3 + CHIPS :]
    lse_ref, gq_ref, gk_ref, gv_ref, sums_ref, g_all, aq_ref, ak_ref, av_ref = refs
    tokens = q_ref.shape[1]
    rows = tokens // GROUP
    own = tokens // CHIPS
    allowed = below_diagonal(tile)
    for head in range(HEADS_HERE):
        span = slice(head * HEAD_DIM, (head + 1) * HEAD_DIM)
        for mask, low, place in sorted_blocks(ids_ref, block_ref, rows):
            g_all[head, place, :] = g_refs[mask][low : low + BLK, span]

    def one_head(head, carry):
        k_turned = k_ref[head].T
        for t in range(tokens // tile):
            here = slice(t * tile, (t + 1) * tile)
            q_tile = q_ref[head, here, :]
            g_tile = g_all[head, here, :]
            lse = lse_ref[head, :, here]
            scores = dot_right(k_ref[head, here, :], q_tile) * (score_scale * log2_e)
            probs = jnp.exp2(jnp.where(allowed, scores, masked_score) - lse)
            grads = dot_right(v_ref[head, here, :], g_tile)
            delta = jnp.sum(probs * grads, axis=0, keepdims=True)
            if t:
                before = slice(0, t * tile)
                earlier = dot_right(k_ref[head, before, :], q_tile) * (score_scale * log2_e)
                early_probs = jnp.exp2(earlier - lse)
                early_grads = dot_right(v_ref[head, before, :], g_tile)
                delta = delta + jnp.sum(early_probs * early_grads, axis=0, keepdims=True)
            grad_scores = (probs * (grads - delta)).astype(bf16)
            grad_query = dot(k_turned[:, here], grad_scores)
            ak_ref[head, here, :] = dot(grad_scores, q_tile)
            av_ref[head, here, :] = dot(probs.astype(bf16), g_tile)
            if t:
                grad_scores = (early_probs * (early_grads - delta)).astype(bf16)
                grad_query = grad_query + dot(k_turned[:, before], grad_scores)
                ak_ref[head, before, :] += dot(grad_scores, q_tile)
                av_ref[head, before, :] += dot(early_probs.astype(bf16), g_tile)
            aq_ref[head, here, :] = grad_query.T * score_scale
        return carry

    lax.fori_loop(0, HEADS_HERE, one_head, 0)
    sums_ref[...] = jnp.zeros_like(sums_ref)
    for head in range(HEADS_HERE):
        span = slice(head * HEAD_DIM, (head + 1) * HEAD_DIM)
        sums_ref[0:1, span] = column_total(aq_ref[head])
        sums_ref[1:2, span] = column_total(av_ref[head])
        for mask, low, place in sorted_blocks(ids_ref, block_ref, rows):
            goal = slice(mask * own + low, mask * own + low + BLK)
            gq_ref[goal, span] = aq_ref[head, place, :].astype(bf16)
            gk_ref[goal, span] = (ak_ref[head, place, :] * score_scale).astype(bf16)
            gv_ref[goal, span] = av_ref[head, place, :].astype(bf16)


def qkv_back_kernel(gq_ref, gk_ref, gv_ref, w_ref, *part_refs):
    own = gq_ref.shape[0] // CHIPS
    for mask in range(CHIPS):
        rows = slice(mask * own, (mask + 1) * own)
        part_refs[mask][...] = (
            dot_right(gq_ref[rows, :], w_ref[:, :COLS])
            + dot_right(gk_ref[rows, :], w_ref[:, COLS : 2 * COLS])
            + dot_right(gv_ref[rows, :], w_ref[:, 2 * COLS :])
        ).astype(part_refs[mask].dtype)


def hidden_kernel(res_ref, *refs):
    parts, (own_ref, send_ref) = refs[:CHIPS], refs[CHIPS:]
    total = res_ref[...] + tree_sum(ref[...].astype(f32) for ref in parts)
    rows = own_ref.shape[0]
    own_ref[...] = total[:rows, :]
    send_ref[...] = total[rows:, :]


def late_grad_kernel(n_shard, counts, ids_ref, *refs):
    k = ids_ref[IK]
    groups = []
    for count in counts:
        groups.append(refs[:count])
        refs = refs[count:]
    acts, feeds, firsts, inners = (groups[i * CHIPS : (i + 1) * CHIPS] for i in range(4))
    own_ref, send_ref, down_ref, in_ref = refs
    down_ref[...] = tree_sum(dot_left(whole(a), whole(g)) for a, g in zip(acts, feeds))
    in_ref[...] = tree_sum(dot_left(whole(a), whole(g)) for a, g in zip(firsts, inners))
    few = FF // n_shard // GROUP
    rows_z = D // n_shard
    each = rows_z + 2 * few
    for goal_ref, half in ((own_ref, k), (send_ref, 1 - k)):
        kind = goal_ref.dtype
        lanes = aligned(half * HALF, HALF)
        for place in range(n_shard):
            goal_ref[place, 0:rows_z, :] = in_ref[
                place * rows_z : (place + 1) * rows_z, lanes
            ].astype(kind)
            rows = pl.ds(pl.multiple_of(half * HALF + place * few, few), few)
            goal_ref[place, rows_z : rows_z + few, :] = down_ref[rows, :HALF].astype(kind)
            goal_ref[place, rows_z + few : each, :] = down_ref[rows, HALF:].astype(kind)


def late_split_kernel(n_shard, ids_ref, own_ref, got_ref, *outs):
    for mask in range(n_shard):
        place = ids_ref[IZ] ^ mask
        outs[mask][...] = (own_ref[place] + got_ref[place].astype(f32)).astype(outs[mask].dtype)


def sum_kernel(*refs):
    refs[-1][...] = tree_sum(ref[...].astype(f32) for ref in refs[:-1]).astype(bf16)


def late_final_kernel(n_shard, ids_ref, *refs):
    k, j = ids_ref[IK], ids_ref[IJ]
    pieces, (in_latent_ref, down_latent_ref, in_ref, down_ref, all_ref) = refs[:GROUP], refs[GROUP:]
    few = FF // n_shard // GROUP
    rows_z = D // n_shard
    for core in range(CORES):
        for mask in range(CHIPS):
            all_ref[(j ^ mask) * CORES + (k ^ core)] = pieces[core * CHIPS + mask][...]
    for number in range(GROUP):
        for place in range(n_shard):
            goal = (place * GROUP + number) * few
            lanes = slice(goal, goal + few)
            grad = all_ref[number, 0:rows_z, place * few : (place + 1) * few].astype(f32)
            keep = jnp.abs(in_latent_ref[:, lanes]) <= 1.0
            in_ref[:, lanes] = jnp.where(keep, grad, 0.0)
        rows = slice(number * few, (number + 1) * few)
        for part in range(2):
            lanes = slice(part * HALF, (part + 1) * HALF)
            low = rows_z + part * few
            grad = all_ref[number, low : low + few, :].astype(f32)
            keep = jnp.abs(down_latent_ref[rows, lanes]) <= 1.0
            down_ref[rows, lanes] = jnp.where(keep, grad, 0.0)


def out_grad_kernel(n_shard, ids_ref, *refs):
    j = ids_ref[IJ]
    h_refs, grad_ref = refs[:CHIPS], refs[CHIPS]
    outs, (cols_ref, full_ref) = refs[CHIPS + 1 : CHIPS + 1 + CHIPS], refs[CHIPS + 1 + CHIPS :]
    half = D // n_shard // CORES
    for chip in range(CHIPS):
        cols_ref[chip] = grad_ref[:, chip * COLS : (chip + 1) * COLS]
    for goal in range(CHIPS):
        cols = cols_ref[j ^ goal]
        for mask in range(CHIPS):
            full_ref[aligned((j ^ mask) * COLS, COLS), :] = dot_left(h_refs[mask][...], cols)
        for core in range(CORES):
            for place in range(n_shard):
                low = (place * CORES + core) * half
                outs[goal][place * half : (place + 1) * half, core * COLS : (core + 1) * COLS] = (
                    full_ref[low : low + half, :].astype(outs[goal].dtype)
                )


def split_hi_lo(values):
    high = values.astype(bf16)
    low = (values - high.astype(f32)).astype(bf16)
    return high, low


def early_grad_kernel(n_shard, ids_ref, *refs):
    k = ids_ref[IK]
    own_x, oth_x, gq_ref, gk_ref, gv_ref = refs[:5]
    outs, refs = refs[5 : 5 + CHIPS], refs[5 + CHIPS :]
    branch_sums, loss_sums, res_sums = refs[:3]
    b1_sums, refs = refs[3 : 3 + CHIPS], refs[3 + CHIPS :]
    qv_sums, own_ref, vec_ref, send_ref, full_ref = refs
    half = D // n_shard // CORES
    rows = own_x.shape[0] // CHIPS
    for number, g_ref in enumerate((gq_ref, gk_ref, gv_ref)):
        parts = []
        for core, x_ref in enumerate((own_x, oth_x)):
            for mask in range(CHIPS):
                goal = slice((mask * CORES + core) * rows, (mask * CORES + core + 1) * rows)
                parts.append(dot_left(x_ref[mask * rows : (mask + 1) * rows, :], g_ref[goal, :]))
        full_ref[:, number * COLS : (number + 1) * COLS] = tree_sum(parts)
    total = tree_sum(ref[...].astype(f32) for ref in outs)
    for place in range(n_shard):
        for core in range(CORES):
            low = (place * CORES + core) * half
            full_ref[low : low + half, QKV:] = total[
                place * half : (place + 1) * half, core * COLS : (core + 1) * COLS
            ]
    for place in range(n_shard):
        goal = slice(place * half, (place + 1) * half)
        mine = pl.ds(pl.multiple_of((place * CORES + k) * half, half), half)
        theirs = pl.ds(pl.multiple_of((place * CORES + 1 - k) * half, half), half)
        own_ref[goal, :] = full_ref[mine, :]
        send_ref[goal, :] = full_ref[theirs, :].astype(bf16)
    lane = lax.broadcasted_iota(jnp.int32, (1, 2 * COLS), 1)
    stats = jnp.zeros((1, 2 * COLS), f32)
    for number, row in enumerate(
        (loss_sums[3:4, :], branch_sums[0:1, :], loss_sums[4:5, :], loss_sums[5:6, :])
    ):
        stats = stats + jnp.where(lane == number, jnp.sum(row, axis=1, keepdims=True), 0.0)
    table = jnp.concatenate(
        [
            res_sums[0:1, :],
            loss_sums[0:1, :],
            res_sums[1:3, :],
            loss_sums[1:3, :],
            tree_sum(ref[0:1, :] for ref in b1_sums),
            jnp.concatenate([qv_sums[0:1, :], qv_sums[1:2, :], stats], axis=1),
        ]
    )
    high, low = split_hi_lo(table)
    base = n_shard * half
    send_ref[base : base + VEC_ROWS, :] = high
    send_ref[base + VEC_ROWS : base + 2 * VEC_ROWS, :] = low
    vec_ref[...] = high.astype(f32) + low.astype(f32)


def early_split_kernel(n_shard, ids_ref, own_ref, vec_ref, got_ref, *outs):
    z = ids_ref[IZ]
    half = D // n_shard // CORES
    base = n_shard * half
    table = vec_ref[...] + (
        got_ref[base : base + VEC_ROWS, :].astype(f32)
        + got_ref[base + VEC_ROWS : base + 2 * VEC_ROWS, :].astype(f32)
    )
    high, low = split_hi_lo(table)
    for mask in range(n_shard):
        rows = aligned((z ^ mask) * half, half)
        kind = outs[mask].dtype
        outs[mask][0:half, :] = (own_ref[rows, :] + got_ref[rows, :].astype(f32)).astype(kind)
        outs[mask][half : half + VEC_ROWS, :] = high.astype(kind)
        outs[mask][half + VEC_ROWS : half + 2 * VEC_ROWS, :] = low.astype(kind)


def early_sum_kernel(*refs):
    ins, out_ref = refs[:-1], refs[-1]
    half = out_ref.shape[0] - 2 * VEC_ROWS
    out_ref[0:half, :] = tree_sum(ref[0:half, :].astype(f32) for ref in ins).astype(bf16)
    table = tree_sum(
        ref[half : half + VEC_ROWS, :].astype(f32)
        + ref[half + VEC_ROWS : half + 2 * VEC_ROWS, :].astype(f32)
        for ref in ins
    )
    high, low = split_hi_lo(table)
    out_ref[half : half + VEC_ROWS, :] = high
    out_ref[half + VEC_ROWS : half + 2 * VEC_ROWS, :] = low


def early_final_kernel(n_shard, ids_ref, lengths_ref, *refs):
    k, j = ids_ref[IK], ids_ref[IJ]
    pieces = refs[:GROUP]
    latent_ref, attn_ref, vec_ref, query_ref, stats_ref, all_ref, rows_ref, flat_ref = refs[GROUP:]
    half = D // n_shard // CORES
    few = FF // n_shard // GROUP
    units = FF // n_shard
    for core in range(CORES):
        for mask in range(CHIPS):
            ref = pieces[core * CHIPS + mask]
            all_ref[(j ^ mask) * CORES + (k ^ core)] = ref[0:half, :]
    for chip in range(CHIPS):
        for core in range(CORES):
            for number in range(4):
                lanes = slice(chip * COLS, (chip + 1) * COLS)
                rows = slice(core * half, (core + 1) * half)
                grad = all_ref[
                    chip * CORES + core, :, number * COLS : (number + 1) * COLS
                ].astype(f32)
                keep = jnp.abs(latent_ref[number, rows, lanes]) <= 1.0
                attn_ref[number, rows, lanes] = jnp.where(keep, grad, 0.0)
    tables = [
        pieces[mask][half : half + VEC_ROWS, :].astype(f32)
        + pieces[mask][half + VEC_ROWS : half + 2 * VEC_ROWS, :].astype(f32)
        for mask in range(CHIPS)
    ]
    total = tree_sum(tables)
    for mask in range(CHIPS):
        rows_ref[j ^ mask] = tables[mask]
    count = lengths_ref[0]
    for number in range(1, lengths_ref.shape[0]):
        count = count + lengths_ref[number]
    scale = count.astype(f32) * D
    stats = total[ROW_QV : ROW_QV + 1, 2 * COLS : 2 * COLS + 128] / scale
    lane = lax.broadcasted_iota(jnp.int32, (1, 128), 1)
    stats_ref[...] = jnp.where(lane == 0, stats, jnp.sqrt(stats))
    vec_ref[1:7, :] = total[0:6, :]
    for chip in range(CHIPS):
        lanes = slice(chip * COLS, (chip + 1) * COLS)
        query_ref[:, lanes] = rows_ref[chip, ROW_QV : ROW_QV + 1, 0:COLS]
        vec_ref[0:1, lanes] = rows_ref[chip, ROW_QV : ROW_QV + 1, COLS : 2 * COLS]
        for core in range(CORES):
            for place in range(n_shard):
                start = place * units + (chip * CORES + core) * few
                row, lane = 7 + start // D, start % D
                vec_ref[row : row + 1, lane : lane + few] = rows_ref[
                    chip, ROW_B1 : ROW_B1 + 1, core * HALF + place * few : core * HALF + (place + 1) * few
                ]


def owners_kernel(ids_ref, here_ref, there_ref, out_ref):
    k = ids_ref[IK]
    out_ref[k] = here_ref[...]
    out_ref[1 - k] = there_ref[...]


def body(
    hidden_in,
    block_of,
    lengths,
    attn_latent,
    ffn_in_latent,
    ffn_out_latent,
    student_vec,
    teacher_attn,
    teacher_ffn_in,
    teacher_ffn_out,
    teacher_vec,
):
    seqs, rows, _ = hidden_in.shape
    rest = lax.axis_size("rest")
    n_shard = lax.axis_size("shard")
    own = seqs * rows
    tokens = CHIPS * own
    keys = rest * tokens
    ids = jnp.stack([lax.axis_index(name) for name in ("shard", "core", "chip", "rest")])
    half = D // n_shard // CORES
    few = FF // n_shard // GROUP
    rows_z = D // n_shard
    each = rows_z + 2 * few
    line = Line(ids.astype(jnp.int32))

    def flip(piece, axis, mask):
        size = lax.axis_size(axis)
        return lax.ppermute(piece, axis, [(a, a ^ mask) for a in range(size)])

    def gather(piece, axis):
        return [piece] + [flip(piece, axis, m) for m in range(1, lax.axis_size(axis))]

    def exchange(pieces, axis):
        return [pieces[0]] + [flip(pieces[m], axis, m) for m in range(1, len(pieces))]

    def swap(piece):
        return flip(piece, "core", 1)

    def near_rows(piece):
        return [piece, flip(piece, "chip", 1), flip(piece, "chip", 2)]

    def all_rows(near):
        near = [near[0], *line.behind(*near[1:])]
        half = near[0].shape[0] // 2
        far = (flip(near[2][:half], "chip", 1), flip(near[1][half:], "chip", 2))
        return [(near[0],), (near[1],), (near[2],), far]

    def spread_z(piece):
        bits = n_shard.bit_length() - 1
        own = piece[None]
        for bit in range(bits):
            got = flip(own, "shard", 1 << bit)
            if bit == bits - 1:
                return own, got
            own = line(
                functools.partial(merge_kernel, bit),
                "merge",
                shape((2 * own.shape[0], *own.shape[1:])),
                (),
                (own, got),
                limit=6,
            )

    near = near_rows(hidden_in)
    t_early = early_pieces(line, False, teacher_attn)
    s_early = early_pieces(line, True, attn_latent)
    outs = [shape((own, 1), f32)]
    if rest > 1:
        outs += [shape((1, tokens), jnp.int32), shape((keys, 1), jnp.int32)]
    valid, *positions = line(
        functools.partial(places_kernel, rest, seqs=seqs, rows=rows),
        "places",
        tuple(outs),
        (block_of, lengths),
        (),
    )
    t_qkv_half, t_out_half = line(
        functools.partial(early_kernel, n_shard, 0),
        "early_weights",
        (shape((n_shard * half, QKV)), shape((n_shard * half // 2, 2 * COLS))),
        (),
        gather(t_early, "shard"),
    )
    pieces = [piece for group in all_rows(near) for piece in group]
    t_late = late_pieces(line, n_shard, False, teacher_ffn_in, teacher_ffn_out)
    s_late = late_pieces(line, n_shard, True, ffn_in_latent, ffn_out_latent)
    pieces = pieces[:3] + [piece[0] for piece in pieces[3:]]
    x_own, x_send = line(
        input_kernel,
        "input",
        (shape((tokens // CORES, D)), shape((tokens // CORES, D))),
        (),
        pieces,
    )
    x_oth = swap(x_send)
    def rest_gather(values):
        if rest == 1:
            return values
        return jnp.concatenate(gather(values, "rest"), axis=1)

    def rest_scatter(partial):
        if rest == 1:
            return partial
        view = partial.reshape(rest, tokens, COLS)
        return tree_sum(
            [view[0]]
            + [flip(view[m].astype(bf16), "rest", m).astype(f32) for m in range(1, rest)]
        ).astype(bf16)

    def project(qkv_half, vector):
        heads = shape((HEADS_HERE, tokens, HEAD_DIM))
        query, key, value, w_qkv = line(
            functools.partial(qkv_kernel, n_shard, rest),
            "qkv",
            (heads, heads, heads, shape((D, QKV))),
            (block_of,),
            [x_own, x_oth, qkv_half, swap(qkv_half), vector],
        )
        return query, rest_gather(key), rest_gather(value), w_qkv

    def attend(query, key, value):
        outs = tuple([shape((own, COLS))] * CHIPS + [shape((HEADS_HERE, 1, tokens), f32)])
        scratch = (pltpu.VMEM((HEADS_HERE, tokens, HEAD_DIM), bf16),)
        if rest == 1:
            *heads, lse = line(
                functools.partial(causal_kernel, tile=own),
                "attend",
                outs,
                (block_of,),
                (query, key, value),
                scratch,
            )
        else:
            *heads, lse = line(
                functools.partial(attend_kernel, tile=own),
                "attend",
                outs,
                (),
                (query, key, value, *positions),
                scratch,
                limit=48,
                bare=True,
            )
        return exchange(heads, "chip"), lse

    def branch(student, heads, w_out, vector):
        outs = [shape((own, D), f32), shape((own, D))]
        if student:
            outs += [shape((own, D), f32), shape((8, D), f32)]
        return line(
            functools.partial(branch_kernel, student),
            "branch",
            tuple(outs),
            (),
            (*heads, w_out, x_own, x_oth, vector, valid),
        )

    def late_weights(student, near_far, vector):
        return line(
            functools.partial(late_kernel, n_shard, student),
            "late_weights",
            (shape((D, UNITS)), shape((UNITS, D)), shape((8, UNITS), f32)),
            (),
            [*near_far, *[swap(piece) for piece in near_far], vector],
        )

    def feed(student, pieces, mask, late):
        outs = [shape((own, D), f32 if mask == 0 else bf16)]
        if student:
            outs += [shape((own, UNITS), f32), shape((own, UNITS))]
        return line(
            functools.partial(feed_kernel, student, len(pieces)),
            "feed",
            tuple(outs),
            (),
            (*pieces, *late),
            bare=True,
        )

    t_query, t_key, t_value, _ = project(t_qkv_half, teacher_vec)
    s_qkv_half, out_half = line(
        functools.partial(early_kernel, n_shard, 1),
        "early_weights",
        (shape((n_shard * half, QKV)), shape((n_shard * half, 2 * COLS))),
        (),
        gather(s_early, "shard") + [t_out_half],
    )
    t_late = spread_z(t_late)
    t_heads, _ = attend(t_query, t_key, t_value)
    (s_late,) = line.behind(s_late)
    out_all = list(line.behind(*gather(out_half, "chip")))
    query, key, value, w_qkv = project(s_qkv_half, student_vec)
    s_late = spread_z(s_late)
    t_out, s_out = line(
        functools.partial(out_weight_kernel, n_shard),
        "out_weights",
        (shape((CHIPS, D, COLS)), shape((CHIPS, D, COLS))),
        (),
        out_all + [swap(piece) for piece in out_all],
    )
    t_first, t_sent = branch(False, t_heads, t_out, teacher_vec)
    t_near = near_rows(t_sent)
    heads, lse = attend(query, key, value)
    t_late = late_weights(False, line.behind(*t_late), teacher_vec)
    t_parts = [feed(False, (t_sent,), 0, t_late)[0]]
    t_firsts = all_rows(t_near)
    first, sent, residual, branch_sums = branch(True, heads, s_out, student_vec)
    near = near_rows(sent)
    for m in (1, 2):
        t_parts.append(feed(False, t_firsts[m], m, t_late)[0])
    s_late = late_weights(True, line.behind(*s_late), student_vec)
    w_in, w_down, _ = s_late
    fed = [feed(True, (sent,), 0, s_late)]
    t_parts.append(feed(False, t_firsts[3], 3, t_late)[0])
    t_parts = exchange(t_parts, "chip")
    firsts = all_rows(near)
    fed += [feed(True, firsts[m], m, s_late) for m in range(1, CHIPS)]
    parts, inners, acts = ([f[i] for f in fed] for i in range(3))
    target = line(
        target_kernel,
        "target",
        shape((own, D), f32),
        (),
        (*t_parts, t_first, teacher_vec),
        bare=True,
    )
    out, grad_second, sent, loss_sums = line(
        loss_kernel,
        "loss",
        (shape((own, D)), shape((own, D), f32), shape((own, D)), shape((8, D), f32)),
        (lengths,),
        (*exchange(parts, "chip"), first, student_vec, target, valid),
    )

    near = near_rows(sent)

    def to_owners(here, there):
        return line(
            owners_kernel,
            "owners",
            shape((CORES, *here.shape), here.dtype),
            (),
            (here, swap(there)),
        )

    output = to_owners(out[:rows], out[rows:])
    def feed_back(pieces, m):
        return line(
            functools.partial(feed_back_kernel, len(pieces)),
            "feed_back",
            (
                shape((own, D), f32 if m == 0 else bf16),
                shape((own, UNITS)),
                shape((8, UNITS), f32),
            ),
            (),
            (*pieces, inners[m], w_in, w_down),
            bare=True,
        )

    backs = [feed_back((sent,), 0)]
    feeds = all_rows(near)
    backs += [feed_back(feeds[m], m) for m in range(1, CHIPS)]
    parts, grad_inners, b1_sums = ([b[i] for b in backs] for i in range(3))
    groups = [(act,) for act in acts] + feeds + firsts + [(inner,) for inner in grad_inners]
    keep, send = line(
        functools.partial(late_grad_kernel, n_shard, [len(group) for group in groups]),
        "late_grad",
        (shape((n_shard, each, HALF), f32), shape((n_shard, each, HALF))),
        (),
        [piece for group in groups for piece in group],
        (pltpu.VMEM((UNITS, D), f32), pltpu.VMEM((D, UNITS), f32)),
        limit=24,
    )
    grad_res, grad_branch, *rest_outs = line(
        branch_back_kernel,
        "branch_back",
        tuple(
            [shape((own, D), f32), shape((own, D))]
            + [shape((own, COLS))] * CHIPS
            + [shape((8, D), f32)]
        ),
        (),
        (*exchange(parts, "chip"), grad_second, residual, student_vec, s_out),
    )
    grad_heads, res_sums = exchange(rest_outs[:CHIPS], "chip"), rest_outs[CHIPS]
    late_pieces_out = line(
        functools.partial(late_split_kernel, n_shard),
        "late_split",
        tuple(shape((each, HALF), f32 if m == 0 else bf16) for m in range(n_shard)),
        (),
        (keep, swap(*line.behind(send))),
    )
    late_got = [late_pieces_out[0]]

    def late_exchange(*masks):
        for m in masks:
            if m < n_shard:
                late_got.append(flip(*line.behind(late_pieces_out[m]), "shard", m))

    late_exchange(1)
    line.wait(*grad_heads)
    out_parts = line(
        functools.partial(out_grad_kernel, n_shard),
        "out_grad",
        tuple(
            shape((n_shard * half, 2 * COLS), f32 if m == 0 else bf16) for m in range(CHIPS)
        ),
        (),
        (*heads, grad_branch),
        (pltpu.VMEM((CHIPS, own, COLS), bf16), pltpu.VMEM((D, COLS), f32)),
    )
    line.wait(late_got[-1])
    late_exchange(2)
    outs = (
        shape((tokens, COLS)),
        shape((keys, COLS), bf16 if rest == 1 else f32),
        shape((keys, COLS), bf16 if rest == 1 else f32),
        shape((8, COLS), f32),
    )
    scratch = (
        pltpu.VMEM((HEADS_HERE, tokens, HEAD_DIM), bf16),
        pltpu.VMEM((HEADS_HERE, tokens, HEAD_DIM), f32),
        pltpu.VMEM((HEADS_HERE, keys, HEAD_DIM), f32),
        pltpu.VMEM((HEADS_HERE, keys, HEAD_DIM), f32),
    )
    if rest == 1:
        grad_query, grad_key, grad_value, qv_sums = line(
            functools.partial(causal_back_kernel, tile=own),
            "attend_back",
            outs,
            (block_of,),
            (query, key, value, *grad_heads, lse),
            scratch,
            limit=28,
        )
    else:
        grad_query, grad_key, grad_value, qv_sums = line(
            functools.partial(attend_back_kernel, tile=own),
            "attend_back",
            outs,
            (),
            (query, key, value, *grad_heads, lse, *positions),
            scratch,
            limit=56,
            bare=True,
        )
    grad_key, grad_value = rest_scatter(grad_key), rest_scatter(grad_value)
    line.wait(late_got[-1])
    mine, table, send = line(
        functools.partial(early_grad_kernel, n_shard),
        "early_grad",
        (
            shape((n_shard * half, D), f32),
            shape((VEC_ROWS, D), f32),
            shape((n_shard * half + 2 * VEC_ROWS, D)),
        ),
        (),
        (
            x_own,
            x_oth,
            grad_query,
            grad_key,
            grad_value,
            *exchange(out_parts, "chip"),
            branch_sums,
            loss_sums,
            res_sums,
            *b1_sums,
            qv_sums,
        ),
        (pltpu.VMEM((D, D), f32),),
        limit=20,
    )
    parts = line(
        qkv_back_kernel,
        "qkv_back",
        tuple(shape((own, D), f32 if m == 0 else bf16) for m in range(CHIPS)),
        (),
        (grad_query, grad_key, grad_value, w_qkv),
        bare=True,
    )
    pieces = line(
        functools.partial(early_split_kernel, n_shard),
        "early_split",
        tuple(
            shape((half + 2 * VEC_ROWS, D), f32 if m == 0 else bf16) for m in range(n_shard)
        ),
        (),
        (mine, table, swap(send)),
    )
    parts = line.behind(*parts)
    early = line(
        early_sum_kernel,
        "early_sum",
        shape((half + 2 * VEC_ROWS, D)),
        (),
        exchange(pieces, "shard"),
        bare=True,
    )
    if rest > 1:
        early = line(
            early_sum_kernel, "rest_sum", shape(early.shape), (), gather(early, "rest"), bare=True
        )
    late_exchange(*range(3, n_shard))
    here, there = line(
        hidden_kernel,
        "hidden",
        (shape((rows, D), f32), shape((rows, D), f32)),
        (),
        (grad_res, *exchange(parts, "chip")),
        bare=True,
    )
    late = line(sum_kernel, "late_sum", shape((each, HALF)), (), late_got, bare=True)
    if rest > 1:
        late = line(sum_kernel, "rest_sum", shape(late.shape), (), gather(late, "rest"), bare=True)
    late = gather(late, "chip")
    grad_hidden = to_owners(here, there)
    in_grad, down_grad = line(
        functools.partial(late_final_kernel, n_shard),
        "late_final",
        (shape(ffn_in_latent.shape, f32), shape(ffn_out_latent.shape, f32)),
        (),
        (*late, *[swap(piece) for piece in late], ffn_in_latent, ffn_out_latent),
        (pltpu.VMEM((GROUP, each, HALF), bf16),),
    )
    early = gather(early, "chip")
    attn_grad, vec_grad, query_grad, stats = line(
        functools.partial(early_final_kernel, n_shard),
        "early_final",
        (
            shape(attn_latent.shape, f32),
            shape((7 + FF // D, D), f32),
            shape((1, D), f32),
            shape((1, 128), f32),
        ),
        (lengths,),
        (*early, *[swap(piece) for piece in early], attn_latent),
        (
            pltpu.VMEM((GROUP, half, D), bf16),
            pltpu.VMEM((CHIPS, VEC_ROWS, D), f32),
            pltpu.VMEM((8, D), f32),
        ),
    )
    return (
        output,
        stats[0, :4],
        grad_hidden,
        attn_grad,
        in_grad,
        down_grad,
        vec_grad,
        query_grad[0],
    )


def solution(mesh):
    n_ctx, n_shard = mesh.shape["ctx"], mesh.shape["shard"]
    places = mesh.devices.reshape(n_ctx // GROUP, CHIPS, CORES, n_shard)
    inner = Mesh(places, ("rest", "chip", "core", "shard"))
    ctx = ("rest", "chip", "core")
    in_specs = (
        P("shard", ctx, None),
        P(),
        P(),
        P(None, "shard", None),
        P("shard", None),
        P("shard", None),
        P(),
        P(None, "shard", None),
        P("shard", None),
        P("shard", None),
        P(),
    )
    out_specs = (
        P("shard", ctx, None),
        P(),
        P("shard", ctx, None),
        P(None, "shard", None),
        P("shard", None),
        P("shard", None),
        P(),
        P(),
    )
    return jax.shard_map(
        body, mesh=inner, in_specs=in_specs, out_specs=out_specs, check_vma=False
    )
```

```python
import functools

import jax
import jax.numpy as jnp
from jax import lax
from jax.experimental import pallas as pl
from jax.experimental.pallas import tpu as pltpu
from jax.sharding import Mesh
from jax.sharding import PartitionSpec as P

D = 768
HEADS = 12
HEAD_DIM = 64
FF = 3072
BLK = 64

CHIPS = 4
CORES = 2
GROUP = CHIPS * CORES
COLS = D // CHIPS
HEADS_HERE = HEADS // CHIPS
UNITS = FF // CHIPS
HALF = UNITS // CORES
QKV = 3 * COLS

norm_eps = 1e-05
attn_gains = (2.0, 2.0, 1.0, 4.0)
masked_score = -1e30
score_scale = HEAD_DIM ** (-0.5)
log2_e = 1.4426950408889634
bf16 = jnp.bfloat16
f32 = jnp.float32

IZ, IK, IJ, IR = 0, 1, 2, 3
ROW_BO, ROW_B2, ROW_G1, ROW_C1, ROW_G2, ROW_C2, ROW_B1, ROW_QV = range(8)
VEC_ROWS = 8
EXTRA = 16

SMEM_SPEC = pl.BlockSpec(memory_space=pltpu.SMEM)
HBM_SPEC = pl.BlockSpec(memory_space=pltpu.HBM)
VMEM_SPEC = pl.BlockSpec(memory_space=pltpu.VMEM)


def dot(left_side, right_side):
    return jnp.dot(left_side, right_side, preferred_element_type=f32)


def dot_left(left_side, right_side):
    return lax.dot_general(
        left_side, right_side, (((0,), (0,)), ((), ())), preferred_element_type=f32
    )


def dot_right(left_side, right_side):
    return lax.dot_general(
        left_side, right_side, (((1,), (1,)), ((), ())), preferred_element_type=f32
    )


def normal_cdf(values):
    return 0.5 * (1.0 + lax.erf(values * 0.7071067811865476))


def tree_sum(items):
    items = list(items)
    while len(items) > 1:
        items = [items[i] + items[i + 1] for i in range(0, len(items), 2)]
    return items[0]


def aligned(start, size):
    return pl.ds(pl.multiple_of(start, size), size)


def shape(dims, kind=bf16):
    return jax.ShapeDtypeStruct(dims, kind)


def call(kernel, name, outs, scalars, arrays, scratch=(), limit=16):
    return pl.pallas_call(
        kernel,
        out_shape=outs,
        in_specs=[SMEM_SPEC] * len(scalars) + [VMEM_SPEC] * len(arrays),
        out_specs=jax.tree.map(lambda _: VMEM_SPEC, outs),
        scratch_shapes=list(scratch),
        compiler_params=pltpu.CompilerParams(vmem_limit_bytes=limit * 2**20),
        name=name,
    )(*scalars, *arrays)


def without_ids(kernel, ids_ref, *refs):
    kernel(*refs)


class Line:
    def __init__(self, ids):
        self.ids = ids

    def wait(self, *values):
        self.ids = lax.optimization_barrier((self.ids, *values))[0]

    def behind(self, *values):
        return lax.optimization_barrier((self.ids, *values))[1:]

    def __call__(self, kernel, name, outs, scalars, arrays, scratch=(), limit=16, bare=False):
        if bare:
            kernel = functools.partial(without_ids, kernel)
        result = call(kernel, name, outs, (self.ids, *scalars), arrays, scratch, limit)
        self.wait(jax.tree.leaves(result)[0])
        return result


def pick(place, options):
    value = options[0]
    for number, option in enumerate(options[1:], 1):
        value = jnp.where(place == number, option, value)
    return value


def split_three(values):
    high = values.astype(bf16)
    rest = values - high.astype(f32)
    middle = rest.astype(bf16)
    return high, middle, (rest - middle.astype(f32)).astype(bf16)


def join_three(ref, row, *index):
    return tree_sum(
        [ref[(*index, slice(row + part, row + part + 1))].astype(f32) for part in range(3)]
        + [0.0]
    )


def sign_of(values):
    return jnp.where(values > 0, 1.0, jnp.where(values < 0, -1.0, 0.0))


def choose(size, count, start):
    place = lax.broadcasted_iota(jnp.int32, (size, count), 0)
    goal = lax.broadcasted_iota(jnp.int32, (size, count), 1) + start
    return jnp.where(place == goal, 1.0, 0.0).astype(bf16)


def early_pieces_kernel(student, ids_ref, attn_hbm, early_ref, attn_ref, sem):
    k, j = ids_ref[IK], ids_ref[IJ]
    rows_z = attn_hbm.shape[1]
    half = rows_z // CORES
    if student:
        copy = pltpu.make_async_copy(attn_hbm, attn_ref, sem)
    else:
        copy = pltpu.make_async_copy(attn_hbm.at[:, aligned(k * half, half), :], attn_ref, sem)
    copy.start()
    chosen = choose(D, COLS, j * COLS)
    if student:
        early_ref[half:, :] = jnp.zeros((EXTRA, D), bf16)
    copy.wait()
    for number in range(4):
        lanes = slice(number * COLS, (number + 1) * COLS)
        if student:
            full = sign_of(attn_ref[number, aligned(k * half, half), :]).astype(bf16)
            sums = column_total(jnp.abs(attn_ref[number]))
            sums = pick(j, [sums[:, chip * COLS : (chip + 1) * COLS] for chip in range(CHIPS)])
            for part, row in enumerate(split_three(sums)):
                early_ref[half + part : half + part + 1, lanes] = row
        else:
            full = attn_ref[number]
        early_ref[0:half, lanes] = dot(full, chosen).astype(bf16)


def early_pieces(line, student, attn):
    half = attn.shape[1] // CORES
    result = pl.pallas_call(
        functools.partial(early_pieces_kernel, student),
        out_shape=shape((half + EXTRA * student, D)),
        in_specs=[SMEM_SPEC, HBM_SPEC],
        out_specs=VMEM_SPEC,
        scratch_shapes=[
            pltpu.VMEM((4, attn.shape[1] if student else half, D), attn.dtype),
            pltpu.SemaphoreType.DMA,
        ],
        compiler_params=pltpu.CompilerParams(vmem_limit_bytes=12 * 2**20),
        name="early_pieces",
    )(line.ids, attn)
    line.wait(result)
    return result


def late_pieces_kernel(
    n_shard, student, ids_ref, in_hbm, down_hbm, late_ref, in_ref, down_ref, sems
):
    k, j = ids_ref[IK], ids_ref[IJ]
    units = FF // n_shard
    few = units // GROUP
    rows_z = in_ref.shape[0]
    each = rows_z + 2 * few
    number = j * CORES + k
    mine = aligned(number * few, few)
    down_hbm = down_hbm if student else down_hbm.at[mine, :]
    copies = [
        pltpu.make_async_copy(in_hbm, in_ref, sems.at[0]),
        pltpu.make_async_copy(down_hbm, down_ref, sems.at[1]),
    ]
    for copy in copies:
        copy.start()
    chosen = choose(units, few, number * few)
    copies[1].wait()
    if student:
        full = sign_of(down_ref[mine, :]).astype(bf16)
        late_ref[each:, :] = jnp.zeros((EXTRA, HALF), bf16)
        for part, row in enumerate(split_three(column_total(jnp.abs(down_ref[...])))):
            low = each + 3 + part
            late_ref[low : low + 1, :] = row[:, :HALF]
            late_ref[low + 3 : low + 4, :] = row[:, HALF:]
    else:
        full = down_ref[...]
    late_ref[rows_z : rows_z + few, :] = full[:, :HALF]
    late_ref[rows_z + few : each, :] = full[:, HALF:]
    copies[0].wait()
    for place in range(n_shard):
        lanes = slice(place * few, (place + 1) * few)
        full = in_ref[:, place * units : (place + 1) * units]
        if student:
            sums = column_total(jnp.abs(full))
            sums = pick(number, [sums[:, n * few : (n + 1) * few] for n in range(GROUP)])
            for part, row in enumerate(split_three(sums)):
                late_ref[each + part : each + part + 1, lanes] = row
            full = sign_of(full).astype(bf16)
        late_ref[0:rows_z, lanes] = dot(full, chosen).astype(bf16)


def late_pieces(line, n_shard, student, w_in, w_down):
    few = FF // n_shard // GROUP
    rows_z = w_in.shape[0]
    result = pl.pallas_call(
        functools.partial(late_pieces_kernel, n_shard, student),
        out_shape=shape((rows_z + 2 * few + EXTRA * student, HALF)),
        in_specs=[SMEM_SPEC, HBM_SPEC, HBM_SPEC],
        out_specs=VMEM_SPEC,
        scratch_shapes=[
            pltpu.VMEM((rows_z, FF), w_in.dtype),
            pltpu.VMEM((w_down.shape[0] if student else few, D), w_down.dtype),
            pltpu.SemaphoreType.DMA((2,)),
        ],
        compiler_params=pltpu.CompilerParams(vmem_limit_bytes=20 * 2**20),
        name="late_pieces",
    )(line.ids, w_in, w_down)
    line.wait(result)
    return result


def scale_row(sums, gain, fan_in):
    return gain * (sums / fan_in) * fan_in ** (-0.5)


def scaled(values, scale):
    return (values.astype(f32) * scale).astype(bf16)


def early_kernel(n_shard, model, ids_ref, *refs):
    group, refs = refs[:n_shard], refs[n_shard:]
    qkv_ref, out_ref = refs[-2:]
    z = ids_ref[IZ]
    half = D // n_shard // CORES
    fold = n_shard // 2
    base = model * fold * half
    if model:
        out_ref[0:base, :] = refs[0][...]
        sums = tree_sum(join_three(ref, half) for ref in group)
        scale = jnp.concatenate(
            [
                scale_row(sums[:, number * COLS : (number + 1) * COLS], attn_gains[number], D)
                for number in range(4)
            ],
            axis=1,
        )
    for mask, ref in enumerate(group):
        place = z ^ mask
        piece = ref[0:half, :]
        if model:
            piece = scaled(piece, scale)
        qkv_ref[aligned(place * half, half), :] = piece[:, :QKV]
        low = pl.ds(pl.multiple_of(base + lax.rem(place, fold) * half, half), half)

        @pl.when(place < fold)
        def _():
            out_ref[low, 0:COLS] = piece[:, QKV:]

        @pl.when(place >= fold)
        def _():
            out_ref[low, COLS:] = piece[:, QKV:]


def out_weight_kernel(n_shard, ids_ref, *refs):
    k, j = ids_ref[IK], ids_ref[IJ]
    t_ref, s_ref = refs[2 * CHIPS :]
    half = D // n_shard // CORES
    span = n_shard * half // 2
    for core in range(CORES):
        for mask in range(CHIPS):
            ref = refs[core * CHIPS + mask]
            for model, goal in enumerate((t_ref, s_ref)):
                for place in range(n_shard):
                    fold = n_shard // 2
                    low = model * span + (place % fold) * half
                    lanes = slice(0, COLS) if place < fold else slice(COLS, 2 * COLS)
                    rows = pl.ds(
                        pl.multiple_of((place * CORES + (k ^ core)) * half, half), half
                    )
                    goal[j ^ mask, rows, :] = ref[low : low + half, lanes]


def merge_kernel(bit, ids_ref, own_ref, got_ref, both_ref):
    size = own_ref.shape[0]
    mine = (ids_ref[IZ] >> bit) & 1
    both_ref[pl.ds(mine * size, size)] = own_ref[...]
    both_ref[pl.ds((1 - mine) * size, size)] = got_ref[...]


def late_kernel(n_shard, student, ids_ref, *refs):
    groups, vec_ref, refs = refs[:4], refs[4], refs[5:]
    in_ref, down_ref, b1_ref = refs
    z, k, j = ids_ref[IZ], ids_ref[IK], ids_ref[IJ]
    units = FF // n_shard
    few = units // GROUP
    rows_z = D // n_shard
    each = rows_z + 2 * few
    fold = n_shard // 2
    side = lax.div(z, fold)

    def mine(ref, row, core, place):
        options = []
        for chip in range(CHIPS):
            start = place * units + (chip * CORES + core) * few
            low, lane = row + start // D, start % D
            options.append(ref[low : low + 1, lane : lane + few])
        return pick(j, options)

    for core in range(CORES):
        for place in range(n_shard):
            goal = slice(core * HALF + place * few, core * HALF + (place + 1) * few)
            b1_ref[0:1, goal] = mine(vec_ref, 8, core, place)
    if student:
        sums = [
            tree_sum(
                join_three(groups[far], each + 3 * part, number)
                for far in range(2)
                for number in range(fold)
            )
            for part in (1, 2)
        ]
        left_scale, right_scale = (scale_row(row, 1.0, FF) for row in sums)
    for core in range(CORES):
        which = k ^ core
        lanes = aligned(which * HALF, HALF)
        if student:
            scale = tree_sum(
                join_three(groups[core * 2 + far], each, number)
                for far in range(2)
                for number in range(fold)
            )
            scale = scale_row(scale, 1.0, D)
        for far in range(2):
            ref = groups[core * 2 + far]
            for number in range(fold):
                place = (side ^ far) * fold + number
                piece = ref[number, 0:rows_z, :]
                left = ref[number, rows_z : rows_z + few, :]
                right = ref[number, rows_z + few : each, :]
                if student:
                    piece = scaled(piece, scale)
                    left = scaled(left, left_scale)
                    right = scaled(right, right_scale)
                in_ref[aligned(place * rows_z, rows_z), lanes] = piece
                rows = pl.ds(pl.multiple_of(which * HALF + place * few, few), few)
                down_ref[rows, 0:HALF] = left
                down_ref[rows, HALF:] = right


def block_place(rest, per, ids_ref, block_ref, far, mask, core, part):
    k, j, r = ids_ref[IK], ids_ref[IJ], ids_ref[IR]
    chip = (r ^ far) * CHIPS + (j ^ mask)
    return block_ref[(chip * CORES + (k ^ core)) * per + part]


def places_kernel(rest, ids_ref, block_ref, lengths_ref, valid_ref, *outs, seqs, rows):
    length = lengths_ref[ids_ref[IZ] * seqs + ids_ref[IK]]
    per = rows // BLK
    number = 0
    for far in range(rest):
        for mask in range(CHIPS):
            for core in range(CORES):
                for part in range(per):
                    goal = slice(number * BLK, (number + 1) * BLK)
                    number += 1
                    if not outs and mask:
                        continue
                    base = block_place(rest, per, ids_ref, block_ref, far, mask, core, part) * BLK
                    col = base + lax.broadcasted_iota(jnp.int32, (BLK, 1), 0)
                    if far == 0 and mask == 0:
                        valid_ref[goal, :] = jnp.where(col < length, 1.0, 0.0)
                    if outs:
                        outs[1][goal, :] = col
                        if far == 0:
                            row = lax.broadcasted_iota(jnp.int32, (1, BLK), 1)
                            outs[0][:, goal] = base + row


def input_kernel(ids_ref, here_ref, x_ref, y_ref, xy0_ref, xy1_ref, own_ref, send_ref):
    k = ids_ref[IK]
    rows = here_ref.shape[1]
    for mask, ref in enumerate((here_ref, x_ref, y_ref)):
        goal = slice(mask * rows, (mask + 1) * rows)
        own_ref[goal, :] = ref[k]
        send_ref[goal, :] = ref[1 - k]
    goal = slice(3 * rows, 4 * rows)

    @pl.when(k == 0)
    def _():
        own_ref[goal, :] = xy0_ref[...]
        send_ref[goal, :] = xy1_ref[...]

    @pl.when(k == 1)
    def _():
        own_ref[goal, :] = xy1_ref[...]
        send_ref[goal, :] = xy0_ref[...]


def qkv_kernel(n_shard, rest, ids_ref, block_ref, own_ref, oth_ref, half_ref, peer_ref, vec_ref, *outs):
    k, j = ids_ref[IK], ids_ref[IJ]
    q_ref, k_ref, v_ref, w_ref = outs
    half = D // n_shard // CORES
    for core, ref in enumerate((half_ref, peer_ref)):
        for place in range(n_shard):
            rows = pl.ds(pl.multiple_of((place * CORES + (k ^ core)) * half, half), half)
            w_ref[rows, :] = ref[place * half : (place + 1) * half, :]
    weight = w_ref[...]
    chips = [slice(chip * COLS, (chip + 1) * COLS) for chip in range(CHIPS)]
    q_bias = pick(j, [vec_ref[0:1, chip] for chip in chips])
    v_bias = pick(j, [vec_ref[1:2, chip] for chip in chips])
    rows = own_ref.shape[0] // CHIPS
    per = rows // BLK
    for core, ref in enumerate((own_ref, oth_ref)):
        full = dot(ref[...], weight)
        for mask in range(CHIPS):
            result = full[mask * rows : (mask + 1) * rows, :]
            goal = slice((mask * CORES + core) * rows, (mask * CORES + core + 1) * rows)
            sets = (
                (q_ref, result[:, :COLS] + q_bias),
                (k_ref, result[:, COLS : 2 * COLS]),
                (v_ref, result[:, 2 * COLS :] + v_bias),
            )
            for goal_ref, values in sets:
                values = values.astype(bf16)
                for head in range(HEADS_HERE):
                    span = slice(head * HEAD_DIM, (head + 1) * HEAD_DIM)
                    if rest > 1:
                        goal_ref[head, goal, :] = values[:, span]
                        continue
                    for part in range(per):
                        place = block_place(rest, per, ids_ref, block_ref, 0, mask, core, part)
                        goal_ref[head, aligned(place * BLK, BLK), :] = values[
                            part * BLK : (part + 1) * BLK, span
                        ]


def attend_kernel(q_ref, k_ref, v_ref, pq_ref, pk_ref, *outs, tile):
    o_refs, lse_ref, all_ref = outs[:CHIPS], outs[CHIPS], outs[CHIPS + 1]
    tokens = q_ref.shape[1]
    own = tokens // CHIPS

    def one_head(head, carry):
        k_head = k_ref[head]
        v_turned = v_ref[head].T
        for t in range(tokens // tile):
            rows = slice(t * tile, (t + 1) * tile)
            scores = dot_right(k_head, q_ref[head, rows, :]) * (score_scale * log2_e)
            allowed = pq_ref[:, rows] >= pk_ref[...]
            scores = jnp.where(allowed, scores, masked_score)
            peak = jnp.max(scores, axis=0, keepdims=True)
            powers = jnp.exp2(scores - peak)
            total = jnp.sum(powers, axis=0, keepdims=True)
            mixed = dot(v_turned, powers.astype(bf16)) / total
            all_ref[head, rows, :] = mixed.T.astype(bf16)
            lse_ref[head, :, rows] = peak + jnp.log2(total)
        return carry

    lax.fori_loop(0, HEADS_HERE, one_head, 0)
    for head in range(HEADS_HERE):
        span = slice(head * HEAD_DIM, (head + 1) * HEAD_DIM)
        for mask in range(CHIPS):
            o_refs[mask][:, span] = all_ref[head, mask * own : (mask + 1) * own, :]


def sorted_blocks(ids_ref, block_ref, rows):
    per = rows // BLK
    for mask in range(CHIPS):
        for core in range(CORES):
            for part in range(per):
                place = block_place(1, per, ids_ref, block_ref, 0, mask, core, part)
                yield mask, core * rows + part * BLK, aligned(place * BLK, BLK)


def below_diagonal(tile):
    key = lax.broadcasted_iota(jnp.int32, (tile, tile), 0)
    query = lax.broadcasted_iota(jnp.int32, (tile, tile), 1)
    return key <= query


def causal_kernel(ids_ref, block_ref, q_ref, k_ref, v_ref, *outs, tile):
    o_refs, lse_ref, all_ref = outs[:CHIPS], outs[CHIPS], outs[CHIPS + 1]
    tokens = q_ref.shape[1]
    rows = tokens // GROUP
    allowed = below_diagonal(tile)

    def one_head(head, carry):
        v_turned = v_ref[head].T
        for t in range(tokens // tile):
            here = slice(t * tile, (t + 1) * tile)
            q_tile = q_ref[head, here, :]
            scores = dot_right(k_ref[head, here, :], q_tile) * (score_scale * log2_e)
            scores = jnp.where(allowed, scores, masked_score)
            peak = jnp.max(scores, axis=0, keepdims=True)
            if t:
                before = slice(0, t * tile)
                earlier = dot_right(k_ref[head, before, :], q_tile) * (score_scale * log2_e)
                peak = jnp.maximum(peak, jnp.max(earlier, axis=0, keepdims=True))
            powers = jnp.exp2(scores - peak)
            total = jnp.sum(powers, axis=0, keepdims=True)
            mixed = dot(v_turned[:, here], powers.astype(bf16))
            if t:
                powers = jnp.exp2(earlier - peak)
                total = total + jnp.sum(powers, axis=0, keepdims=True)
                mixed = mixed + dot(v_turned[:, before], powers.astype(bf16))
            all_ref[head, here, :] = (mixed / total).T.astype(bf16)
            lse_ref[head, :, here] = peak + jnp.log2(total)
        return carry

    lax.fori_loop(0, HEADS_HERE, one_head, 0)
    for head in range(HEADS_HERE):
        span = slice(head * HEAD_DIM, (head + 1) * HEAD_DIM)
        for mask, low, place in sorted_blocks(ids_ref, block_ref, rows):
            o_refs[mask][low : low + BLK, span] = all_ref[head, place, :]


def norm_parts(values):
    middle = jnp.mean(values, axis=-1, keepdims=True)
    centred = values - middle
    spread = jnp.mean(centred * centred, axis=-1, keepdims=True)
    inverse = lax.rsqrt(spread + norm_eps)
    return centred * inverse, inverse


def norm_back(values, gain, grad_out):
    normal, inverse = norm_parts(values)
    scaled = grad_out * gain
    grad_in = (
        scaled
        - jnp.mean(scaled, axis=-1, keepdims=True)
        - normal * jnp.mean(scaled * normal, axis=-1, keepdims=True)
    ) * inverse
    return grad_in, normal


def column_total(values):
    return jnp.sum(values, axis=0, keepdims=True)


def branch_kernel(student, ids_ref, *refs):
    j = ids_ref[IJ]
    h_refs, (w_ref, own_ref, oth_ref, vec_ref, valid_ref) = refs[:CHIPS], refs[CHIPS : CHIPS + 5]
    outs = refs[CHIPS + 5 :]
    first_ref, sent_ref = outs[:2]
    rows = own_ref.shape[0] // CHIPS
    if student:
        residual_ref, sums_ref = outs[2:]
        sums_ref[...] = jnp.zeros_like(sums_ref)
    for core, x_ref in enumerate((own_ref, oth_ref)):
        goal = slice(core * rows, (core + 1) * rows)
        parts = []
        for chip in range(CHIPS):
            parts.append(
                tree_sum(
                    dot(
                        h_refs[mask][goal, :],
                        w_ref[chip, aligned((j ^ mask) * COLS, COLS), :],
                    )
                    for mask in range(CHIPS)
                )
            )
        branch = jnp.concatenate(parts, axis=1) + vec_ref[2:3, :]
        residual = x_ref[0:rows, :].astype(f32) + branch
        normal, _ = norm_parts(residual)
        first = normal * vec_ref[4:5, :] + vec_ref[5:6, :]
        first_ref[goal, :] = first
        sent_ref[goal, :] = first.astype(bf16)
        if student:
            residual_ref[goal, :] = residual
            sums_ref[0:1, :] += column_total(valid_ref[goal, :] * branch * branch)


def whole(refs):
    if len(refs) == 1:
        return refs[0][...]
    return jnp.concatenate([ref[...] for ref in refs])


def feed_kernel(student, count, *refs):
    pieces, (in_ref, down_ref, b1_ref, part_ref, *outs) = refs[:count], refs[count:]
    inner = dot(whole(pieces), in_ref[...]) + b1_ref[0:1, :]
    act = (inner * normal_cdf(inner)).astype(bf16)
    if student:
        outs[0][...] = inner
        outs[1][...] = act
    part_ref[...] = dot(act, down_ref[...]).astype(part_ref.dtype)


def target_kernel(*refs):
    parts, (first_ref, vec_ref, target_ref) = refs[:CHIPS], refs[CHIPS:]
    feed = tree_sum(ref[...].astype(f32) for ref in parts) + vec_ref[3:4, :]
    normal, _ = norm_parts(first_ref[...] + feed)
    target_ref[...] = normal * vec_ref[6:7, :] + vec_ref[7:8, :]


def loss_kernel(ids_ref, lengths_ref, *refs):
    parts, rest = refs[:CHIPS], refs[CHIPS:]
    first_ref, vec_ref, target_ref, valid_ref, out_ref, grad_ref, sent_ref, sums_ref = rest
    count = lengths_ref[0]
    for number in range(1, lengths_ref.shape[0]):
        count = count + lengths_ref[number]
    share = 1.0 / (count.astype(f32) * D)
    feed = tree_sum(ref[...].astype(f32) for ref in parts) + vec_ref[3:4, :]
    second = first_ref[...] + feed
    normal, inverse = norm_parts(second)
    out = normal * vec_ref[6:7, :] + vec_ref[7:8, :]
    out_ref[...] = out.astype(bf16)
    valid = valid_ref[...]
    mismatch = valid * (out - target_ref[...])
    grad_out = mismatch * share
    scaled = grad_out * vec_ref[6:7, :]
    grad = (
        scaled
        - jnp.mean(scaled, axis=-1, keepdims=True)
        - normal * jnp.mean(scaled * normal, axis=-1, keepdims=True)
    ) * inverse
    grad_ref[...] = grad
    sent_ref[...] = grad.astype(bf16)
    sums_ref[...] = jnp.concatenate(
        [
            column_total(grad),
            column_total(grad_out * normal),
            column_total(grad_out),
            0.5 * column_total(mismatch * mismatch),
            column_total(valid * feed * feed),
            column_total(valid * second * second),
            jnp.zeros((2, D), f32),
        ]
    )


def feed_back_kernel(count, *refs):
    pieces, refs = refs[:count], refs[count:]
    inner_ref, in_ref, down_ref, part_ref, grad_ref, sum_ref = refs
    inner = inner_ref[...]
    slope = normal_cdf(inner) + inner * jnp.exp(-0.5 * inner * inner) * 0.3989422804014327
    grad = dot_right(whole(pieces), down_ref[...]) * slope
    sum_ref[...] = jnp.broadcast_to(column_total(grad), sum_ref.shape)
    grad = grad.astype(bf16)
    grad_ref[...] = grad
    part_ref[...] = dot_right(grad, in_ref[...]).astype(part_ref.dtype)


def branch_back_kernel(ids_ref, *refs):
    j = ids_ref[IJ]
    parts, rest = refs[:CHIPS], refs[CHIPS:]
    second_ref, residual_ref, vec_ref, w_ref = rest[:4]
    grad_ref, sent_ref = rest[4:6]
    h_refs, (sums_ref,) = rest[6 : 6 + CHIPS], rest[6 + CHIPS :]
    grad_first = second_ref[...] + tree_sum(ref[...].astype(f32) for ref in parts)
    grad, normal = norm_back(residual_ref[...], vec_ref[4:5, :], grad_first)
    grad_ref[...] = grad
    sums_ref[...] = jnp.concatenate(
        [
            column_total(grad),
            column_total(grad_first * normal),
            column_total(grad_first),
            jnp.zeros((5, D), f32),
        ]
    )
    grad = grad.astype(bf16)
    sent_ref[...] = grad
    chips = [grad[:, chip * COLS : (chip + 1) * COLS] for chip in range(CHIPS)]
    for mask in range(CHIPS):
        rows = aligned((j ^ mask) * COLS, COLS)
        h_refs[mask][...] = tree_sum(
            dot_right(chips[chip], w_ref[chip, rows, :]) for chip in range(CHIPS)
        ).astype(bf16)


def attend_back_kernel(*refs, tile):
    q_ref, k_ref, v_ref = refs[:3]
    g_refs, refs = refs[3 : 3 + CHIPS], refs[3 + CHIPS :]
    lse_ref, pq_ref, pk_ref, gq_ref, gk_ref, gv_ref, sums_ref = refs[:7]
    g_all, aq_ref, ak_ref, av_ref = refs[7:]
    tokens = q_ref.shape[1]
    own = tokens // CHIPS
    for head in range(HEADS_HERE):
        span = slice(head * HEAD_DIM, (head + 1) * HEAD_DIM)
        for mask in range(CHIPS):
            g_all[head, mask * own : (mask + 1) * own, :] = g_refs[mask][:, span]

    def one_head(head, carry):
        k_head = k_ref[head]
        v_head = v_ref[head]
        k_turned = k_head.T
        for t in range(tokens // tile):
            rows = slice(t * tile, (t + 1) * tile)
            q_tile = q_ref[head, rows, :]
            g_tile = g_all[head, rows, :]
            scores = dot_right(k_head, q_tile) * (score_scale * log2_e)
            allowed = pq_ref[:, rows] >= pk_ref[...]
            scores = jnp.where(allowed, scores, masked_score)
            probs = jnp.exp2(scores - lse_ref[head, :, rows])
            grad_probs = dot_right(v_head, g_tile)
            delta = jnp.sum(probs * grad_probs, axis=0, keepdims=True)
            grad_scores = (probs * (grad_probs - delta)).astype(bf16)
            aq_ref[head, rows, :] = dot(k_turned, grad_scores).T * score_scale
            if t == 0:
                ak_ref[head] = dot(grad_scores, q_tile)
                av_ref[head] = dot(probs.astype(bf16), g_tile)
            else:
                ak_ref[head] += dot(grad_scores, q_tile)
                av_ref[head] += dot(probs.astype(bf16), g_tile)
        return carry

    lax.fori_loop(0, HEADS_HERE, one_head, 0)
    sums_ref[...] = jnp.zeros_like(sums_ref)
    for head in range(HEADS_HERE):
        span = slice(head * HEAD_DIM, (head + 1) * HEAD_DIM)
        grad_query = aq_ref[head]
        grad_value = av_ref[head]
        gq_ref[:, span] = grad_query.astype(bf16)
        gk_ref[:, span] = (ak_ref[head] * score_scale).astype(gk_ref.dtype)
        gv_ref[:, span] = grad_value.astype(gv_ref.dtype)
        sums_ref[0:1, span] = column_total(grad_query)
        sums_ref[1:2, span] = column_total(grad_value)


def causal_back_kernel(ids_ref, block_ref, *refs, tile):
    q_ref, k_ref, v_ref = refs[:3]
    g_refs, refs = refs[3 : 3 + CHIPS], refs[3 + CHIPS :]
    lse_ref, gq_ref, gk_ref, gv_ref, sums_ref, g_all, aq_ref, ak_ref, av_ref = refs
    tokens = q_ref.shape[1]
    rows = tokens // GROUP
    own = tokens // CHIPS
    allowed = below_diagonal(tile)
    for head in range(HEADS_HERE):
        span = slice(head * HEAD_DIM, (head + 1) * HEAD_DIM)
        for mask, low, place in sorted_blocks(ids_ref, block_ref, rows):
            g_all[head, place, :] = g_refs[mask][low : low + BLK, span]

    def one_head(head, carry):
        k_turned = k_ref[head].T
        for t in range(tokens // tile):
            here = slice(t * tile, (t + 1) * tile)
            q_tile = q_ref[head, here, :]
            g_tile = g_all[head, here, :]
            lse = lse_ref[head, :, here]
            scores = dot_right(k_ref[head, here, :], q_tile) * (score_scale * log2_e)
            probs = jnp.exp2(jnp.where(allowed, scores, masked_score) - lse)
            grads = dot_right(v_ref[head, here, :], g_tile)
            delta = jnp.sum(probs * grads, axis=0, keepdims=True)
            if t:
                before = slice(0, t * tile)
                earlier = dot_right(k_ref[head, before, :], q_tile) * (score_scale * log2_e)
                early_probs = jnp.exp2(earlier - lse)
                early_grads = dot_right(v_ref[head, before, :], g_tile)
                delta = delta + jnp.sum(early_probs * early_grads, axis=0, keepdims=True)
            grad_scores = (probs * (grads - delta)).astype(bf16)
            grad_query = dot(k_turned[:, here], grad_scores)
            ak_ref[head, here, :] = dot(grad_scores, q_tile)
            av_ref[head, here, :] = dot(probs.astype(bf16), g_tile)
            if t:
                grad_scores = (early_probs * (early_grads - delta)).astype(bf16)
                grad_query = grad_query + dot(k_turned[:, before], grad_scores)
                ak_ref[head, before, :] += dot(grad_scores, q_tile)
                av_ref[head, before, :] += dot(early_probs.astype(bf16), g_tile)
            aq_ref[head, here, :] = grad_query.T * score_scale
        return carry

    lax.fori_loop(0, HEADS_HERE, one_head, 0)
    sums_ref[...] = jnp.zeros_like(sums_ref)
    for head in range(HEADS_HERE):
        span = slice(head * HEAD_DIM, (head + 1) * HEAD_DIM)
        sums_ref[0:1, span] = column_total(aq_ref[head])
        sums_ref[1:2, span] = column_total(av_ref[head])
        for mask, low, place in sorted_blocks(ids_ref, block_ref, rows):
            goal = slice(mask * own + low, mask * own + low + BLK)
            gq_ref[goal, span] = aq_ref[head, place, :].astype(bf16)
            gk_ref[goal, span] = (ak_ref[head, place, :] * score_scale).astype(bf16)
            gv_ref[goal, span] = av_ref[head, place, :].astype(bf16)


def qkv_back_kernel(gq_ref, gk_ref, gv_ref, w_ref, *part_refs):
    own = gq_ref.shape[0] // CHIPS
    for mask in range(CHIPS):
        rows = slice(mask * own, (mask + 1) * own)
        part_refs[mask][...] = (
            dot_right(gq_ref[rows, :], w_ref[:, :COLS])
            + dot_right(gk_ref[rows, :], w_ref[:, COLS : 2 * COLS])
            + dot_right(gv_ref[rows, :], w_ref[:, 2 * COLS :])
        ).astype(part_refs[mask].dtype)


def hidden_kernel(res_ref, *refs):
    parts, (own_ref, send_ref) = refs[:CHIPS], refs[CHIPS:]
    total = res_ref[...] + tree_sum(ref[...].astype(f32) for ref in parts)
    rows = own_ref.shape[0]
    own_ref[...] = total[:rows, :]
    send_ref[...] = total[rows:, :]


def late_grad_kernel(n_shard, counts, ids_ref, *refs):
    k = ids_ref[IK]
    groups = []
    for count in counts:
        groups.append(refs[:count])
        refs = refs[count:]
    acts, feeds, firsts, inners = (groups[i * CHIPS : (i + 1) * CHIPS] for i in range(4))
    own_ref, send_ref, down_ref, in_ref = refs
    down_ref[...] = tree_sum(dot_left(whole(a), whole(g)) for a, g in zip(acts, feeds))
    in_ref[...] = tree_sum(dot_left(whole(a), whole(g)) for a, g in zip(firsts, inners))
    few = FF // n_shard // GROUP
    rows_z = D // n_shard
    each = rows_z + 2 * few
    for goal_ref, half in ((own_ref, k), (send_ref, 1 - k)):
        kind = goal_ref.dtype
        lanes = aligned(half * HALF, HALF)
        for place in range(n_shard):
            goal_ref[place, 0:rows_z, :] = in_ref[
                place * rows_z : (place + 1) * rows_z, lanes
            ].astype(kind)
            rows = pl.ds(pl.multiple_of(half * HALF + place * few, few), few)
            goal_ref[place, rows_z : rows_z + few, :] = down_ref[rows, :HALF].astype(kind)
            goal_ref[place, rows_z + few : each, :] = down_ref[rows, HALF:].astype(kind)


def late_split_kernel(n_shard, ids_ref, own_ref, got_ref, *outs):
    for mask in range(n_shard):
        place = ids_ref[IZ] ^ mask
        outs[mask][...] = (own_ref[place] + got_ref[place].astype(f32)).astype(outs[mask].dtype)


def sum_kernel(*refs):
    refs[-1][...] = tree_sum(ref[...].astype(f32) for ref in refs[:-1]).astype(bf16)


def late_final_kernel(n_shard, ids_ref, *refs):
    k, j = ids_ref[IK], ids_ref[IJ]
    pieces, (in_latent_ref, down_latent_ref, in_ref, down_ref, all_ref) = refs[:GROUP], refs[GROUP:]
    few = FF // n_shard // GROUP
    rows_z = D // n_shard
    for core in range(CORES):
        for mask in range(CHIPS):
            all_ref[(j ^ mask) * CORES + (k ^ core)] = pieces[core * CHIPS + mask][...]
    for number in range(GROUP):
        for place in range(n_shard):
            goal = (place * GROUP + number) * few
            lanes = slice(goal, goal + few)
            grad = all_ref[number, 0:rows_z, place * few : (place + 1) * few].astype(f32)
            keep = jnp.abs(in_latent_ref[:, lanes]) <= 1.0
            in_ref[:, lanes] = jnp.where(keep, grad, 0.0)
        rows = slice(number * few, (number + 1) * few)
        for part in range(2):
            lanes = slice(part * HALF, (part + 1) * HALF)
            low = rows_z + part * few
            grad = all_ref[number, low : low + few, :].astype(f32)
            keep = jnp.abs(down_latent_ref[rows, lanes]) <= 1.0
            down_ref[rows, lanes] = jnp.where(keep, grad, 0.0)


def out_grad_kernel(n_shard, ids_ref, *refs):
    j = ids_ref[IJ]
    h_refs, grad_ref = refs[:CHIPS], refs[CHIPS]
    outs, (cols_ref, full_ref) = refs[CHIPS + 1 : CHIPS + 1 + CHIPS], refs[CHIPS + 1 + CHIPS :]
    half = D // n_shard // CORES
    for chip in range(CHIPS):
        cols_ref[chip] = grad_ref[:, chip * COLS : (chip + 1) * COLS]
    for goal in range(CHIPS):
        cols = cols_ref[j ^ goal]
        for mask in range(CHIPS):
            full_ref[aligned((j ^ mask) * COLS, COLS), :] = dot_left(h_refs[mask][...], cols)
        for core in range(CORES):
            for place in range(n_shard):
                low = (place * CORES + core) * half
                outs[goal][place * half : (place + 1) * half, core * COLS : (core + 1) * COLS] = (
                    full_ref[low : low + half, :].astype(outs[goal].dtype)
                )


def split_hi_lo(values):
    high = values.astype(bf16)
    low = (values - high.astype(f32)).astype(bf16)
    return high, low


def early_grad_kernel(n_shard, ids_ref, *refs):
    k = ids_ref[IK]
    own_x, oth_x, gq_ref, gk_ref, gv_ref = refs[:5]
    outs, refs = refs[5 : 5 + CHIPS], refs[5 + CHIPS :]
    branch_sums, loss_sums, res_sums = refs[:3]
    b1_sums, refs = refs[3 : 3 + CHIPS], refs[3 + CHIPS :]
    qv_sums, own_ref, vec_ref, send_ref, full_ref = refs
    half = D // n_shard // CORES
    rows = own_x.shape[0] // CHIPS
    for number, g_ref in enumerate((gq_ref, gk_ref, gv_ref)):
        parts = []
        for core, x_ref in enumerate((own_x, oth_x)):
            for mask in range(CHIPS):
                goal = slice((mask * CORES + core) * rows, (mask * CORES + core + 1) * rows)
                parts.append(dot_left(x_ref[mask * rows : (mask + 1) * rows, :], g_ref[goal, :]))
        full_ref[:, number * COLS : (number + 1) * COLS] = tree_sum(parts)
    total = tree_sum(ref[...].astype(f32) for ref in outs)
    for place in range(n_shard):
        for core in range(CORES):
            low = (place * CORES + core) * half
            full_ref[low : low + half, QKV:] = total[
                place * half : (place + 1) * half, core * COLS : (core + 1) * COLS
            ]
    for place in range(n_shard):
        goal = slice(place * half, (place + 1) * half)
        mine = pl.ds(pl.multiple_of((place * CORES + k) * half, half), half)
        theirs = pl.ds(pl.multiple_of((place * CORES + 1 - k) * half, half), half)
        own_ref[goal, :] = full_ref[mine, :]
        send_ref[goal, :] = full_ref[theirs, :].astype(bf16)
    lane = lax.broadcasted_iota(jnp.int32, (1, 2 * COLS), 1)
    stats = jnp.zeros((1, 2 * COLS), f32)
    for number, row in enumerate(
        (loss_sums[3:4, :], branch_sums[0:1, :], loss_sums[4:5, :], loss_sums[5:6, :])
    ):
        stats = stats + jnp.where(lane == number, jnp.sum(row, axis=1, keepdims=True), 0.0)
    table = jnp.concatenate(
        [
            res_sums[0:1, :],
            loss_sums[0:1, :],
            res_sums[1:3, :],
            loss_sums[1:3, :],
            tree_sum(ref[0:1, :] for ref in b1_sums),
            jnp.concatenate([qv_sums[0:1, :], qv_sums[1:2, :], stats], axis=1),
        ]
    )
    high, low = split_hi_lo(table)
    base = n_shard * half
    send_ref[base : base + VEC_ROWS, :] = high
    send_ref[base + VEC_ROWS : base + 2 * VEC_ROWS, :] = low
    vec_ref[...] = high.astype(f32) + low.astype(f32)


def early_split_kernel(n_shard, ids_ref, own_ref, vec_ref, got_ref, *outs):
    z = ids_ref[IZ]
    half = D // n_shard // CORES
    base = n_shard * half
    table = vec_ref[...] + (
        got_ref[base : base + VEC_ROWS, :].astype(f32)
        + got_ref[base + VEC_ROWS : base + 2 * VEC_ROWS, :].astype(f32)
    )
    high, low = split_hi_lo(table)
    for mask in range(n_shard):
        rows = aligned((z ^ mask) * half, half)
        kind = outs[mask].dtype
        outs[mask][0:half, :] = (own_ref[rows, :] + got_ref[rows, :].astype(f32)).astype(kind)
        outs[mask][half : half + VEC_ROWS, :] = high.astype(kind)
        outs[mask][half + VEC_ROWS : half + 2 * VEC_ROWS, :] = low.astype(kind)


def early_sum_kernel(*refs):
    ins, out_ref = refs[:-1], refs[-1]
    half = out_ref.shape[0] - 2 * VEC_ROWS
    out_ref[0:half, :] = tree_sum(ref[0:half, :].astype(f32) for ref in ins).astype(bf16)
    table = tree_sum(
        ref[half : half + VEC_ROWS, :].astype(f32)
        + ref[half + VEC_ROWS : half + 2 * VEC_ROWS, :].astype(f32)
        for ref in ins
    )
    high, low = split_hi_lo(table)
    out_ref[half : half + VEC_ROWS, :] = high
    out_ref[half + VEC_ROWS : half + 2 * VEC_ROWS, :] = low


def early_final_kernel(n_shard, ids_ref, lengths_ref, *refs):
    k, j = ids_ref[IK], ids_ref[IJ]
    pieces = refs[:GROUP]
    latent_ref, attn_ref, vec_ref, query_ref, stats_ref, all_ref, rows_ref, flat_ref = refs[GROUP:]
    half = D // n_shard // CORES
    few = FF // n_shard // GROUP
    units = FF // n_shard
    for core in range(CORES):
        for mask in range(CHIPS):
            ref = pieces[core * CHIPS + mask]
            all_ref[(j ^ mask) * CORES + (k ^ core)] = ref[0:half, :]
    for chip in range(CHIPS):
        for core in range(CORES):
            for number in range(4):
                lanes = slice(chip * COLS, (chip + 1) * COLS)
                rows = slice(core * half, (core + 1) * half)
                grad = all_ref[
                    chip * CORES + core, :, number * COLS : (number + 1) * COLS
                ].astype(f32)
                keep = jnp.abs(latent_ref[number, rows, lanes]) <= 1.0
                attn_ref[number, rows, lanes] = jnp.where(keep, grad, 0.0)
    tables = [
        pieces[mask][half : half + VEC_ROWS, :].astype(f32)
        + pieces[mask][half + VEC_ROWS : half + 2 * VEC_ROWS, :].astype(f32)
        for mask in range(CHIPS)
    ]
    total = tree_sum(tables)
    for mask in range(CHIPS):
        rows_ref[j ^ mask] = tables[mask]
    count = lengths_ref[0]
    for number in range(1, lengths_ref.shape[0]):
        count = count + lengths_ref[number]
    scale = count.astype(f32) * D
    stats = total[ROW_QV : ROW_QV + 1, 2 * COLS : 2 * COLS + 128] / scale
    lane = lax.broadcasted_iota(jnp.int32, (1, 128), 1)
    stats_ref[...] = jnp.where(lane == 0, stats, jnp.sqrt(stats))
    vec_ref[1:7, :] = total[0:6, :]
    for chip in range(CHIPS):
        lanes = slice(chip * COLS, (chip + 1) * COLS)
        query_ref[:, lanes] = rows_ref[chip, ROW_QV : ROW_QV + 1, 0:COLS]
        vec_ref[0:1, lanes] = rows_ref[chip, ROW_QV : ROW_QV + 1, COLS : 2 * COLS]
        for core in range(CORES):
            for place in range(n_shard):
                start = place * units + (chip * CORES + core) * few
                row, lane = 7 + start // D, start % D
                vec_ref[row : row + 1, lane : lane + few] = rows_ref[
                    chip, ROW_B1 : ROW_B1 + 1, core * HALF + place * few : core * HALF + (place + 1) * few
                ]


def owners_kernel(ids_ref, here_ref, there_ref, out_ref):
    k = ids_ref[IK]
    out_ref[k] = here_ref[...]
    out_ref[1 - k] = there_ref[...]


def body(
    hidden_in,
    block_of,
    lengths,
    attn_latent,
    ffn_in_latent,
    ffn_out_latent,
    student_vec,
    teacher_attn,
    teacher_ffn_in,
    teacher_ffn_out,
    teacher_vec,
):
    seqs, rows, _ = hidden_in.shape
    rest = lax.axis_size("rest")
    n_shard = lax.axis_size("shard")
    own = seqs * rows
    tokens = CHIPS * own
    keys = rest * tokens
    ids = jnp.stack([lax.axis_index(name) for name in ("shard", "core", "chip", "rest")])
    half = D // n_shard // CORES
    few = FF // n_shard // GROUP
    rows_z = D // n_shard
    each = rows_z + 2 * few
    line = Line(ids.astype(jnp.int32))

    def flip(piece, axis, mask):
        size = lax.axis_size(axis)
        return lax.ppermute(piece, axis, [(a, a ^ mask) for a in range(size)])

    def gather(piece, axis):
        return [piece] + [flip(piece, axis, m) for m in range(1, lax.axis_size(axis))]

    def exchange(pieces, axis):
        return [pieces[0]] + [flip(pieces[m], axis, m) for m in range(1, len(pieces))]

    def swap(piece):
        return flip(piece, "core", 1)

    def near_rows(piece):
        return [piece, flip(piece, "chip", 1), flip(piece, "chip", 2)]

    def all_rows(near):
        near = [near[0], *line.behind(*near[1:])]
        half = near[0].shape[0] // 2
        far = (flip(near[2][:half], "chip", 1), flip(near[1][half:], "chip", 2))
        return [(near[0],), (near[1],), (near[2],), far]

    def spread_z(piece):
        bits = n_shard.bit_length() - 1
        own = piece[None]
        for bit in range(bits):
            got = flip(own, "shard", 1 << bit)
            if bit == bits - 1:
                return own, got
            own = line(
                functools.partial(merge_kernel, bit),
                "merge",
                shape((2 * own.shape[0], *own.shape[1:])),
                (),
                (own, got),
                limit=6,
            )

    near = near_rows(hidden_in)
    t_early = early_pieces(line, False, teacher_attn)
    s_early = early_pieces(line, True, attn_latent)
    outs = [shape((own, 1), f32)]
    if rest > 1:
        outs += [shape((1, tokens), jnp.int32), shape((keys, 1), jnp.int32)]
    valid, *positions = line(
        functools.partial(places_kernel, rest, seqs=seqs, rows=rows),
        "places",
        tuple(outs),
        (block_of, lengths),
        (),
    )
    t_qkv_half, t_out_half = line(
        functools.partial(early_kernel, n_shard, 0),
        "early_weights",
        (shape((n_shard * half, QKV)), shape((n_shard * half // 2, 2 * COLS))),
        (),
        gather(t_early, "shard"),
    )
    pieces = [piece for group in all_rows(near) for piece in group]
    t_late = late_pieces(line, n_shard, False, teacher_ffn_in, teacher_ffn_out)
    s_late = late_pieces(line, n_shard, True, ffn_in_latent, ffn_out_latent)
    pieces = pieces[:3] + [piece[0] for piece in pieces[3:]]
    x_own, x_send = line(
        input_kernel,
        "input",
        (shape((tokens // CORES, D)), shape((tokens // CORES, D))),
        (),
        pieces,
    )
    x_oth = swap(x_send)
    def rest_gather(values):
        if rest == 1:
            return values
        return jnp.concatenate(gather(values, "rest"), axis=1)

    def rest_scatter(partial):
        if rest == 1:
            return partial
        view = partial.reshape(rest, tokens, COLS)
        return tree_sum(
            [view[0]]
            + [flip(view[m].astype(bf16), "rest", m).astype(f32) for m in range(1, rest)]
        ).astype(bf16)

    def project(qkv_half, vector):
        heads = shape((HEADS_HERE, tokens, HEAD_DIM))
        query, key, value, w_qkv = line(
            functools.partial(qkv_kernel, n_shard, rest),
            "qkv",
            (heads, heads, heads, shape((D, QKV))),
            (block_of,),
            [x_own, x_oth, qkv_half, swap(qkv_half), vector],
        )
        return query, rest_gather(key), rest_gather(value), w_qkv

    def attend(query, key, value):
        outs = tuple([shape((own, COLS))] * CHIPS + [shape((HEADS_HERE, 1, tokens), f32)])
        scratch = (pltpu.VMEM((HEADS_HERE, tokens, HEAD_DIM), bf16),)
        if rest == 1:
            *heads, lse = line(
                functools.partial(causal_kernel, tile=own),
                "attend",
                outs,
                (block_of,),
                (query, key, value),
                scratch,
            )
        else:
            *heads, lse = line(
                functools.partial(attend_kernel, tile=own),
                "attend",
                outs,
                (),
                (query, key, value, *positions),
                scratch,
                limit=48,
                bare=True,
            )
        return exchange(heads, "chip"), lse

    def branch(student, heads, w_out, vector):
        outs = [shape((own, D), f32), shape((own, D))]
        if student:
            outs += [shape((own, D), f32), shape((8, D), f32)]
        return line(
            functools.partial(branch_kernel, student),
            "branch",
            tuple(outs),
            (),
            (*heads, w_out, x_own, x_oth, vector, valid),
        )

    def late_weights(student, near_far, vector):
        return line(
            functools.partial(late_kernel, n_shard, student),
            "late_weights",
            (shape((D, UNITS)), shape((UNITS, D)), shape((8, UNITS), f32)),
            (),
            [*near_far, *[swap(piece) for piece in near_far], vector],
        )

    def feed(student, pieces, mask, late):
        outs = [shape((own, D), f32 if mask == 0 else bf16)]
        if student:
            outs += [shape((own, UNITS), f32), shape((own, UNITS))]
        return line(
            functools.partial(feed_kernel, student, len(pieces)),
            "feed",
            tuple(outs),
            (),
            (*pieces, *late),
            bare=True,
        )

    t_query, t_key, t_value, _ = project(t_qkv_half, teacher_vec)
    s_qkv_half, out_half = line(
        functools.partial(early_kernel, n_shard, 1),
        "early_weights",
        (shape((n_shard * half, QKV)), shape((n_shard * half, 2 * COLS))),
        (),
        gather(s_early, "shard") + [t_out_half],
    )
    t_late = spread_z(t_late)
    t_heads, _ = attend(t_query, t_key, t_value)
    (s_late,) = line.behind(s_late)
    out_all = gather(out_half, "chip")
    query, key, value, w_qkv = project(s_qkv_half, student_vec)
    s_late = spread_z(s_late)
    t_out, s_out = line(
        functools.partial(out_weight_kernel, n_shard),
        "out_weights",
        (shape((CHIPS, D, COLS)), shape((CHIPS, D, COLS))),
        (),
        out_all + [swap(piece) for piece in out_all],
    )
    t_first, t_sent = branch(False, t_heads, t_out, teacher_vec)
    t_near = near_rows(t_sent)
    t_late = line.behind(*t_late)
    heads, lse = attend(query, key, value)
    t_late = late_weights(False, t_late, teacher_vec)
    t_parts = [feed(False, (t_sent,), 0, t_late)[0]]
    t_firsts = all_rows(t_near)
    first, sent, residual, branch_sums = branch(True, heads, s_out, student_vec)
    near = near_rows(sent)
    for m in (1, 2):
        t_parts.append(feed(False, t_firsts[m], m, t_late)[0])
    s_late = late_weights(True, line.behind(*s_late), student_vec)
    w_in, w_down, _ = s_late
    fed = [feed(True, (sent,), 0, s_late)]
    firsts = all_rows(near)
    t_parts.append(feed(False, t_firsts[3], 3, t_late)[0])
    t_parts = exchange(t_parts, "chip")
    fed += [feed(True, firsts[m], m, s_late) for m in range(1, CHIPS)]
    parts, inners, acts = ([f[i] for f in fed] for i in range(3))
    target = line(
        target_kernel,
        "target",
        shape((own, D), f32),
        (),
        (*t_parts, t_first, teacher_vec),
        bare=True,
    )
    out, grad_second, sent, loss_sums = line(
        loss_kernel,
        "loss",
        (shape((own, D)), shape((own, D), f32), shape((own, D)), shape((8, D), f32)),
        (lengths,),
        (*exchange(parts, "chip"), first, student_vec, target, valid),
    )

    near = near_rows(sent)

    def to_owners(here, there):
        return line(
            owners_kernel,
            "owners",
            shape((CORES, *here.shape), here.dtype),
            (),
            (here, swap(there)),
        )

    def feed_back(pieces, m):
        return line(
            functools.partial(feed_back_kernel, len(pieces)),
            "feed_back",
            (
                shape((own, D), f32 if m == 0 else bf16),
                shape((own, UNITS)),
                shape((8, UNITS), f32),
            ),
            (),
            (*pieces, inners[m], w_in, w_down),
            bare=True,
        )

    backs = [feed_back((sent,), 0)]
    feeds = all_rows(near)
    backs += [feed_back(feeds[m], m) for m in range(1, CHIPS)]
    output = to_owners(out[:rows], out[rows:])
    parts, grad_inners, b1_sums = ([b[i] for b in backs] for i in range(3))
    groups = [(act,) for act in acts] + feeds + firsts + [(inner,) for inner in grad_inners]
    keep, send = line(
        functools.partial(late_grad_kernel, n_shard, [len(group) for group in groups]),
        "late_grad",
        (shape((n_shard, each, HALF), f32), shape((n_shard, each, HALF))),
        (),
        [piece for group in groups for piece in group],
        (pltpu.VMEM((UNITS, D), f32), pltpu.VMEM((D, UNITS), f32)),
        limit=24,
    )
    grad_res, grad_branch, *rest_outs = line(
        branch_back_kernel,
        "branch_back",
        tuple(
            [shape((own, D), f32), shape((own, D))]
            + [shape((own, COLS))] * CHIPS
            + [shape((8, D), f32)]
        ),
        (),
        (*exchange(parts, "chip"), grad_second, residual, student_vec, s_out),
    )
    grad_heads, res_sums = exchange(rest_outs[:CHIPS], "chip"), rest_outs[CHIPS]
    late_pieces_out = line(
        functools.partial(late_split_kernel, n_shard),
        "late_split",
        tuple(shape((each, HALF), f32 if m == 0 else bf16) for m in range(n_shard)),
        (),
        (keep, swap(*line.behind(send))),
    )
    late_got = [late_pieces_out[0]]

    def late_exchange(*masks):
        for m in masks:
            if m < n_shard:
                late_got.append(flip(*line.behind(late_pieces_out[m]), "shard", m))

    late_exchange(1)
    out_parts = line(
        functools.partial(out_grad_kernel, n_shard),
        "out_grad",
        tuple(
            shape((n_shard * half, 2 * COLS), f32 if m == 0 else bf16) for m in range(CHIPS)
        ),
        (),
        (*heads, grad_branch),
        (pltpu.VMEM((CHIPS, own, COLS), bf16), pltpu.VMEM((D, COLS), f32)),
    )
    line.wait(*grad_heads)
    out_parts = list(line.behind(*out_parts))
    late_exchange(2)
    outs = (
        shape((tokens, COLS)),
        shape((keys, COLS), bf16 if rest == 1 else f32),
        shape((keys, COLS), bf16 if rest == 1 else f32),
        shape((8, COLS), f32),
    )
    scratch = (
        pltpu.VMEM((HEADS_HERE, tokens, HEAD_DIM), bf16),
        pltpu.VMEM((HEADS_HERE, tokens, HEAD_DIM), f32),
        pltpu.VMEM((HEADS_HERE, keys, HEAD_DIM), f32),
        pltpu.VMEM((HEADS_HERE, keys, HEAD_DIM), f32),
    )
    if rest == 1:
        grad_query, grad_key, grad_value, qv_sums = line(
            functools.partial(causal_back_kernel, tile=own),
            "attend_back",
            outs,
            (block_of,),
            (query, key, value, *grad_heads, lse),
            scratch,
            limit=28,
        )
    else:
        grad_query, grad_key, grad_value, qv_sums = line(
            functools.partial(attend_back_kernel, tile=own),
            "attend_back",
            outs,
            (),
            (query, key, value, *grad_heads, lse, *positions),
            scratch,
            limit=56,
            bare=True,
        )
    grad_key, grad_value = rest_scatter(grad_key), rest_scatter(grad_value)
    line.wait(late_got[-1])
    mine, table, send = line(
        functools.partial(early_grad_kernel, n_shard),
        "early_grad",
        (
            shape((n_shard * half, D), f32),
            shape((VEC_ROWS, D), f32),
            shape((n_shard * half + 2 * VEC_ROWS, D)),
        ),
        (),
        (
            x_own,
            x_oth,
            grad_query,
            grad_key,
            grad_value,
            *exchange(out_parts, "chip"),
            branch_sums,
            loss_sums,
            res_sums,
            *b1_sums,
            qv_sums,
        ),
        (pltpu.VMEM((D, D), f32),),
        limit=20,
    )
    parts = line(
        qkv_back_kernel,
        "qkv_back",
        tuple(shape((own, D), f32 if m == 0 else bf16) for m in range(CHIPS)),
        (),
        (grad_query, grad_key, grad_value, w_qkv),
        bare=True,
    )
    pieces = line(
        functools.partial(early_split_kernel, n_shard),
        "early_split",
        tuple(
            shape((half + 2 * VEC_ROWS, D), f32 if m == 0 else bf16) for m in range(n_shard)
        ),
        (),
        (mine, table, swap(send)),
    )
    parts = line.behind(*parts)
    early = line(
        early_sum_kernel,
        "early_sum",
        shape((half + 2 * VEC_ROWS, D)),
        (),
        exchange(pieces, "shard"),
        bare=True,
    )
    if rest > 1:
        early = line(
            early_sum_kernel, "rest_sum", shape(early.shape), (), gather(early, "rest"), bare=True
        )
    late_exchange(*range(3, n_shard))
    here, there = line(
        hidden_kernel,
        "hidden",
        (shape((rows, D), f32), shape((rows, D), f32)),
        (),
        (grad_res, *exchange(parts, "chip")),
        bare=True,
    )
    late = line(sum_kernel, "late_sum", shape((each, HALF)), (), late_got, bare=True)
    if rest > 1:
        late = line(sum_kernel, "rest_sum", shape(late.shape), (), gather(late, "rest"), bare=True)
    late = gather(late, "chip")
    grad_hidden = to_owners(here, there)
    early = gather(early, "chip")
    attn_grad, vec_grad, query_grad, stats = line(
        functools.partial(early_final_kernel, n_shard),
        "early_final",
        (
            shape(attn_latent.shape, f32),
            shape((7 + FF // D, D), f32),
            shape((1, D), f32),
            shape((1, 128), f32),
        ),
        (lengths,),
        (*early, *[swap(piece) for piece in early], attn_latent),
        (
            pltpu.VMEM((GROUP, half, D), bf16),
            pltpu.VMEM((CHIPS, VEC_ROWS, D), f32),
            pltpu.VMEM((8, D), f32),
        ),
    )
    in_grad, down_grad = line(
        functools.partial(late_final_kernel, n_shard),
        "late_final",
        (shape(ffn_in_latent.shape, f32), shape(ffn_out_latent.shape, f32)),
        (),
        (*late, *[swap(piece) for piece in late], ffn_in_latent, ffn_out_latent),
        (pltpu.VMEM((GROUP, each, HALF), bf16),),
    )
    return (
        output,
        stats[0, :4],
        grad_hidden,
        attn_grad,
        in_grad,
        down_grad,
        vec_grad,
        query_grad[0],
    )


def solution(mesh):
    n_ctx, n_shard = mesh.shape["ctx"], mesh.shape["shard"]
    places = mesh.devices.reshape(n_ctx // GROUP, CHIPS, CORES, n_shard)
    inner = Mesh(places, ("rest", "chip", "core", "shard"))
    ctx = ("rest", "chip", "core")
    in_specs = (
        P("shard", ctx, None),
        P(),
        P(),
        P(None, "shard", None),
        P("shard", None),
        P("shard", None),
        P(),
        P(None, "shard", None),
        P("shard", None),
        P("shard", None),
        P(),
    )
    out_specs = (
        P("shard", ctx, None),
        P(),
        P("shard", ctx, None),
        P(None, "shard", None),
        P("shard", None),
        P("shard", None),
        P(),
        P(),
    )
    return jax.shard_map(
        body, mesh=inner, in_specs=in_specs, out_specs=out_specs, check_vma=False
    )
```

```python
import functools

import jax
import jax.numpy as jnp
from jax import lax
from jax.experimental import pallas as pl
from jax.experimental.pallas import tpu as pltpu
from jax.sharding import Mesh
from jax.sharding import PartitionSpec as P

D = 768
HEADS = 12
HEAD_DIM = 64
FF = 3072
BLK = 64

CHIPS = 4
CORES = 2
GROUP = CHIPS * CORES
COLS = D // CHIPS
HEADS_HERE = HEADS // CHIPS
UNITS = FF // CHIPS
HALF = UNITS // CORES
QKV = 3 * COLS

norm_eps = 1e-05
attn_gains = (2.0, 2.0, 1.0, 4.0)
masked_score = -1e30
score_scale = HEAD_DIM ** (-0.5)
log2_e = 1.4426950408889634
bf16 = jnp.bfloat16
f32 = jnp.float32

IZ, IK, IJ, IR = 0, 1, 2, 3
ROW_BO, ROW_B2, ROW_G1, ROW_C1, ROW_G2, ROW_C2, ROW_B1, ROW_QV = range(8)
VEC_ROWS = 8
EXTRA = 16

SMEM_SPEC = pl.BlockSpec(memory_space=pltpu.SMEM)
HBM_SPEC = pl.BlockSpec(memory_space=pltpu.HBM)
VMEM_SPEC = pl.BlockSpec(memory_space=pltpu.VMEM)


def dot(left_side, right_side):
    return jnp.dot(left_side, right_side, preferred_element_type=f32)


def dot_left(left_side, right_side):
    return lax.dot_general(
        left_side, right_side, (((0,), (0,)), ((), ())), preferred_element_type=f32
    )


def dot_right(left_side, right_side):
    return lax.dot_general(
        left_side, right_side, (((1,), (1,)), ((), ())), preferred_element_type=f32
    )


def normal_cdf(values):
    return 0.5 * (1.0 + lax.erf(values * 0.7071067811865476))


def tree_sum(items):
    items = list(items)
    while len(items) > 1:
        items = [items[i] + items[i + 1] for i in range(0, len(items), 2)]
    return items[0]


def aligned(start, size):
    return pl.ds(pl.multiple_of(start, size), size)


def shape(dims, kind=bf16):
    return jax.ShapeDtypeStruct(dims, kind)


def call(kernel, name, outs, scalars, arrays, scratch=(), limit=16):
    return pl.pallas_call(
        kernel,
        out_shape=outs,
        in_specs=[SMEM_SPEC] * len(scalars) + [VMEM_SPEC] * len(arrays),
        out_specs=jax.tree.map(lambda _: VMEM_SPEC, outs),
        scratch_shapes=list(scratch),
        compiler_params=pltpu.CompilerParams(vmem_limit_bytes=limit * 2**20),
        name=name,
    )(*scalars, *arrays)


def without_ids(kernel, ids_ref, *refs):
    kernel(*refs)


class Line:
    def __init__(self, ids):
        self.ids = ids

    def wait(self, *values):
        self.ids = lax.optimization_barrier((self.ids, *values))[0]

    def behind(self, *values):
        return lax.optimization_barrier((self.ids, *values))[1:]

    def __call__(self, kernel, name, outs, scalars, arrays, scratch=(), limit=16, bare=False):
        if bare:
            kernel = functools.partial(without_ids, kernel)
        result = call(kernel, name, outs, (self.ids, *scalars), arrays, scratch, limit)
        self.wait(jax.tree.leaves(result)[0])
        return result


def pick(place, options):
    value = options[0]
    for number, option in enumerate(options[1:], 1):
        value = jnp.where(place == number, option, value)
    return value


def split_three(values):
    high = values.astype(bf16)
    rest = values - high.astype(f32)
    middle = rest.astype(bf16)
    return high, middle, (rest - middle.astype(f32)).astype(bf16)


def join_three(ref, row, *index):
    return tree_sum(
        [ref[(*index, slice(row + part, row + part + 1))].astype(f32) for part in range(3)]
        + [0.0]
    )


def sign_of(values):
    return jnp.where(values > 0, 1.0, jnp.where(values < 0, -1.0, 0.0))


def choose(size, count, start):
    place = lax.broadcasted_iota(jnp.int32, (size, count), 0)
    goal = lax.broadcasted_iota(jnp.int32, (size, count), 1) + start
    return jnp.where(place == goal, 1.0, 0.0).astype(bf16)


def early_pieces_kernel(student, ids_ref, attn_hbm, early_ref, attn_ref, sem):
    k, j = ids_ref[IK], ids_ref[IJ]
    rows_z = attn_hbm.shape[1]
    half = rows_z // CORES
    if student:
        copy = pltpu.make_async_copy(attn_hbm, attn_ref, sem)
    else:
        copy = pltpu.make_async_copy(attn_hbm.at[:, aligned(k * half, half), :], attn_ref, sem)
    copy.start()
    chosen = choose(D, COLS, j * COLS)
    if student:
        early_ref[half:, :] = jnp.zeros((EXTRA, D), bf16)
    copy.wait()
    for number in range(4):
        lanes = slice(number * COLS, (number + 1) * COLS)
        if student:
            full = sign_of(attn_ref[number, aligned(k * half, half), :]).astype(bf16)
            sums = column_total(jnp.abs(attn_ref[number]))
            sums = pick(j, [sums[:, chip * COLS : (chip + 1) * COLS] for chip in range(CHIPS)])
            for part, row in enumerate(split_three(sums)):
                early_ref[half + part : half + part + 1, lanes] = row
        else:
            full = attn_ref[number]
        early_ref[0:half, lanes] = dot(full, chosen).astype(bf16)


def early_pieces(line, student, attn):
    half = attn.shape[1] // CORES
    result = pl.pallas_call(
        functools.partial(early_pieces_kernel, student),
        out_shape=shape((half + EXTRA * student, D)),
        in_specs=[SMEM_SPEC, HBM_SPEC],
        out_specs=VMEM_SPEC,
        scratch_shapes=[
            pltpu.VMEM((4, attn.shape[1] if student else half, D), attn.dtype),
            pltpu.SemaphoreType.DMA,
        ],
        compiler_params=pltpu.CompilerParams(vmem_limit_bytes=12 * 2**20),
        name="early_pieces",
    )(line.ids, attn)
    line.wait(result)
    return result


def late_pieces_kernel(
    n_shard, student, ids_ref, in_hbm, down_hbm, late_ref, in_ref, down_ref, sems
):
    k, j = ids_ref[IK], ids_ref[IJ]
    units = FF // n_shard
    few = units // GROUP
    rows_z = in_ref.shape[0]
    each = rows_z + 2 * few
    number = j * CORES + k
    mine = aligned(number * few, few)
    down_hbm = down_hbm if student else down_hbm.at[mine, :]
    copies = [
        pltpu.make_async_copy(in_hbm, in_ref, sems.at[0]),
        pltpu.make_async_copy(down_hbm, down_ref, sems.at[1]),
    ]
    for copy in copies:
        copy.start()
    chosen = choose(units, few, number * few)
    copies[1].wait()
    if student:
        full = sign_of(down_ref[mine, :]).astype(bf16)
        late_ref[each:, :] = jnp.zeros((EXTRA, HALF), bf16)
        for part, row in enumerate(split_three(column_total(jnp.abs(down_ref[...])))):
            low = each + 3 + part
            late_ref[low : low + 1, :] = row[:, :HALF]
            late_ref[low + 3 : low + 4, :] = row[:, HALF:]
    else:
        full = down_ref[...]
    late_ref[rows_z : rows_z + few, :] = full[:, :HALF]
    late_ref[rows_z + few : each, :] = full[:, HALF:]
    copies[0].wait()
    for place in range(n_shard):
        lanes = slice(place * few, (place + 1) * few)
        full = in_ref[:, place * units : (place + 1) * units]
        if student:
            sums = column_total(jnp.abs(full))
            sums = pick(number, [sums[:, n * few : (n + 1) * few] for n in range(GROUP)])
            for part, row in enumerate(split_three(sums)):
                late_ref[each + part : each + part + 1, lanes] = row
            full = sign_of(full).astype(bf16)
        late_ref[0:rows_z, lanes] = dot(full, chosen).astype(bf16)


def late_pieces(line, n_shard, student, w_in, w_down):
    few = FF // n_shard // GROUP
    rows_z = w_in.shape[0]
    result = pl.pallas_call(
        functools.partial(late_pieces_kernel, n_shard, student),
        out_shape=shape((rows_z + 2 * few + EXTRA * student, HALF)),
        in_specs=[SMEM_SPEC, HBM_SPEC, HBM_SPEC],
        out_specs=VMEM_SPEC,
        scratch_shapes=[
            pltpu.VMEM((rows_z, FF), w_in.dtype),
            pltpu.VMEM((w_down.shape[0] if student else few, D), w_down.dtype),
            pltpu.SemaphoreType.DMA((2,)),
        ],
        compiler_params=pltpu.CompilerParams(vmem_limit_bytes=20 * 2**20),
        name="late_pieces",
    )(line.ids, w_in, w_down)
    line.wait(result)
    return result


def scale_row(sums, gain, fan_in):
    return gain * (sums / fan_in) * fan_in ** (-0.5)


def scaled(values, scale):
    return (values.astype(f32) * scale).astype(bf16)


def early_kernel(n_shard, model, ids_ref, *refs):
    group, refs = refs[:n_shard], refs[n_shard:]
    qkv_ref, out_ref = refs[-2:]
    z = ids_ref[IZ]
    half = D // n_shard // CORES
    fold = n_shard // 2
    base = model * fold * half
    if model:
        out_ref[0:base, :] = refs[0][...]
        sums = tree_sum(join_three(ref, half) for ref in group)
        scale = jnp.concatenate(
            [
                scale_row(sums[:, number * COLS : (number + 1) * COLS], attn_gains[number], D)
                for number in range(4)
            ],
            axis=1,
        )
    for mask, ref in enumerate(group):
        place = z ^ mask
        piece = ref[0:half, :]
        if model:
            piece = scaled(piece, scale)
        qkv_ref[aligned(place * half, half), :] = piece[:, :QKV]
        low = pl.ds(pl.multiple_of(base + lax.rem(place, fold) * half, half), half)

        @pl.when(place < fold)
        def _():
            out_ref[low, 0:COLS] = piece[:, QKV:]

        @pl.when(place >= fold)
        def _():
            out_ref[low, COLS:] = piece[:, QKV:]


def out_weight_kernel(n_shard, ids_ref, *refs):
    k, j = ids_ref[IK], ids_ref[IJ]
    t_ref, s_ref = refs[2 * CHIPS :]
    half = D // n_shard // CORES
    span = n_shard * half // 2
    for core in range(CORES):
        for mask in range(CHIPS):
            ref = refs[core * CHIPS + mask]
            for model, goal in enumerate((t_ref, s_ref)):
                for place in range(n_shard):
                    fold = n_shard // 2
                    low = model * span + (place % fold) * half
                    lanes = slice(0, COLS) if place < fold else slice(COLS, 2 * COLS)
                    rows = pl.ds(
                        pl.multiple_of((place * CORES + (k ^ core)) * half, half), half
                    )
                    goal[j ^ mask, rows, :] = ref[low : low + half, lanes]


def merge_kernel(bit, ids_ref, own_ref, got_ref, both_ref):
    size = own_ref.shape[0]
    mine = (ids_ref[IZ] >> bit) & 1
    both_ref[pl.ds(mine * size, size)] = own_ref[...]
    both_ref[pl.ds((1 - mine) * size, size)] = got_ref[...]


def late_kernel(n_shard, student, ids_ref, *refs):
    groups, vec_ref, refs = refs[:4], refs[4], refs[5:]
    in_ref, down_ref, b1_ref = refs
    z, k, j = ids_ref[IZ], ids_ref[IK], ids_ref[IJ]
    units = FF // n_shard
    few = units // GROUP
    rows_z = D // n_shard
    each = rows_z + 2 * few
    fold = n_shard // 2
    side = lax.div(z, fold)

    def mine(ref, row, core, place):
        options = []
        for chip in range(CHIPS):
            start = place * units + (chip * CORES + core) * few
            low, lane = row + start // D, start % D
            options.append(ref[low : low + 1, lane : lane + few])
        return pick(j, options)

    for core in range(CORES):
        for place in range(n_shard):
            goal = slice(core * HALF + place * few, core * HALF + (place + 1) * few)
            b1_ref[0:1, goal] = mine(vec_ref, 8, core, place)
    if student:
        sums = [
            tree_sum(
                join_three(groups[far], each + 3 * part, number)
                for far in range(2)
                for number in range(fold)
            )
            for part in (1, 2)
        ]
        left_scale, right_scale = (scale_row(row, 1.0, FF) for row in sums)
    for core in range(CORES):
        which = k ^ core
        lanes = aligned(which * HALF, HALF)
        if student:
            scale = tree_sum(
                join_three(groups[core * 2 + far], each, number)
                for far in range(2)
                for number in range(fold)
            )
            scale = scale_row(scale, 1.0, D)
        for far in range(2):
            ref = groups[core * 2 + far]
            for number in range(fold):
                place = (side ^ far) * fold + number
                piece = ref[number, 0:rows_z, :]
                left = ref[number, rows_z : rows_z + few, :]
                right = ref[number, rows_z + few : each, :]
                if student:
                    piece = scaled(piece, scale)
                    left = scaled(left, left_scale)
                    right = scaled(right, right_scale)
                in_ref[aligned(place * rows_z, rows_z), lanes] = piece
                rows = pl.ds(pl.multiple_of(which * HALF + place * few, few), few)
                down_ref[rows, 0:HALF] = left
                down_ref[rows, HALF:] = right


def block_place(rest, per, ids_ref, block_ref, far, mask, core, part):
    k, j, r = ids_ref[IK], ids_ref[IJ], ids_ref[IR]
    chip = (r ^ far) * CHIPS + (j ^ mask)
    return block_ref[(chip * CORES + (k ^ core)) * per + part]


def places_kernel(rest, ids_ref, block_ref, lengths_ref, valid_ref, *outs, seqs, rows):
    length = lengths_ref[ids_ref[IZ] * seqs + ids_ref[IK]]
    per = rows // BLK
    number = 0
    for far in range(rest):
        for mask in range(CHIPS):
            for core in range(CORES):
                for part in range(per):
                    goal = slice(number * BLK, (number + 1) * BLK)
                    number += 1
                    if not outs and mask:
                        continue
                    base = block_place(rest, per, ids_ref, block_ref, far, mask, core, part) * BLK
                    col = base + lax.broadcasted_iota(jnp.int32, (BLK, 1), 0)
                    if far == 0 and mask == 0:
                        valid_ref[goal, :] = jnp.where(col < length, 1.0, 0.0)
                    if outs:
                        outs[1][goal, :] = col
                        if far == 0:
                            row = lax.broadcasted_iota(jnp.int32, (1, BLK), 1)
                            outs[0][:, goal] = base + row


def input_kernel(ids_ref, here_ref, x_ref, y_ref, xy0_ref, xy1_ref, own_ref, send_ref):
    k = ids_ref[IK]
    rows = here_ref.shape[1]
    for mask, ref in enumerate((here_ref, x_ref, y_ref)):
        goal = slice(mask * rows, (mask + 1) * rows)
        own_ref[goal, :] = ref[k]
        send_ref[goal, :] = ref[1 - k]
    goal = slice(3 * rows, 4 * rows)

    @pl.when(k == 0)
    def _():
        own_ref[goal, :] = xy0_ref[...]
        send_ref[goal, :] = xy1_ref[...]

    @pl.when(k == 1)
    def _():
        own_ref[goal, :] = xy1_ref[...]
        send_ref[goal, :] = xy0_ref[...]


def qkv_kernel(n_shard, rest, ids_ref, block_ref, own_ref, oth_ref, half_ref, peer_ref, vec_ref, *outs):
    k, j = ids_ref[IK], ids_ref[IJ]
    q_ref, k_ref, v_ref, w_ref = outs
    half = D // n_shard // CORES
    for core, ref in enumerate((half_ref, peer_ref)):
        for place in range(n_shard):
            rows = pl.ds(pl.multiple_of((place * CORES + (k ^ core)) * half, half), half)
            w_ref[rows, :] = ref[place * half : (place + 1) * half, :]
    weight = w_ref[...]
    chips = [slice(chip * COLS, (chip + 1) * COLS) for chip in range(CHIPS)]
    q_bias = pick(j, [vec_ref[0:1, chip] for chip in chips])
    v_bias = pick(j, [vec_ref[1:2, chip] for chip in chips])
    rows = own_ref.shape[0] // CHIPS
    per = rows // BLK
    for core, ref in enumerate((own_ref, oth_ref)):
        full = dot(ref[...], weight)
        for mask in range(CHIPS):
            result = full[mask * rows : (mask + 1) * rows, :]
            goal = slice((mask * CORES + core) * rows, (mask * CORES + core + 1) * rows)
            sets = (
                (q_ref, result[:, :COLS] + q_bias),
                (k_ref, result[:, COLS : 2 * COLS]),
                (v_ref, result[:, 2 * COLS :] + v_bias),
            )
            for goal_ref, values in sets:
                values = values.astype(bf16)
                for head in range(HEADS_HERE):
                    span = slice(head * HEAD_DIM, (head + 1) * HEAD_DIM)
                    if rest > 1:
                        goal_ref[head, goal, :] = values[:, span]
                        continue
                    for part in range(per):
                        place = block_place(rest, per, ids_ref, block_ref, 0, mask, core, part)
                        goal_ref[head, aligned(place * BLK, BLK), :] = values[
                            part * BLK : (part + 1) * BLK, span
                        ]


def attend_kernel(q_ref, k_ref, v_ref, pq_ref, pk_ref, *outs, tile):
    o_refs, lse_ref, all_ref = outs[:CHIPS], outs[CHIPS], outs[CHIPS + 1]
    tokens = q_ref.shape[1]
    own = tokens // CHIPS

    def one_head(head, carry):
        k_head = k_ref[head]
        v_turned = v_ref[head].T
        for t in range(tokens // tile):
            rows = slice(t * tile, (t + 1) * tile)
            scores = dot_right(k_head, q_ref[head, rows, :]) * (score_scale * log2_e)
            allowed = pq_ref[:, rows] >= pk_ref[...]
            scores = jnp.where(allowed, scores, masked_score)
            peak = jnp.max(scores, axis=0, keepdims=True)
            powers = jnp.exp2(scores - peak)
            total = jnp.sum(powers, axis=0, keepdims=True)
            mixed = dot(v_turned, powers.astype(bf16)) / total
            all_ref[head, rows, :] = mixed.T.astype(bf16)
            lse_ref[head, :, rows] = peak + jnp.log2(total)
        return carry

    lax.fori_loop(0, HEADS_HERE, one_head, 0)
    for head in range(HEADS_HERE):
        span = slice(head * HEAD_DIM, (head + 1) * HEAD_DIM)
        for mask in range(CHIPS):
            o_refs[mask][:, span] = all_ref[head, mask * own : (mask + 1) * own, :]


def sorted_blocks(ids_ref, block_ref, rows):
    per = rows // BLK
    for mask in range(CHIPS):
        for core in range(CORES):
            for part in range(per):
                place = block_place(1, per, ids_ref, block_ref, 0, mask, core, part)
                yield mask, core * rows + part * BLK, aligned(place * BLK, BLK)


def below_diagonal(tile):
    key = lax.broadcasted_iota(jnp.int32, (tile, tile), 0)
    query = lax.broadcasted_iota(jnp.int32, (tile, tile), 1)
    return key <= query


def causal_kernel(ids_ref, block_ref, q_ref, k_ref, v_ref, *outs, tile):
    o_refs, lse_ref, all_ref = outs[:CHIPS], outs[CHIPS], outs[CHIPS + 1]
    tokens = q_ref.shape[1]
    rows = tokens // GROUP
    allowed = below_diagonal(tile)

    def one_head(head, carry):
        v_turned = v_ref[head].T
        for t in range(tokens // tile):
            here = slice(t * tile, (t + 1) * tile)
            q_tile = q_ref[head, here, :]
            scores = dot_right(k_ref[head, here, :], q_tile) * (score_scale * log2_e)
            scores = jnp.where(allowed, scores, masked_score)
            peak = jnp.max(scores, axis=0, keepdims=True)
            if t:
                before = slice(0, t * tile)
                earlier = dot_right(k_ref[head, before, :], q_tile) * (score_scale * log2_e)
                peak = jnp.maximum(peak, jnp.max(earlier, axis=0, keepdims=True))
            powers = jnp.exp2(scores - peak)
            total = jnp.sum(powers, axis=0, keepdims=True)
            mixed = dot(v_turned[:, here], powers.astype(bf16))
            if t:
                powers = jnp.exp2(earlier - peak)
                total = total + jnp.sum(powers, axis=0, keepdims=True)
                mixed = mixed + dot(v_turned[:, before], powers.astype(bf16))
            all_ref[head, here, :] = (mixed / total).T.astype(bf16)
            lse_ref[head, :, here] = peak + jnp.log2(total)
        return carry

    lax.fori_loop(0, HEADS_HERE, one_head, 0)
    for head in range(HEADS_HERE):
        span = slice(head * HEAD_DIM, (head + 1) * HEAD_DIM)
        for mask, low, place in sorted_blocks(ids_ref, block_ref, rows):
            o_refs[mask][low : low + BLK, span] = all_ref[head, place, :]


def norm_parts(values):
    middle = jnp.mean(values, axis=-1, keepdims=True)
    centred = values - middle
    spread = jnp.mean(centred * centred, axis=-1, keepdims=True)
    inverse = lax.rsqrt(spread + norm_eps)
    return centred * inverse, inverse


def norm_back(values, gain, grad_out):
    normal, inverse = norm_parts(values)
    scaled = grad_out * gain
    grad_in = (
        scaled
        - jnp.mean(scaled, axis=-1, keepdims=True)
        - normal * jnp.mean(scaled * normal, axis=-1, keepdims=True)
    ) * inverse
    return grad_in, normal


def column_total(values):
    return jnp.sum(values, axis=0, keepdims=True)


def branch_kernel(student, ids_ref, *refs):
    j = ids_ref[IJ]
    h_refs, (w_ref, own_ref, oth_ref, vec_ref, valid_ref) = refs[:CHIPS], refs[CHIPS : CHIPS + 5]
    outs = refs[CHIPS + 5 :]
    first_ref, sent_ref = outs[:2]
    rows = own_ref.shape[0] // CHIPS
    if student:
        residual_ref, sums_ref = outs[2:]
        sums_ref[...] = jnp.zeros_like(sums_ref)
    for core, x_ref in enumerate((own_ref, oth_ref)):
        goal = slice(core * rows, (core + 1) * rows)
        parts = []
        for chip in range(CHIPS):
            parts.append(
                tree_sum(
                    dot(
                        h_refs[mask][goal, :],
                        w_ref[chip, aligned((j ^ mask) * COLS, COLS), :],
                    )
                    for mask in range(CHIPS)
                )
            )
        branch = jnp.concatenate(parts, axis=1) + vec_ref[2:3, :]
        residual = x_ref[0:rows, :].astype(f32) + branch
        normal, _ = norm_parts(residual)
        first = normal * vec_ref[4:5, :] + vec_ref[5:6, :]
        first_ref[goal, :] = first
        sent_ref[goal, :] = first.astype(bf16)
        if student:
            residual_ref[goal, :] = residual
            sums_ref[0:1, :] += column_total(valid_ref[goal, :] * branch * branch)


def whole(refs):
    if len(refs) == 1:
        return refs[0][...]
    return jnp.concatenate([ref[...] for ref in refs])


def feed_kernel(student, count, *refs):
    pieces, (in_ref, down_ref, b1_ref, part_ref, *outs) = refs[:count], refs[count:]
    inner = dot(whole(pieces), in_ref[...]) + b1_ref[0:1, :]
    act = (inner * normal_cdf(inner)).astype(bf16)
    if student:
        outs[0][...] = inner
        outs[1][...] = act
    part_ref[...] = dot(act, down_ref[...]).astype(part_ref.dtype)


def target_kernel(*refs):
    parts, (first_ref, vec_ref, target_ref) = refs[:CHIPS], refs[CHIPS:]
    feed = tree_sum(ref[...].astype(f32) for ref in parts) + vec_ref[3:4, :]
    normal, _ = norm_parts(first_ref[...] + feed)
    target_ref[...] = normal * vec_ref[6:7, :] + vec_ref[7:8, :]


def loss_kernel(ids_ref, lengths_ref, *refs):
    parts, rest = refs[:CHIPS], refs[CHIPS:]
    first_ref, vec_ref, target_ref, valid_ref, out_ref, grad_ref, sent_ref, sums_ref = rest
    count = lengths_ref[0]
    for number in range(1, lengths_ref.shape[0]):
        count = count + lengths_ref[number]
    share = 1.0 / (count.astype(f32) * D)
    feed = tree_sum(ref[...].astype(f32) for ref in parts) + vec_ref[3:4, :]
    second = first_ref[...] + feed
    normal, inverse = norm_parts(second)
    out = normal * vec_ref[6:7, :] + vec_ref[7:8, :]
    out_ref[...] = out.astype(bf16)
    valid = valid_ref[...]
    mismatch = valid * (out - target_ref[...])
    grad_out = mismatch * share
    scaled = grad_out * vec_ref[6:7, :]
    grad = (
        scaled
        - jnp.mean(scaled, axis=-1, keepdims=True)
        - normal * jnp.mean(scaled * normal, axis=-1, keepdims=True)
    ) * inverse
    grad_ref[...] = grad
    sent_ref[...] = grad.astype(bf16)
    sums_ref[...] = jnp.concatenate(
        [
            column_total(grad),
            column_total(grad_out * normal),
            column_total(grad_out),
            0.5 * column_total(mismatch * mismatch),
            column_total(valid * feed * feed),
            column_total(valid * second * second),
            jnp.zeros((2, D), f32),
        ]
    )


def feed_back_kernel(count, *refs):
    pieces, refs = refs[:count], refs[count:]
    inner_ref, in_ref, down_ref, part_ref, grad_ref, sum_ref = refs
    inner = inner_ref[...]
    slope = normal_cdf(inner) + inner * jnp.exp(-0.5 * inner * inner) * 0.3989422804014327
    grad = dot_right(whole(pieces), down_ref[...]) * slope
    sum_ref[...] = jnp.broadcast_to(column_total(grad), sum_ref.shape)
    grad = grad.astype(bf16)
    grad_ref[...] = grad
    part_ref[...] = dot_right(grad, in_ref[...]).astype(part_ref.dtype)


def branch_back_kernel(ids_ref, *refs):
    j = ids_ref[IJ]
    parts, rest = refs[:CHIPS], refs[CHIPS:]
    second_ref, residual_ref, vec_ref, w_ref = rest[:4]
    grad_ref, sent_ref = rest[4:6]
    h_refs, (sums_ref,) = rest[6 : 6 + CHIPS], rest[6 + CHIPS :]
    grad_first = second_ref[...] + tree_sum(ref[...].astype(f32) for ref in parts)
    grad, normal = norm_back(residual_ref[...], vec_ref[4:5, :], grad_first)
    grad_ref[...] = grad
    sums_ref[...] = jnp.concatenate(
        [
            column_total(grad),
            column_total(grad_first * normal),
            column_total(grad_first),
            jnp.zeros((5, D), f32),
        ]
    )
    grad = grad.astype(bf16)
    sent_ref[...] = grad
    chips = [grad[:, chip * COLS : (chip + 1) * COLS] for chip in range(CHIPS)]
    for mask in range(CHIPS):
        rows = aligned((j ^ mask) * COLS, COLS)
        h_refs[mask][...] = tree_sum(
            dot_right(chips[chip], w_ref[chip, rows, :]) for chip in range(CHIPS)
        ).astype(bf16)


def attend_back_kernel(*refs, tile):
    q_ref, k_ref, v_ref = refs[:3]
    g_refs, refs = refs[3 : 3 + CHIPS], refs[3 + CHIPS :]
    lse_ref, pq_ref, pk_ref, gq_ref, gk_ref, gv_ref, sums_ref = refs[:7]
    g_all, aq_ref, ak_ref, av_ref = refs[7:]
    tokens = q_ref.shape[1]
    own = tokens // CHIPS
    for head in range(HEADS_HERE):
        span = slice(head * HEAD_DIM, (head + 1) * HEAD_DIM)
        for mask in range(CHIPS):
            g_all[head, mask * own : (mask + 1) * own, :] = g_refs[mask][:, span]

    def one_head(head, carry):
        k_head = k_ref[head]
        v_head = v_ref[head]
        k_turned = k_head.T
        for t in range(tokens // tile):
            rows = slice(t * tile, (t + 1) * tile)
            q_tile = q_ref[head, rows, :]
            g_tile = g_all[head, rows, :]
            scores = dot_right(k_head, q_tile) * (score_scale * log2_e)
            allowed = pq_ref[:, rows] >= pk_ref[...]
            scores = jnp.where(allowed, scores, masked_score)
            probs = jnp.exp2(scores - lse_ref[head, :, rows])
            grad_probs = dot_right(v_head, g_tile)
            delta = jnp.sum(probs * grad_probs, axis=0, keepdims=True)
            grad_scores = (probs * (grad_probs - delta)).astype(bf16)
            aq_ref[head, rows, :] = dot(k_turned, grad_scores).T * score_scale
            if t == 0:
                ak_ref[head] = dot(grad_scores, q_tile)
                av_ref[head] = dot(probs.astype(bf16), g_tile)
            else:
                ak_ref[head] += dot(grad_scores, q_tile)
                av_ref[head] += dot(probs.astype(bf16), g_tile)
        return carry

    lax.fori_loop(0, HEADS_HERE, one_head, 0)
    sums_ref[...] = jnp.zeros_like(sums_ref)
    for head in range(HEADS_HERE):
        span = slice(head * HEAD_DIM, (head + 1) * HEAD_DIM)
        grad_query = aq_ref[head]
        grad_value = av_ref[head]
        gq_ref[:, span] = grad_query.astype(bf16)
        gk_ref[:, span] = (ak_ref[head] * score_scale).astype(gk_ref.dtype)
        gv_ref[:, span] = grad_value.astype(gv_ref.dtype)
        sums_ref[0:1, span] = column_total(grad_query)
        sums_ref[1:2, span] = column_total(grad_value)


def causal_back_kernel(ids_ref, block_ref, *refs, tile):
    q_ref, k_ref, v_ref = refs[:3]
    g_refs, refs = refs[3 : 3 + CHIPS], refs[3 + CHIPS :]
    lse_ref, gq_ref, gk_ref, gv_ref, sums_ref, g_all, aq_ref, ak_ref, av_ref = refs
    tokens = q_ref.shape[1]
    rows = tokens // GROUP
    own = tokens // CHIPS
    allowed = below_diagonal(tile)
    for head in range(HEADS_HERE):
        span = slice(head * HEAD_DIM, (head + 1) * HEAD_DIM)
        for mask, low, place in sorted_blocks(ids_ref, block_ref, rows):
            g_all[head, place, :] = g_refs[mask][low : low + BLK, span]

    def one_head(head, carry):
        k_turned = k_ref[head].T
        for t in range(tokens // tile):
            here = slice(t * tile, (t + 1) * tile)
            q_tile = q_ref[head, here, :]
            g_tile = g_all[head, here, :]
            lse = lse_ref[head, :, here]
            scores = dot_right(k_ref[head, here, :], q_tile) * (score_scale * log2_e)
            probs = jnp.exp2(jnp.where(allowed, scores, masked_score) - lse)
            grads = dot_right(v_ref[head, here, :], g_tile)
            delta = jnp.sum(probs * grads, axis=0, keepdims=True)
            if t:
                before = slice(0, t * tile)
                earlier = dot_right(k_ref[head, before, :], q_tile) * (score_scale * log2_e)
                early_probs = jnp.exp2(earlier - lse)
                early_grads = dot_right(v_ref[head, before, :], g_tile)
                delta = delta + jnp.sum(early_probs * early_grads, axis=0, keepdims=True)
            grad_scores = (probs * (grads - delta)).astype(bf16)
            grad_query = dot(k_turned[:, here], grad_scores)
            ak_ref[head, here, :] = dot(grad_scores, q_tile)
            av_ref[head, here, :] = dot(probs.astype(bf16), g_tile)
            if t:
                grad_scores = (early_probs * (early_grads - delta)).astype(bf16)
                grad_query = grad_query + dot(k_turned[:, before], grad_scores)
                ak_ref[head, before, :] += dot(grad_scores, q_tile)
                av_ref[head, before, :] += dot(early_probs.astype(bf16), g_tile)
            aq_ref[head, here, :] = grad_query.T * score_scale
        return carry

    lax.fori_loop(0, HEADS_HERE, one_head, 0)
    sums_ref[...] = jnp.zeros_like(sums_ref)
    for head in range(HEADS_HERE):
        span = slice(head * HEAD_DIM, (head + 1) * HEAD_DIM)
        sums_ref[0:1, span] = column_total(aq_ref[head])
        sums_ref[1:2, span] = column_total(av_ref[head])
        for mask, low, place in sorted_blocks(ids_ref, block_ref, rows):
            goal = slice(mask * own + low, mask * own + low + BLK)
            gq_ref[goal, span] = aq_ref[head, place, :].astype(bf16)
            gk_ref[goal, span] = (ak_ref[head, place, :] * score_scale).astype(bf16)
            gv_ref[goal, span] = av_ref[head, place, :].astype(bf16)


def qkv_back_kernel(gq_ref, gk_ref, gv_ref, w_ref, *part_refs):
    own = gq_ref.shape[0] // CHIPS
    for mask in range(CHIPS):
        rows = slice(mask * own, (mask + 1) * own)
        part_refs[mask][...] = (
            dot_right(gq_ref[rows, :], w_ref[:, :COLS])
            + dot_right(gk_ref[rows, :], w_ref[:, COLS : 2 * COLS])
            + dot_right(gv_ref[rows, :], w_ref[:, 2 * COLS :])
        ).astype(part_refs[mask].dtype)


def hidden_kernel(res_ref, *refs):
    parts, (own_ref, send_ref) = refs[:CHIPS], refs[CHIPS:]
    total = res_ref[...] + tree_sum(ref[...].astype(f32) for ref in parts)
    rows = own_ref.shape[0]
    own_ref[...] = total[:rows, :]
    send_ref[...] = total[rows:, :]


def late_grad_kernel(n_shard, counts, ids_ref, *refs):
    k = ids_ref[IK]
    groups = []
    for count in counts:
        groups.append(refs[:count])
        refs = refs[count:]
    acts, feeds, firsts, inners = (groups[i * CHIPS : (i + 1) * CHIPS] for i in range(4))
    own_ref, send_ref, down_ref, in_ref = refs
    down_ref[...] = tree_sum(dot_left(whole(a), whole(g)) for a, g in zip(acts, feeds))
    in_ref[...] = tree_sum(dot_left(whole(a), whole(g)) for a, g in zip(firsts, inners))
    few = FF // n_shard // GROUP
    rows_z = D // n_shard
    each = rows_z + 2 * few
    for goal_ref, half in ((own_ref, k), (send_ref, 1 - k)):
        kind = goal_ref.dtype
        lanes = aligned(half * HALF, HALF)
        for place in range(n_shard):
            goal_ref[place, 0:rows_z, :] = in_ref[
                place * rows_z : (place + 1) * rows_z, lanes
            ].astype(kind)
            rows = pl.ds(pl.multiple_of(half * HALF + place * few, few), few)
            goal_ref[place, rows_z : rows_z + few, :] = down_ref[rows, :HALF].astype(kind)
            goal_ref[place, rows_z + few : each, :] = down_ref[rows, HALF:].astype(kind)


def late_split_kernel(n_shard, ids_ref, own_ref, got_ref, *outs):
    for mask in range(n_shard):
        place = ids_ref[IZ] ^ mask
        outs[mask][...] = (own_ref[place] + got_ref[place].astype(f32)).astype(outs[mask].dtype)


def sum_kernel(*refs):
    refs[-1][...] = tree_sum(ref[...].astype(f32) for ref in refs[:-1]).astype(bf16)


def late_final_kernel(n_shard, ids_ref, *refs):
    k, j = ids_ref[IK], ids_ref[IJ]
    pieces, (in_latent_ref, down_latent_ref, in_ref, down_ref, all_ref) = refs[:GROUP], refs[GROUP:]
    few = FF // n_shard // GROUP
    rows_z = D // n_shard
    for core in range(CORES):
        for mask in range(CHIPS):
            all_ref[(j ^ mask) * CORES + (k ^ core)] = pieces[core * CHIPS + mask][...]
    for number in range(GROUP):
        for place in range(n_shard):
            goal = (place * GROUP + number) * few
            lanes = slice(goal, goal + few)
            grad = all_ref[number, 0:rows_z, place * few : (place + 1) * few].astype(f32)
            keep = jnp.abs(in_latent_ref[:, lanes]) <= 1.0
            in_ref[:, lanes] = jnp.where(keep, grad, 0.0)
        rows = slice(number * few, (number + 1) * few)
        for part in range(2):
            lanes = slice(part * HALF, (part + 1) * HALF)
            low = rows_z + part * few
            grad = all_ref[number, low : low + few, :].astype(f32)
            keep = jnp.abs(down_latent_ref[rows, lanes]) <= 1.0
            down_ref[rows, lanes] = jnp.where(keep, grad, 0.0)


def out_grad_kernel(n_shard, ids_ref, *refs):
    j = ids_ref[IJ]
    h_refs, grad_ref = refs[:CHIPS], refs[CHIPS]
    outs, (cols_ref, full_ref) = refs[CHIPS + 1 : CHIPS + 1 + CHIPS], refs[CHIPS + 1 + CHIPS :]
    half = D // n_shard // CORES
    for chip in range(CHIPS):
        cols_ref[chip] = grad_ref[:, chip * COLS : (chip + 1) * COLS]
    for goal in range(CHIPS):
        cols = cols_ref[j ^ goal]
        for mask in range(CHIPS):
            full_ref[aligned((j ^ mask) * COLS, COLS), :] = dot_left(h_refs[mask][...], cols)
        for core in range(CORES):
            for place in range(n_shard):
                low = (place * CORES + core) * half
                outs[goal][place * half : (place + 1) * half, core * COLS : (core + 1) * COLS] = (
                    full_ref[low : low + half, :].astype(outs[goal].dtype)
                )


def split_hi_lo(values):
    high = values.astype(bf16)
    low = (values - high.astype(f32)).astype(bf16)
    return high, low


def early_grad_kernel(n_shard, ids_ref, *refs):
    k = ids_ref[IK]
    own_x, oth_x, gq_ref, gk_ref, gv_ref = refs[:5]
    outs, refs = refs[5 : 5 + CHIPS], refs[5 + CHIPS :]
    branch_sums, loss_sums, res_sums = refs[:3]
    b1_sums, refs = refs[3 : 3 + CHIPS], refs[3 + CHIPS :]
    qv_sums, own_ref, vec_ref, send_ref, full_ref = refs
    half = D // n_shard // CORES
    rows = own_x.shape[0] // CHIPS
    for number, g_ref in enumerate((gq_ref, gk_ref, gv_ref)):
        parts = []
        for core, x_ref in enumerate((own_x, oth_x)):
            for mask in range(CHIPS):
                goal = slice((mask * CORES + core) * rows, (mask * CORES + core + 1) * rows)
                parts.append(dot_left(x_ref[mask * rows : (mask + 1) * rows, :], g_ref[goal, :]))
        full_ref[:, number * COLS : (number + 1) * COLS] = tree_sum(parts)
    total = tree_sum(ref[...].astype(f32) for ref in outs)
    for place in range(n_shard):
        for core in range(CORES):
            low = (place * CORES + core) * half
            full_ref[low : low + half, QKV:] = total[
                place * half : (place + 1) * half, core * COLS : (core + 1) * COLS
            ]
    for place in range(n_shard):
        goal = slice(place * half, (place + 1) * half)
        mine = pl.ds(pl.multiple_of((place * CORES + k) * half, half), half)
        theirs = pl.ds(pl.multiple_of((place * CORES + 1 - k) * half, half), half)
        own_ref[goal, :] = full_ref[mine, :]
        send_ref[goal, :] = full_ref[theirs, :].astype(bf16)
    lane = lax.broadcasted_iota(jnp.int32, (1, 2 * COLS), 1)
    stats = jnp.zeros((1, 2 * COLS), f32)
    for number, row in enumerate(
        (loss_sums[3:4, :], branch_sums[0:1, :], loss_sums[4:5, :], loss_sums[5:6, :])
    ):
        stats = stats + jnp.where(lane == number, jnp.sum(row, axis=1, keepdims=True), 0.0)
    table = jnp.concatenate(
        [
            res_sums[0:1, :],
            loss_sums[0:1, :],
            res_sums[1:3, :],
            loss_sums[1:3, :],
            tree_sum(ref[0:1, :] for ref in b1_sums),
            jnp.concatenate([qv_sums[0:1, :], qv_sums[1:2, :], stats], axis=1),
        ]
    )
    high, low = split_hi_lo(table)
    base = n_shard * half
    send_ref[base : base + VEC_ROWS, :] = high
    send_ref[base + VEC_ROWS : base + 2 * VEC_ROWS, :] = low
    vec_ref[...] = high.astype(f32) + low.astype(f32)


def early_split_kernel(n_shard, ids_ref, own_ref, vec_ref, got_ref, *outs):
    z = ids_ref[IZ]
    half = D // n_shard // CORES
    base = n_shard * half
    table = vec_ref[...] + (
        got_ref[base : base + VEC_ROWS, :].astype(f32)
        + got_ref[base + VEC_ROWS : base + 2 * VEC_ROWS, :].astype(f32)
    )
    high, low = split_hi_lo(table)
    for mask in range(n_shard):
        rows = aligned((z ^ mask) * half, half)
        kind = outs[mask].dtype
        outs[mask][0:half, :] = (own_ref[rows, :] + got_ref[rows, :].astype(f32)).astype(kind)
        outs[mask][half : half + VEC_ROWS, :] = high.astype(kind)
        outs[mask][half + VEC_ROWS : half + 2 * VEC_ROWS, :] = low.astype(kind)


def early_sum_kernel(*refs):
    ins, out_ref = refs[:-1], refs[-1]
    half = out_ref.shape[0] - 2 * VEC_ROWS
    out_ref[0:half, :] = tree_sum(ref[0:half, :].astype(f32) for ref in ins).astype(bf16)
    table = tree_sum(
        ref[half : half + VEC_ROWS, :].astype(f32)
        + ref[half + VEC_ROWS : half + 2 * VEC_ROWS, :].astype(f32)
        for ref in ins
    )
    high, low = split_hi_lo(table)
    out_ref[half : half + VEC_ROWS, :] = high
    out_ref[half + VEC_ROWS : half + 2 * VEC_ROWS, :] = low


def early_final_kernel(n_shard, ids_ref, lengths_ref, *refs):
    k, j = ids_ref[IK], ids_ref[IJ]
    pieces = refs[:GROUP]
    latent_ref, attn_ref, vec_ref, query_ref, stats_ref, all_ref, rows_ref, flat_ref = refs[GROUP:]
    half = D // n_shard // CORES
    few = FF // n_shard // GROUP
    units = FF // n_shard
    for core in range(CORES):
        for mask in range(CHIPS):
            ref = pieces[core * CHIPS + mask]
            all_ref[(j ^ mask) * CORES + (k ^ core)] = ref[0:half, :]
    for chip in range(CHIPS):
        for core in range(CORES):
            for number in range(4):
                lanes = slice(chip * COLS, (chip + 1) * COLS)
                rows = slice(core * half, (core + 1) * half)
                grad = all_ref[
                    chip * CORES + core, :, number * COLS : (number + 1) * COLS
                ].astype(f32)
                keep = jnp.abs(latent_ref[number, rows, lanes]) <= 1.0
                attn_ref[number, rows, lanes] = jnp.where(keep, grad, 0.0)
    tables = [
        pieces[mask][half : half + VEC_ROWS, :].astype(f32)
        + pieces[mask][half + VEC_ROWS : half + 2 * VEC_ROWS, :].astype(f32)
        for mask in range(CHIPS)
    ]
    total = tree_sum(tables)
    for mask in range(CHIPS):
        rows_ref[j ^ mask] = tables[mask]
    count = lengths_ref[0]
    for number in range(1, lengths_ref.shape[0]):
        count = count + lengths_ref[number]
    scale = count.astype(f32) * D
    stats = total[ROW_QV : ROW_QV + 1, 2 * COLS : 2 * COLS + 128] / scale
    lane = lax.broadcasted_iota(jnp.int32, (1, 128), 1)
    stats_ref[...] = jnp.where(lane == 0, stats, jnp.sqrt(stats))
    vec_ref[1:7, :] = total[0:6, :]
    for chip in range(CHIPS):
        lanes = slice(chip * COLS, (chip + 1) * COLS)
        query_ref[:, lanes] = rows_ref[chip, ROW_QV : ROW_QV + 1, 0:COLS]
        vec_ref[0:1, lanes] = rows_ref[chip, ROW_QV : ROW_QV + 1, COLS : 2 * COLS]
        for core in range(CORES):
            for place in range(n_shard):
                start = place * units + (chip * CORES + core) * few
                row, lane = 7 + start // D, start % D
                vec_ref[row : row + 1, lane : lane + few] = rows_ref[
                    chip, ROW_B1 : ROW_B1 + 1, core * HALF + place * few : core * HALF + (place + 1) * few
                ]


def owners_kernel(ids_ref, here_ref, there_ref, out_ref):
    k = ids_ref[IK]
    out_ref[k] = here_ref[...]
    out_ref[1 - k] = there_ref[...]


def body(
    hidden_in,
    block_of,
    lengths,
    attn_latent,
    ffn_in_latent,
    ffn_out_latent,
    student_vec,
    teacher_attn,
    teacher_ffn_in,
    teacher_ffn_out,
    teacher_vec,
):
    seqs, rows, _ = hidden_in.shape
    rest = lax.axis_size("rest")
    n_shard = lax.axis_size("shard")
    own = seqs * rows
    tokens = CHIPS * own
    keys = rest * tokens
    ids = jnp.stack([lax.axis_index(name) for name in ("shard", "core", "chip", "rest")])
    half = D // n_shard // CORES
    few = FF // n_shard // GROUP
    rows_z = D // n_shard
    each = rows_z + 2 * few
    line = Line(ids.astype(jnp.int32))

    def flip(piece, axis, mask):
        size = lax.axis_size(axis)
        return lax.ppermute(piece, axis, [(a, a ^ mask) for a in range(size)])

    def gather(piece, axis):
        return [piece] + [flip(piece, axis, m) for m in range(1, lax.axis_size(axis))]

    def exchange(pieces, axis):
        return [pieces[0]] + [flip(pieces[m], axis, m) for m in range(1, len(pieces))]

    def swap(piece):
        return flip(piece, "core", 1)

    def near_rows(piece):
        return [piece, flip(piece, "chip", 1), flip(piece, "chip", 2)]

    def all_rows(near):
        near = [near[0], *line.behind(*near[1:])]
        half = near[0].shape[0] // 2
        far = (flip(near[2][:half], "chip", 1), flip(near[1][half:], "chip", 2))
        return [(near[0],), (near[1],), (near[2],), far]

    def spread_z(piece):
        bits = n_shard.bit_length() - 1
        own = piece[None]
        for bit in range(bits):
            got = flip(own, "shard", 1 << bit)
            if bit == bits - 1:
                return own, got
            own = line(
                functools.partial(merge_kernel, bit),
                "merge",
                shape((2 * own.shape[0], *own.shape[1:])),
                (),
                (own, got),
                limit=6,
            )

    near = near_rows(hidden_in)
    t_early = early_pieces(line, False, teacher_attn)
    s_early = early_pieces(line, True, attn_latent)
    outs = [shape((own, 1), f32)]
    if rest > 1:
        outs += [shape((1, tokens), jnp.int32), shape((keys, 1), jnp.int32)]
    valid, *positions = line(
        functools.partial(places_kernel, rest, seqs=seqs, rows=rows),
        "places",
        tuple(outs),
        (block_of, lengths),
        (),
    )
    t_qkv_half, t_out_half = line(
        functools.partial(early_kernel, n_shard, 0),
        "early_weights",
        (shape((n_shard * half, QKV)), shape((n_shard * half // 2, 2 * COLS))),
        (),
        gather(t_early, "shard"),
    )
    pieces = [piece for group in all_rows(near) for piece in group]
    t_late = late_pieces(line, n_shard, False, teacher_ffn_in, teacher_ffn_out)
    s_late = late_pieces(line, n_shard, True, ffn_in_latent, ffn_out_latent)
    pieces = pieces[:3] + [piece[0] for piece in pieces[3:]]
    x_own, x_send = line(
        input_kernel,
        "input",
        (shape((tokens // CORES, D)), shape((tokens // CORES, D))),
        (),
        pieces,
    )
    x_oth = swap(x_send)
    def rest_gather(values):
        if rest == 1:
            return values
        return jnp.concatenate(gather(values, "rest"), axis=1)

    def rest_scatter(partial):
        if rest == 1:
            return partial
        view = partial.reshape(rest, tokens, COLS)
        return tree_sum(
            [view[0]]
            + [flip(view[m].astype(bf16), "rest", m).astype(f32) for m in range(1, rest)]
        ).astype(bf16)

    def project(qkv_half, vector):
        heads = shape((HEADS_HERE, tokens, HEAD_DIM))
        query, key, value, w_qkv = line(
            functools.partial(qkv_kernel, n_shard, rest),
            "qkv",
            (heads, heads, heads, shape((D, QKV))),
            (block_of,),
            [x_own, x_oth, qkv_half, swap(qkv_half), vector],
        )
        return query, rest_gather(key), rest_gather(value), w_qkv

    def attend(query, key, value):
        outs = tuple([shape((own, COLS))] * CHIPS + [shape((HEADS_HERE, 1, tokens), f32)])
        scratch = (pltpu.VMEM((HEADS_HERE, tokens, HEAD_DIM), bf16),)
        if rest == 1:
            *heads, lse = line(
                functools.partial(causal_kernel, tile=own),
                "attend",
                outs,
                (block_of,),
                (query, key, value),
                scratch,
            )
        else:
            *heads, lse = line(
                functools.partial(attend_kernel, tile=own),
                "attend",
                outs,
                (),
                (query, key, value, *positions),
                scratch,
                limit=48,
                bare=True,
            )
        return exchange(heads, "chip"), lse

    def branch(student, heads, w_out, vector):
        outs = [shape((own, D), f32), shape((own, D))]
        if student:
            outs += [shape((own, D), f32), shape((8, D), f32)]
        return line(
            functools.partial(branch_kernel, student),
            "branch",
            tuple(outs),
            (),
            (*heads, w_out, x_own, x_oth, vector, valid),
        )

    def late_weights(student, near_far, vector):
        return line(
            functools.partial(late_kernel, n_shard, student),
            "late_weights",
            (shape((D, UNITS)), shape((UNITS, D)), shape((8, UNITS), f32)),
            (),
            [*near_far, *[swap(piece) for piece in near_far], vector],
        )

    def feed(student, pieces, mask, late):
        outs = [shape((own, D), f32 if mask == 0 else bf16)]
        if student:
            outs += [shape((own, UNITS), f32), shape((own, UNITS))]
        return line(
            functools.partial(feed_kernel, student, len(pieces)),
            "feed",
            tuple(outs),
            (),
            (*pieces, *late),
            bare=True,
        )

    t_query, t_key, t_value, _ = project(t_qkv_half, teacher_vec)
    (s_late,) = line.behind(s_late)
    s_qkv_half, out_half = line(
        functools.partial(early_kernel, n_shard, 1),
        "early_weights",
        (shape((n_shard * half, QKV)), shape((n_shard * half, 2 * COLS))),
        (),
        gather(s_early, "shard") + [t_out_half],
    )
    t_late = spread_z(t_late)
    t_heads, _ = attend(t_query, t_key, t_value)
    out_all = gather(out_half, "chip")
    query, key, value, w_qkv = project(s_qkv_half, student_vec)
    s_late = spread_z(s_late)
    t_out, s_out = line(
        functools.partial(out_weight_kernel, n_shard),
        "out_weights",
        (shape((CHIPS, D, COLS)), shape((CHIPS, D, COLS))),
        (),
        out_all + [swap(piece) for piece in out_all],
    )
    t_first, t_sent = branch(False, t_heads, t_out, teacher_vec)
    t_near = near_rows(t_sent)
    t_late = line.behind(*t_late)
    heads, lse = attend(query, key, value)
    t_late = late_weights(False, t_late, teacher_vec)
    t_parts = [feed(False, (t_sent,), 0, t_late)[0]]
    t_firsts = all_rows(t_near)
    first, sent, residual, branch_sums = branch(True, heads, s_out, student_vec)
    near = near_rows(sent)
    for m in (1, 2):
        t_parts.append(feed(False, t_firsts[m], m, t_late)[0])
    s_late = late_weights(True, line.behind(*s_late), student_vec)
    w_in, w_down, _ = s_late
    fed = [feed(True, (sent,), 0, s_late)]
    firsts = all_rows(near)
    t_parts.append(feed(False, t_firsts[3], 3, t_late)[0])
    t_parts = exchange(t_parts, "chip")
    fed += [feed(True, firsts[m], m, s_late) for m in range(1, CHIPS)]
    parts, inners, acts = ([f[i] for f in fed] for i in range(3))
    target = line(
        target_kernel,
        "target",
        shape((own, D), f32),
        (),
        (*t_parts, t_first, teacher_vec),
        bare=True,
    )
    out, grad_second, sent, loss_sums = line(
        loss_kernel,
        "loss",
        (shape((own, D)), shape((own, D), f32), shape((own, D)), shape((8, D), f32)),
        (lengths,),
        (*exchange(parts, "chip"), first, student_vec, target, valid),
    )

    near = near_rows(sent)

    def to_owners(here, there):
        return line(
            owners_kernel,
            "owners",
            shape((CORES, *here.shape), here.dtype),
            (),
            (here, swap(there)),
        )

    def feed_back(pieces, m):
        return line(
            functools.partial(feed_back_kernel, len(pieces)),
            "feed_back",
            (
                shape((own, D), f32 if m == 0 else bf16),
                shape((own, UNITS)),
                shape((8, UNITS), f32),
            ),
            (),
            (*pieces, inners[m], w_in, w_down),
            bare=True,
        )

    backs = [feed_back((sent,), 0)]
    feeds = all_rows(near)
    backs += [feed_back(feeds[m], m) for m in range(1, CHIPS)]
    output = to_owners(out[:rows], out[rows:])
    parts, grad_inners, b1_sums = ([b[i] for b in backs] for i in range(3))
    groups = [(act,) for act in acts] + feeds + firsts + [(inner,) for inner in grad_inners]
    keep, send = line(
        functools.partial(late_grad_kernel, n_shard, [len(group) for group in groups]),
        "late_grad",
        (shape((n_shard, each, HALF), f32), shape((n_shard, each, HALF))),
        (),
        [piece for group in groups for piece in group],
        (pltpu.VMEM((UNITS, D), f32), pltpu.VMEM((D, UNITS), f32)),
        limit=24,
    )
    grad_res, grad_branch, *rest_outs = line(
        branch_back_kernel,
        "branch_back",
        tuple(
            [shape((own, D), f32), shape((own, D))]
            + [shape((own, COLS))] * CHIPS
            + [shape((8, D), f32)]
        ),
        (),
        (*exchange(parts, "chip"), grad_second, residual, student_vec, s_out),
    )
    grad_heads, res_sums = exchange(rest_outs[:CHIPS], "chip"), rest_outs[CHIPS]
    late_pieces_out = line(
        functools.partial(late_split_kernel, n_shard),
        "late_split",
        tuple(shape((each, HALF), f32 if m == 0 else bf16) for m in range(n_shard)),
        (),
        (keep, swap(*line.behind(send))),
    )
    late_got = [late_pieces_out[0]]

    def late_exchange(*masks):
        for m in masks:
            if m < n_shard:
                late_got.append(flip(*line.behind(late_pieces_out[m]), "shard", m))

    late_exchange(1)
    out_parts = line(
        functools.partial(out_grad_kernel, n_shard),
        "out_grad",
        tuple(
            shape((n_shard * half, 2 * COLS), f32 if m == 0 else bf16) for m in range(CHIPS)
        ),
        (),
        (*heads, grad_branch),
        (pltpu.VMEM((CHIPS, own, COLS), bf16), pltpu.VMEM((D, COLS), f32)),
    )
    line.wait(*grad_heads)
    out_parts = list(line.behind(*out_parts))
    late_exchange(2)
    outs = (
        shape((tokens, COLS)),
        shape((keys, COLS), bf16 if rest == 1 else f32),
        shape((keys, COLS), bf16 if rest == 1 else f32),
        shape((8, COLS), f32),
    )
    scratch = (
        pltpu.VMEM((HEADS_HERE, tokens, HEAD_DIM), bf16),
        pltpu.VMEM((HEADS_HERE, tokens, HEAD_DIM), f32),
        pltpu.VMEM((HEADS_HERE, keys, HEAD_DIM), f32),
        pltpu.VMEM((HEADS_HERE, keys, HEAD_DIM), f32),
    )
    if rest == 1:
        grad_query, grad_key, grad_value, qv_sums = line(
            functools.partial(causal_back_kernel, tile=own),
            "attend_back",
            outs,
            (block_of,),
            (query, key, value, *grad_heads, lse),
            scratch,
            limit=28,
        )
    else:
        grad_query, grad_key, grad_value, qv_sums = line(
            functools.partial(attend_back_kernel, tile=own),
            "attend_back",
            outs,
            (),
            (query, key, value, *grad_heads, lse, *positions),
            scratch,
            limit=56,
            bare=True,
        )
    grad_key, grad_value = rest_scatter(grad_key), rest_scatter(grad_value)
    line.wait(late_got[-1])
    mine, table, send = line(
        functools.partial(early_grad_kernel, n_shard),
        "early_grad",
        (
            shape((n_shard * half, D), f32),
            shape((VEC_ROWS, D), f32),
            shape((n_shard * half + 2 * VEC_ROWS, D)),
        ),
        (),
        (
            x_own,
            x_oth,
            grad_query,
            grad_key,
            grad_value,
            *exchange(out_parts, "chip"),
            branch_sums,
            loss_sums,
            res_sums,
            *b1_sums,
            qv_sums,
        ),
        (pltpu.VMEM((D, D), f32),),
        limit=20,
    )
    parts = line(
        qkv_back_kernel,
        "qkv_back",
        tuple(shape((own, D), f32 if m == 0 else bf16) for m in range(CHIPS)),
        (),
        (grad_query, grad_key, grad_value, w_qkv),
        bare=True,
    )
    pieces = line(
        functools.partial(early_split_kernel, n_shard),
        "early_split",
        tuple(
            shape((half + 2 * VEC_ROWS, D), f32 if m == 0 else bf16) for m in range(n_shard)
        ),
        (),
        (mine, table, swap(send)),
    )
    late_exchange(*range(3, n_shard))
    parts = line.behind(*parts)
    early = line(
        early_sum_kernel,
        "early_sum",
        shape((half + 2 * VEC_ROWS, D)),
        (),
        exchange(pieces, "shard"),
        bare=True,
    )
    if rest > 1:
        early = line(
            early_sum_kernel, "rest_sum", shape(early.shape), (), gather(early, "rest"), bare=True
        )
    here, there = line(
        hidden_kernel,
        "hidden",
        (shape((rows, D), f32), shape((rows, D), f32)),
        (),
        (grad_res, *exchange(parts, "chip")),
        bare=True,
    )
    late = line(sum_kernel, "late_sum", shape((each, HALF)), (), late_got, bare=True)
    if rest > 1:
        late = line(sum_kernel, "rest_sum", shape(late.shape), (), gather(late, "rest"), bare=True)
    late = gather(late, "chip")
    grad_hidden = to_owners(here, there)
    early = gather(early, "chip")
    attn_grad, vec_grad, query_grad, stats = line(
        functools.partial(early_final_kernel, n_shard),
        "early_final",
        (
            shape(attn_latent.shape, f32),
            shape((7 + FF // D, D), f32),
            shape((1, D), f32),
            shape((1, 128), f32),
        ),
        (lengths,),
        (*early, *[swap(piece) for piece in early], attn_latent),
        (
            pltpu.VMEM((GROUP, half, D), bf16),
            pltpu.VMEM((CHIPS, VEC_ROWS, D), f32),
            pltpu.VMEM((8, D), f32),
        ),
    )
    in_grad, down_grad = line(
        functools.partial(late_final_kernel, n_shard),
        "late_final",
        (shape(ffn_in_latent.shape, f32), shape(ffn_out_latent.shape, f32)),
        (),
        (*late, *[swap(piece) for piece in late], ffn_in_latent, ffn_out_latent),
        (pltpu.VMEM((GROUP, each, HALF), bf16),),
    )
    return (
        output,
        stats[0, :4],
        grad_hidden,
        attn_grad,
        in_grad,
        down_grad,
        vec_grad,
        query_grad[0],
    )


def solution(mesh):
    n_ctx, n_shard = mesh.shape["ctx"], mesh.shape["shard"]
    places = mesh.devices.reshape(n_ctx // GROUP, CHIPS, CORES, n_shard)
    inner = Mesh(places, ("rest", "chip", "core", "shard"))
    ctx = ("rest", "chip", "core")
    in_specs = (
        P("shard", ctx, None),
        P(),
        P(),
        P(None, "shard", None),
        P("shard", None),
        P("shard", None),
        P(),
        P(None, "shard", None),
        P("shard", None),
        P("shard", None),
        P(),
    )
    out_specs = (
        P("shard", ctx, None),
        P(),
        P("shard", ctx, None),
        P(None, "shard", None),
        P("shard", None),
        P("shard", None),
        P(),
        P(),
    )
    return jax.shard_map(
        body, mesh=inner, in_specs=in_specs, out_specs=out_specs, check_vma=False
    )
```

```python
import functools

import jax
import jax.numpy as jnp
from jax import lax
from jax.experimental import pallas as pl
from jax.experimental.pallas import tpu as pltpu
from jax.sharding import Mesh
from jax.sharding import PartitionSpec as P

D = 768
HEADS = 12
HEAD_DIM = 64
FF = 3072
BLK = 64

CHIPS = 4
CORES = 2
GROUP = CHIPS * CORES
COLS = D // CHIPS
HEADS_HERE = HEADS // CHIPS
UNITS = FF // CHIPS
HALF = UNITS // CORES
QKV = 3 * COLS

norm_eps = 1e-05
attn_gains = (2.0, 2.0, 1.0, 4.0)
masked_score = -1e30
score_scale = HEAD_DIM ** (-0.5)
log2_e = 1.4426950408889634
bf16 = jnp.bfloat16
f32 = jnp.float32

IZ, IK, IJ, IR = 0, 1, 2, 3
ROW_BO, ROW_B2, ROW_G1, ROW_C1, ROW_G2, ROW_C2, ROW_B1, ROW_QV = range(8)
VEC_ROWS = 8
EXTRA = 16

SMEM_SPEC = pl.BlockSpec(memory_space=pltpu.SMEM)
VMEM_SPEC = pl.BlockSpec(memory_space=pltpu.VMEM)


def dot(left_side, right_side):
    return jnp.dot(left_side, right_side, preferred_element_type=f32)


def dot_left(left_side, right_side):
    return lax.dot_general(
        left_side, right_side, (((0,), (0,)), ((), ())), preferred_element_type=f32
    )


def dot_right(left_side, right_side):
    return lax.dot_general(
        left_side, right_side, (((1,), (1,)), ((), ())), preferred_element_type=f32
    )


def normal_cdf(values):
    return 0.5 * (1.0 + lax.erf(values * 0.7071067811865476))


def tree_sum(items):
    items = list(items)
    while len(items) > 1:
        items = [items[i] + items[i + 1] for i in range(0, len(items), 2)]
    return items[0]


def aligned(start, size):
    return pl.ds(pl.multiple_of(start, size), size)


def shape(dims, kind=bf16):
    return jax.ShapeDtypeStruct(dims, kind)


def call(kernel, name, outs, scalars, arrays, scratch=(), limit=16):
    return pl.pallas_call(
        kernel,
        out_shape=outs,
        in_specs=[SMEM_SPEC] * len(scalars) + [VMEM_SPEC] * len(arrays),
        out_specs=jax.tree.map(lambda _: VMEM_SPEC, outs),
        scratch_shapes=list(scratch),
        compiler_params=pltpu.CompilerParams(vmem_limit_bytes=limit * 2**20),
        name=name,
    )(*scalars, *arrays)


def without_ids(kernel, ids_ref, *refs):
    kernel(*refs)


class Line:
    def __init__(self, ids):
        self.ids = ids

    def wait(self, *values):
        self.ids = lax.optimization_barrier((self.ids, *values))[0]

    def behind(self, *values):
        return lax.optimization_barrier((self.ids, *values))[1:]

    def __call__(self, kernel, name, outs, scalars, arrays, scratch=(), limit=16, bare=False):
        if bare:
            kernel = functools.partial(without_ids, kernel)
        result = call(kernel, name, outs, (self.ids, *scalars), arrays, scratch, limit)
        self.wait(jax.tree.leaves(result)[0])
        return result


def pick(place, options):
    value = options[0]
    for number, option in enumerate(options[1:], 1):
        value = jnp.where(place == number, option, value)
    return value


def split_three(values):
    high = values.astype(bf16)
    rest = values - high.astype(f32)
    middle = rest.astype(bf16)
    return high, middle, (rest - middle.astype(f32)).astype(bf16)


def join_three(ref, row, *index):
    return tree_sum(
        [ref[(*index, slice(row + part, row + part + 1))].astype(f32) for part in range(3)]
        + [0.0]
    )


def sign_of(values):
    return jnp.where(values > 0, 1.0, jnp.where(values < 0, -1.0, 0.0))


def choose(size, count, start):
    place = lax.broadcasted_iota(jnp.int32, (size, count), 0)
    goal = lax.broadcasted_iota(jnp.int32, (size, count), 1) + start
    return jnp.where(place == goal, 1.0, 0.0).astype(bf16)


def early_pieces_kernel(student, ids_ref, attn_ref, early_ref):
    k, j = ids_ref[IK], ids_ref[IJ]
    rows_z = attn_ref.shape[1]
    half = rows_z // CORES
    chosen = choose(D, COLS, j * COLS)
    if student:
        early_ref[half:, :] = jnp.zeros((EXTRA, D), bf16)
    for number in range(4):
        lanes = slice(number * COLS, (number + 1) * COLS)
        if student:
            full = sign_of(attn_ref[number, aligned(k * half, half), :]).astype(bf16)
            sums = column_total(jnp.abs(attn_ref[number]))
            sums = pick(j, [sums[:, chip * COLS : (chip + 1) * COLS] for chip in range(CHIPS)])
            for part, row in enumerate(split_three(sums)):
                early_ref[half + part : half + part + 1, lanes] = row
        else:
            full = attn_ref[number, aligned(k * half, half), :]
        early_ref[0:half, lanes] = dot(full, chosen).astype(bf16)


def early_pieces(line, student, attn):
    half = attn.shape[1] // CORES
    result = pl.pallas_call(
        functools.partial(early_pieces_kernel, student),
        out_shape=shape((half + EXTRA * student, D)),
        in_specs=[SMEM_SPEC, VMEM_SPEC],
        out_specs=VMEM_SPEC,
        compiler_params=pltpu.CompilerParams(vmem_limit_bytes=12 * 2**20),
        name="early_pieces",
    )(line.ids, attn)
    line.wait(result)
    return result


def late_pieces_kernel(
    n_shard, student, ids_ref, in_ref, down_ref, late_ref
):
    k, j = ids_ref[IK], ids_ref[IJ]
    units = FF // n_shard
    few = units // GROUP
    rows_z = in_ref.shape[0]
    each = rows_z + 2 * few
    number = j * CORES + k
    mine = aligned(number * few, few)
    chosen = choose(units, few, number * few)
    if student:
        full = sign_of(down_ref[mine, :]).astype(bf16)
        late_ref[each:, :] = jnp.zeros((EXTRA, HALF), bf16)
        for part, row in enumerate(split_three(column_total(jnp.abs(down_ref[...])))):
            low = each + 3 + part
            late_ref[low : low + 1, :] = row[:, :HALF]
            late_ref[low + 3 : low + 4, :] = row[:, HALF:]
    else:
        full = down_ref[mine, :]
    late_ref[rows_z : rows_z + few, :] = full[:, :HALF]
    late_ref[rows_z + few : each, :] = full[:, HALF:]
    for place in range(n_shard):
        lanes = slice(place * few, (place + 1) * few)
        full = in_ref[:, place * units : (place + 1) * units]
        if student:
            sums = column_total(jnp.abs(full))
            sums = pick(number, [sums[:, n * few : (n + 1) * few] for n in range(GROUP)])
            for part, row in enumerate(split_three(sums)):
                late_ref[each + part : each + part + 1, lanes] = row
            full = sign_of(full).astype(bf16)
        late_ref[0:rows_z, lanes] = dot(full, chosen).astype(bf16)


def late_pieces(line, n_shard, student, w_in, w_down):
    few = FF // n_shard // GROUP
    rows_z = w_in.shape[0]
    result = pl.pallas_call(
        functools.partial(late_pieces_kernel, n_shard, student),
        out_shape=shape((rows_z + 2 * few + EXTRA * student, HALF)),
        in_specs=[SMEM_SPEC, VMEM_SPEC, VMEM_SPEC],
        out_specs=VMEM_SPEC,
        compiler_params=pltpu.CompilerParams(vmem_limit_bytes=20 * 2**20),
        name="late_pieces",
    )(line.ids, w_in, w_down)
    line.wait(result)
    return result


def scale_row(sums, gain, fan_in):
    return gain * (sums / fan_in) * fan_in ** (-0.5)


def scaled(values, scale):
    return (values.astype(f32) * scale).astype(bf16)


def early_kernel(n_shard, model, ids_ref, *refs):
    group, refs = refs[:n_shard], refs[n_shard:]
    qkv_ref, out_ref = refs[-2:]
    z = ids_ref[IZ]
    half = D // n_shard // CORES
    fold = n_shard // 2
    base = model * fold * half
    if model:
        out_ref[0:base, :] = refs[0][...]
        sums = tree_sum(join_three(ref, half) for ref in group)
        scale = jnp.concatenate(
            [
                scale_row(sums[:, number * COLS : (number + 1) * COLS], attn_gains[number], D)
                for number in range(4)
            ],
            axis=1,
        )
    for mask, ref in enumerate(group):
        place = z ^ mask
        piece = ref[0:half, :]
        if model:
            piece = scaled(piece, scale)
        qkv_ref[aligned(place * half, half), :] = piece[:, :QKV]
        low = pl.ds(pl.multiple_of(base + lax.rem(place, fold) * half, half), half)

        @pl.when(place < fold)
        def _():
            out_ref[low, 0:COLS] = piece[:, QKV:]

        @pl.when(place >= fold)
        def _():
            out_ref[low, COLS:] = piece[:, QKV:]


def out_weight_kernel(n_shard, ids_ref, *refs):
    k, j = ids_ref[IK], ids_ref[IJ]
    t_ref, s_ref = refs[2 * CHIPS :]
    half = D // n_shard // CORES
    span = n_shard * half // 2
    for core in range(CORES):
        for mask in range(CHIPS):
            ref = refs[core * CHIPS + mask]
            for model, goal in enumerate((t_ref, s_ref)):
                for place in range(n_shard):
                    fold = n_shard // 2
                    low = model * span + (place % fold) * half
                    lanes = slice(0, COLS) if place < fold else slice(COLS, 2 * COLS)
                    rows = pl.ds(
                        pl.multiple_of((place * CORES + (k ^ core)) * half, half), half
                    )
                    goal[j ^ mask, rows, :] = ref[low : low + half, lanes]


def merge_kernel(bit, ids_ref, own_ref, got_ref, both_ref):
    size = own_ref.shape[0]
    mine = (ids_ref[IZ] >> bit) & 1
    both_ref[pl.ds(mine * size, size)] = own_ref[...]
    both_ref[pl.ds((1 - mine) * size, size)] = got_ref[...]


def late_kernel(n_shard, student, ids_ref, *refs):
    groups, vec_ref, refs = refs[:4], refs[4], refs[5:]
    in_ref, down_ref, b1_ref = refs
    z, k, j = ids_ref[IZ], ids_ref[IK], ids_ref[IJ]
    units = FF // n_shard
    few = units // GROUP
    rows_z = D // n_shard
    each = rows_z + 2 * few
    fold = n_shard // 2
    side = lax.div(z, fold)

    def mine(ref, row, core, place):
        options = []
        for chip in range(CHIPS):
            start = place * units + (chip * CORES + core) * few
            low, lane = row + start // D, start % D
            options.append(ref[low : low + 1, lane : lane + few])
        return pick(j, options)

    for core in range(CORES):
        for place in range(n_shard):
            goal = slice(core * HALF + place * few, core * HALF + (place + 1) * few)
            b1_ref[0:1, goal] = mine(vec_ref, 8, core, place)
    if student:
        sums = [
            tree_sum(
                join_three(groups[far], each + 3 * part, number)
                for far in range(2)
                for number in range(fold)
            )
            for part in (1, 2)
        ]
        left_scale, right_scale = (scale_row(row, 1.0, FF) for row in sums)
    for core in range(CORES):
        which = k ^ core
        lanes = aligned(which * HALF, HALF)
        if student:
            scale = tree_sum(
                join_three(groups[core * 2 + far], each, number)
                for far in range(2)
                for number in range(fold)
            )
            scale = scale_row(scale, 1.0, D)
        for far in range(2):
            ref = groups[core * 2 + far]
            for number in range(fold):
                place = (side ^ far) * fold + number
                piece = ref[number, 0:rows_z, :]
                left = ref[number, rows_z : rows_z + few, :]
                right = ref[number, rows_z + few : each, :]
                if student:
                    piece = scaled(piece, scale)
                    left = scaled(left, left_scale)
                    right = scaled(right, right_scale)
                in_ref[aligned(place * rows_z, rows_z), lanes] = piece
                rows = pl.ds(pl.multiple_of(which * HALF + place * few, few), few)
                down_ref[rows, 0:HALF] = left
                down_ref[rows, HALF:] = right


def block_place(rest, per, ids_ref, block_ref, far, mask, core, part):
    k, j, r = ids_ref[IK], ids_ref[IJ], ids_ref[IR]
    chip = (r ^ far) * CHIPS + (j ^ mask)
    return block_ref[(chip * CORES + (k ^ core)) * per + part]


def places_kernel(rest, ids_ref, block_ref, lengths_ref, valid_ref, *outs, seqs, rows):
    length = lengths_ref[ids_ref[IZ] * seqs + ids_ref[IK]]
    per = rows // BLK
    number = 0
    for far in range(rest):
        for mask in range(CHIPS):
            for core in range(CORES):
                for part in range(per):
                    goal = slice(number * BLK, (number + 1) * BLK)
                    number += 1
                    if not outs and mask:
                        continue
                    base = block_place(rest, per, ids_ref, block_ref, far, mask, core, part) * BLK
                    col = base + lax.broadcasted_iota(jnp.int32, (BLK, 1), 0)
                    if far == 0 and mask == 0:
                        valid_ref[goal, :] = jnp.where(col < length, 1.0, 0.0)
                    if outs:
                        outs[1][goal, :] = col
                        if far == 0:
                            row = lax.broadcasted_iota(jnp.int32, (1, BLK), 1)
                            outs[0][:, goal] = base + row


def input_kernel(ids_ref, here_ref, x_ref, y_ref, xy0_ref, xy1_ref, own_ref, send_ref):
    k = ids_ref[IK]
    rows = here_ref.shape[1]
    for mask, ref in enumerate((here_ref, x_ref, y_ref)):
        goal = slice(mask * rows, (mask + 1) * rows)
        own_ref[goal, :] = ref[k]
        send_ref[goal, :] = ref[1 - k]
    goal = slice(3 * rows, 4 * rows)

    @pl.when(k == 0)
    def _():
        own_ref[goal, :] = xy0_ref[...]
        send_ref[goal, :] = xy1_ref[...]

    @pl.when(k == 1)
    def _():
        own_ref[goal, :] = xy1_ref[...]
        send_ref[goal, :] = xy0_ref[...]


def qkv_kernel(n_shard, rest, ids_ref, block_ref, own_ref, oth_ref, half_ref, peer_ref, vec_ref, *outs):
    k, j = ids_ref[IK], ids_ref[IJ]
    q_ref, k_ref, v_ref, w_ref = outs
    half = D // n_shard // CORES
    for core, ref in enumerate((half_ref, peer_ref)):
        for place in range(n_shard):
            rows = pl.ds(pl.multiple_of((place * CORES + (k ^ core)) * half, half), half)
            w_ref[rows, :] = ref[place * half : (place + 1) * half, :]
    weight = w_ref[...]
    chips = [slice(chip * COLS, (chip + 1) * COLS) for chip in range(CHIPS)]
    q_bias = pick(j, [vec_ref[0:1, chip] for chip in chips])
    v_bias = pick(j, [vec_ref[1:2, chip] for chip in chips])
    rows = own_ref.shape[0] // CHIPS
    per = rows // BLK
    for core, ref in enumerate((own_ref, oth_ref)):
        full = dot(ref[...], weight)
        for mask in range(CHIPS):
            result = full[mask * rows : (mask + 1) * rows, :]
            goal = slice((mask * CORES + core) * rows, (mask * CORES + core + 1) * rows)
            sets = (
                (q_ref, result[:, :COLS] + q_bias),
                (k_ref, result[:, COLS : 2 * COLS]),
                (v_ref, result[:, 2 * COLS :] + v_bias),
            )
            for goal_ref, values in sets:
                values = values.astype(bf16)
                for head in range(HEADS_HERE):
                    span = slice(head * HEAD_DIM, (head + 1) * HEAD_DIM)
                    if rest > 1:
                        goal_ref[head, goal, :] = values[:, span]
                        continue
                    for part in range(per):
                        place = block_place(rest, per, ids_ref, block_ref, 0, mask, core, part)
                        goal_ref[head, aligned(place * BLK, BLK), :] = values[
                            part * BLK : (part + 1) * BLK, span
                        ]


def attend_kernel(q_ref, k_ref, v_ref, pq_ref, pk_ref, *outs, tile):
    o_refs, lse_ref, all_ref = outs[:CHIPS], outs[CHIPS], outs[CHIPS + 1]
    tokens = q_ref.shape[1]
    own = tokens // CHIPS

    def one_head(head, carry):
        k_head = k_ref[head]
        v_turned = v_ref[head].T
        for t in range(tokens // tile):
            rows = slice(t * tile, (t + 1) * tile)
            scores = dot_right(k_head, q_ref[head, rows, :]) * (score_scale * log2_e)
            allowed = pq_ref[:, rows] >= pk_ref[...]
            scores = jnp.where(allowed, scores, masked_score)
            peak = jnp.max(scores, axis=0, keepdims=True)
            powers = jnp.exp2(scores - peak)
            total = jnp.sum(powers, axis=0, keepdims=True)
            mixed = dot(v_turned, powers.astype(bf16)) / total
            all_ref[head, rows, :] = mixed.T.astype(bf16)
            lse_ref[head, :, rows] = peak + jnp.log2(total)
        return carry

    lax.fori_loop(0, HEADS_HERE, one_head, 0)
    for head in range(HEADS_HERE):
        span = slice(head * HEAD_DIM, (head + 1) * HEAD_DIM)
        for mask in range(CHIPS):
            o_refs[mask][:, span] = all_ref[head, mask * own : (mask + 1) * own, :]


def sorted_blocks(ids_ref, block_ref, rows):
    per = rows // BLK
    for mask in range(CHIPS):
        for core in range(CORES):
            for part in range(per):
                place = block_place(1, per, ids_ref, block_ref, 0, mask, core, part)
                yield mask, core * rows + part * BLK, aligned(place * BLK, BLK)


def below_diagonal(tile):
    key = lax.broadcasted_iota(jnp.int32, (tile, tile), 0)
    query = lax.broadcasted_iota(jnp.int32, (tile, tile), 1)
    return key <= query


def causal_kernel(ids_ref, block_ref, q_ref, k_ref, v_ref, *outs, tile):
    o_refs, lse_ref, all_ref = outs[:CHIPS], outs[CHIPS], outs[CHIPS + 1]
    tokens = q_ref.shape[1]
    rows = tokens // GROUP
    allowed = below_diagonal(tile)

    def one_head(head, carry):
        v_turned = v_ref[head].T
        for t in range(tokens // tile):
            here = slice(t * tile, (t + 1) * tile)
            q_tile = q_ref[head, here, :]
            scores = dot_right(k_ref[head, here, :], q_tile) * (score_scale * log2_e)
            scores = jnp.where(allowed, scores, masked_score)
            peak = jnp.max(scores, axis=0, keepdims=True)
            if t:
                before = slice(0, t * tile)
                earlier = dot_right(k_ref[head, before, :], q_tile) * (score_scale * log2_e)
                peak = jnp.maximum(peak, jnp.max(earlier, axis=0, keepdims=True))
            powers = jnp.exp2(scores - peak)
            total = jnp.sum(powers, axis=0, keepdims=True)
            mixed = dot(v_turned[:, here], powers.astype(bf16))
            if t:
                powers = jnp.exp2(earlier - peak)
                total = total + jnp.sum(powers, axis=0, keepdims=True)
                mixed = mixed + dot(v_turned[:, before], powers.astype(bf16))
            all_ref[head, here, :] = (mixed / total).T.astype(bf16)
            lse_ref[head, :, here] = peak + jnp.log2(total)
        return carry

    lax.fori_loop(0, HEADS_HERE, one_head, 0)
    for head in range(HEADS_HERE):
        span = slice(head * HEAD_DIM, (head + 1) * HEAD_DIM)
        for mask, low, place in sorted_blocks(ids_ref, block_ref, rows):
            o_refs[mask][low : low + BLK, span] = all_ref[head, place, :]


def norm_parts(values):
    middle = jnp.mean(values, axis=-1, keepdims=True)
    centred = values - middle
    spread = jnp.mean(centred * centred, axis=-1, keepdims=True)
    inverse = lax.rsqrt(spread + norm_eps)
    return centred * inverse, inverse


def norm_back(values, gain, grad_out):
    normal, inverse = norm_parts(values)
    scaled = grad_out * gain
    grad_in = (
        scaled
        - jnp.mean(scaled, axis=-1, keepdims=True)
        - normal * jnp.mean(scaled * normal, axis=-1, keepdims=True)
    ) * inverse
    return grad_in, normal


def column_total(values):
    return jnp.sum(values, axis=0, keepdims=True)


def branch_kernel(student, ids_ref, *refs):
    j = ids_ref[IJ]
    h_refs, (w_ref, own_ref, oth_ref, vec_ref, valid_ref) = refs[:CHIPS], refs[CHIPS : CHIPS + 5]
    outs = refs[CHIPS + 5 :]
    first_ref, sent_ref = outs[:2]
    rows = own_ref.shape[0] // CHIPS
    if student:
        residual_ref, sums_ref = outs[2:]
        sums_ref[...] = jnp.zeros_like(sums_ref)
    for core, x_ref in enumerate((own_ref, oth_ref)):
        goal = slice(core * rows, (core + 1) * rows)
        parts = []
        for chip in range(CHIPS):
            parts.append(
                tree_sum(
                    dot(
                        h_refs[mask][goal, :],
                        w_ref[chip, aligned((j ^ mask) * COLS, COLS), :],
                    )
                    for mask in range(CHIPS)
                )
            )
        branch = jnp.concatenate(parts, axis=1) + vec_ref[2:3, :]
        residual = x_ref[0:rows, :].astype(f32) + branch
        normal, _ = norm_parts(residual)
        first = normal * vec_ref[4:5, :] + vec_ref[5:6, :]
        first_ref[goal, :] = first
        sent_ref[goal, :] = first.astype(bf16)
        if student:
            residual_ref[goal, :] = residual
            sums_ref[0:1, :] += column_total(valid_ref[goal, :] * branch * branch)


def whole(refs):
    if len(refs) == 1:
        return refs[0][...]
    return jnp.concatenate([ref[...] for ref in refs])


def feed_kernel(student, count, *refs):
    pieces, (in_ref, down_ref, b1_ref, part_ref, *outs) = refs[:count], refs[count:]
    inner = dot(whole(pieces), in_ref[...]) + b1_ref[0:1, :]
    act = (inner * normal_cdf(inner)).astype(bf16)
    if student:
        outs[0][...] = inner
        outs[1][...] = act
    part_ref[...] = dot(act, down_ref[...]).astype(part_ref.dtype)


def target_kernel(*refs):
    parts, (first_ref, vec_ref, target_ref) = refs[:CHIPS], refs[CHIPS:]
    feed = tree_sum(ref[...].astype(f32) for ref in parts) + vec_ref[3:4, :]
    normal, _ = norm_parts(first_ref[...] + feed)
    target_ref[...] = normal * vec_ref[6:7, :] + vec_ref[7:8, :]


def loss_kernel(ids_ref, lengths_ref, *refs):
    parts, rest = refs[:CHIPS], refs[CHIPS:]
    first_ref, vec_ref, target_ref, valid_ref, out_ref, grad_ref, sent_ref, sums_ref = rest
    count = lengths_ref[0]
    for number in range(1, lengths_ref.shape[0]):
        count = count + lengths_ref[number]
    share = 1.0 / (count.astype(f32) * D)
    feed = tree_sum(ref[...].astype(f32) for ref in parts) + vec_ref[3:4, :]
    second = first_ref[...] + feed
    normal, inverse = norm_parts(second)
    out = normal * vec_ref[6:7, :] + vec_ref[7:8, :]
    out_ref[...] = out.astype(bf16)
    valid = valid_ref[...]
    mismatch = valid * (out - target_ref[...])
    grad_out = mismatch * share
    scaled = grad_out * vec_ref[6:7, :]
    grad = (
        scaled
        - jnp.mean(scaled, axis=-1, keepdims=True)
        - normal * jnp.mean(scaled * normal, axis=-1, keepdims=True)
    ) * inverse
    grad_ref[...] = grad
    sent_ref[...] = grad.astype(bf16)
    sums_ref[...] = jnp.concatenate(
        [
            column_total(grad),
            column_total(grad_out * normal),
            column_total(grad_out),
            0.5 * column_total(mismatch * mismatch),
            column_total(valid * feed * feed),
            column_total(valid * second * second),
            jnp.zeros((2, D), f32),
        ]
    )


def feed_back_kernel(count, *refs):
    pieces, refs = refs[:count], refs[count:]
    inner_ref, in_ref, down_ref, part_ref, grad_ref, sum_ref = refs
    inner = inner_ref[...]
    slope = normal_cdf(inner) + inner * jnp.exp(-0.5 * inner * inner) * 0.3989422804014327
    grad = dot_right(whole(pieces), down_ref[...]) * slope
    sum_ref[...] = jnp.broadcast_to(column_total(grad), sum_ref.shape)
    grad = grad.astype(bf16)
    grad_ref[...] = grad
    part_ref[...] = dot_right(grad, in_ref[...]).astype(part_ref.dtype)


def branch_back_kernel(ids_ref, *refs):
    j = ids_ref[IJ]
    parts, rest = refs[:CHIPS], refs[CHIPS:]
    second_ref, residual_ref, vec_ref, w_ref = rest[:4]
    grad_ref, sent_ref = rest[4:6]
    h_refs, (sums_ref,) = rest[6 : 6 + CHIPS], rest[6 + CHIPS :]
    grad_first = second_ref[...] + tree_sum(ref[...].astype(f32) for ref in parts)
    grad, normal = norm_back(residual_ref[...], vec_ref[4:5, :], grad_first)
    grad_ref[...] = grad
    sums_ref[...] = jnp.concatenate(
        [
            column_total(grad),
            column_total(grad_first * normal),
            column_total(grad_first),
            jnp.zeros((5, D), f32),
        ]
    )
    grad = grad.astype(bf16)
    sent_ref[...] = grad
    chips = [grad[:, chip * COLS : (chip + 1) * COLS] for chip in range(CHIPS)]
    for mask in range(CHIPS):
        rows = aligned((j ^ mask) * COLS, COLS)
        h_refs[mask][...] = tree_sum(
            dot_right(chips[chip], w_ref[chip, rows, :]) for chip in range(CHIPS)
        ).astype(bf16)


def attend_back_kernel(*refs, tile):
    q_ref, k_ref, v_ref = refs[:3]
    g_refs, refs = refs[3 : 3 + CHIPS], refs[3 + CHIPS :]
    lse_ref, pq_ref, pk_ref, gq_ref, gk_ref, gv_ref, sums_ref = refs[:7]
    g_all, aq_ref, ak_ref, av_ref = refs[7:]
    tokens = q_ref.shape[1]
    own = tokens // CHIPS
    for head in range(HEADS_HERE):
        span = slice(head * HEAD_DIM, (head + 1) * HEAD_DIM)
        for mask in range(CHIPS):
            g_all[head, mask * own : (mask + 1) * own, :] = g_refs[mask][:, span]

    def one_head(head, carry):
        k_head = k_ref[head]
        v_head = v_ref[head]
        k_turned = k_head.T
        for t in range(tokens // tile):
            rows = slice(t * tile, (t + 1) * tile)
            q_tile = q_ref[head, rows, :]
            g_tile = g_all[head, rows, :]
            scores = dot_right(k_head, q_tile) * (score_scale * log2_e)
            allowed = pq_ref[:, rows] >= pk_ref[...]
            scores = jnp.where(allowed, scores, masked_score)
            probs = jnp.exp2(scores - lse_ref[head, :, rows])
            grad_probs = dot_right(v_head, g_tile)
            delta = jnp.sum(probs * grad_probs, axis=0, keepdims=True)
            grad_scores = (probs * (grad_probs - delta)).astype(bf16)
            aq_ref[head, rows, :] = dot(k_turned, grad_scores).T * score_scale
            if t == 0:
                ak_ref[head] = dot(grad_scores, q_tile)
                av_ref[head] = dot(probs.astype(bf16), g_tile)
            else:
                ak_ref[head] += dot(grad_scores, q_tile)
                av_ref[head] += dot(probs.astype(bf16), g_tile)
        return carry

    lax.fori_loop(0, HEADS_HERE, one_head, 0)
    sums_ref[...] = jnp.zeros_like(sums_ref)
    for head in range(HEADS_HERE):
        span = slice(head * HEAD_DIM, (head + 1) * HEAD_DIM)
        grad_query = aq_ref[head]
        grad_value = av_ref[head]
        gq_ref[:, span] = grad_query.astype(bf16)
        gk_ref[:, span] = (ak_ref[head] * score_scale).astype(gk_ref.dtype)
        gv_ref[:, span] = grad_value.astype(gv_ref.dtype)
        sums_ref[0:1, span] = column_total(grad_query)
        sums_ref[1:2, span] = column_total(grad_value)


def causal_back_kernel(ids_ref, block_ref, *refs, tile):
    q_ref, k_ref, v_ref = refs[:3]
    g_refs, refs = refs[3 : 3 + CHIPS], refs[3 + CHIPS :]
    lse_ref, gq_ref, gk_ref, gv_ref, sums_ref, g_all, aq_ref, ak_ref, av_ref = refs
    tokens = q_ref.shape[1]
    rows = tokens // GROUP
    own = tokens // CHIPS
    allowed = below_diagonal(tile)
    for head in range(HEADS_HERE):
        span = slice(head * HEAD_DIM, (head + 1) * HEAD_DIM)
        for mask, low, place in sorted_blocks(ids_ref, block_ref, rows):
            g_all[head, place, :] = g_refs[mask][low : low + BLK, span]

    def one_head(head, carry):
        k_turned = k_ref[head].T
        for t in range(tokens // tile):
            here = slice(t * tile, (t + 1) * tile)
            q_tile = q_ref[head, here, :]
            g_tile = g_all[head, here, :]
            lse = lse_ref[head, :, here]
            scores = dot_right(k_ref[head, here, :], q_tile) * (score_scale * log2_e)
            probs = jnp.exp2(jnp.where(allowed, scores, masked_score) - lse)
            grads = dot_right(v_ref[head, here, :], g_tile)
            delta = jnp.sum(probs * grads, axis=0, keepdims=True)
            if t:
                before = slice(0, t * tile)
                earlier = dot_right(k_ref[head, before, :], q_tile) * (score_scale * log2_e)
                early_probs = jnp.exp2(earlier - lse)
                early_grads = dot_right(v_ref[head, before, :], g_tile)
                delta = delta + jnp.sum(early_probs * early_grads, axis=0, keepdims=True)
            grad_scores = (probs * (grads - delta)).astype(bf16)
            grad_query = dot(k_turned[:, here], grad_scores)
            ak_ref[head, here, :] = dot(grad_scores, q_tile)
            av_ref[head, here, :] = dot(probs.astype(bf16), g_tile)
            if t:
                grad_scores = (early_probs * (early_grads - delta)).astype(bf16)
                grad_query = grad_query + dot(k_turned[:, before], grad_scores)
                ak_ref[head, before, :] += dot(grad_scores, q_tile)
                av_ref[head, before, :] += dot(early_probs.astype(bf16), g_tile)
            aq_ref[head, here, :] = grad_query.T * score_scale
        return carry

    lax.fori_loop(0, HEADS_HERE, one_head, 0)
    sums_ref[...] = jnp.zeros_like(sums_ref)
    for head in range(HEADS_HERE):
        span = slice(head * HEAD_DIM, (head + 1) * HEAD_DIM)
        sums_ref[0:1, span] = column_total(aq_ref[head])
        sums_ref[1:2, span] = column_total(av_ref[head])
        for mask, low, place in sorted_blocks(ids_ref, block_ref, rows):
            goal = slice(mask * own + low, mask * own + low + BLK)
            gq_ref[goal, span] = aq_ref[head, place, :].astype(bf16)
            gk_ref[goal, span] = (ak_ref[head, place, :] * score_scale).astype(bf16)
            gv_ref[goal, span] = av_ref[head, place, :].astype(bf16)


def qkv_back_kernel(gq_ref, gk_ref, gv_ref, w_ref, *part_refs):
    own = gq_ref.shape[0] // CHIPS
    for mask in range(CHIPS):
        rows = slice(mask * own, (mask + 1) * own)
        part_refs[mask][...] = (
            dot_right(gq_ref[rows, :], w_ref[:, :COLS])
            + dot_right(gk_ref[rows, :], w_ref[:, COLS : 2 * COLS])
            + dot_right(gv_ref[rows, :], w_ref[:, 2 * COLS :])
        ).astype(part_refs[mask].dtype)


def hidden_kernel(res_ref, *refs):
    parts, (own_ref, send_ref) = refs[:CHIPS], refs[CHIPS:]
    total = res_ref[...] + tree_sum(ref[...].astype(f32) for ref in parts)
    rows = own_ref.shape[0]
    own_ref[...] = total[:rows, :]
    send_ref[...] = total[rows:, :]


def late_grad_kernel(n_shard, counts, ids_ref, *refs):
    k = ids_ref[IK]
    groups = []
    for count in counts:
        groups.append(refs[:count])
        refs = refs[count:]
    acts, feeds, firsts, inners = (groups[i * CHIPS : (i + 1) * CHIPS] for i in range(4))
    own_ref, send_ref, down_ref, in_ref = refs
    down_ref[...] = tree_sum(dot_left(whole(a), whole(g)) for a, g in zip(acts, feeds))
    in_ref[...] = tree_sum(dot_left(whole(a), whole(g)) for a, g in zip(firsts, inners))
    few = FF // n_shard // GROUP
    rows_z = D // n_shard
    each = rows_z + 2 * few
    for goal_ref, half in ((own_ref, k), (send_ref, 1 - k)):
        kind = goal_ref.dtype
        lanes = aligned(half * HALF, HALF)
        for place in range(n_shard):
            goal_ref[place, 0:rows_z, :] = in_ref[
                place * rows_z : (place + 1) * rows_z, lanes
            ].astype(kind)
            rows = pl.ds(pl.multiple_of(half * HALF + place * few, few), few)
            goal_ref[place, rows_z : rows_z + few, :] = down_ref[rows, :HALF].astype(kind)
            goal_ref[place, rows_z + few : each, :] = down_ref[rows, HALF:].astype(kind)


def late_split_kernel(n_shard, ids_ref, own_ref, got_ref, *outs):
    for mask in range(n_shard):
        place = ids_ref[IZ] ^ mask
        outs[mask][...] = (own_ref[place] + got_ref[place].astype(f32)).astype(outs[mask].dtype)


def sum_kernel(*refs):
    refs[-1][...] = tree_sum(ref[...].astype(f32) for ref in refs[:-1]).astype(bf16)


def late_final_kernel(n_shard, ids_ref, *refs):
    k, j = ids_ref[IK], ids_ref[IJ]
    pieces, (in_latent_ref, down_latent_ref, in_ref, down_ref, all_ref) = refs[:GROUP], refs[GROUP:]
    few = FF // n_shard // GROUP
    rows_z = D // n_shard
    for core in range(CORES):
        for mask in range(CHIPS):
            all_ref[(j ^ mask) * CORES + (k ^ core)] = pieces[core * CHIPS + mask][...]
    for number in range(GROUP):
        for place in range(n_shard):
            goal = (place * GROUP + number) * few
            lanes = slice(goal, goal + few)
            grad = all_ref[number, 0:rows_z, place * few : (place + 1) * few].astype(f32)
            keep = jnp.abs(in_latent_ref[:, lanes]) <= 1.0
            in_ref[:, lanes] = jnp.where(keep, grad, 0.0)
        rows = slice(number * few, (number + 1) * few)
        for part in range(2):
            lanes = slice(part * HALF, (part + 1) * HALF)
            low = rows_z + part * few
            grad = all_ref[number, low : low + few, :].astype(f32)
            keep = jnp.abs(down_latent_ref[rows, lanes]) <= 1.0
            down_ref[rows, lanes] = jnp.where(keep, grad, 0.0)


def out_grad_kernel(n_shard, ids_ref, *refs):
    j = ids_ref[IJ]
    h_refs, grad_ref = refs[:CHIPS], refs[CHIPS]
    outs, (cols_ref, full_ref) = refs[CHIPS + 1 : CHIPS + 1 + CHIPS], refs[CHIPS + 1 + CHIPS :]
    half = D // n_shard // CORES
    for chip in range(CHIPS):
        cols_ref[chip] = grad_ref[:, chip * COLS : (chip + 1) * COLS]
    for goal in range(CHIPS):
        cols = cols_ref[j ^ goal]
        for mask in range(CHIPS):
            full_ref[aligned((j ^ mask) * COLS, COLS), :] = dot_left(h_refs[mask][...], cols)
        for core in range(CORES):
            for place in range(n_shard):
                low = (place * CORES + core) * half
                outs[goal][place * half : (place + 1) * half, core * COLS : (core + 1) * COLS] = (
                    full_ref[low : low + half, :].astype(outs[goal].dtype)
                )


def split_hi_lo(values):
    high = values.astype(bf16)
    low = (values - high.astype(f32)).astype(bf16)
    return high, low


def early_grad_kernel(n_shard, ids_ref, *refs):
    k = ids_ref[IK]
    own_x, oth_x, gq_ref, gk_ref, gv_ref = refs[:5]
    outs, refs = refs[5 : 5 + CHIPS], refs[5 + CHIPS :]
    branch_sums, loss_sums, res_sums = refs[:3]
    b1_sums, refs = refs[3 : 3 + CHIPS], refs[3 + CHIPS :]
    qv_sums, own_ref, vec_ref, send_ref, full_ref = refs
    half = D // n_shard // CORES
    rows = own_x.shape[0] // CHIPS
    for number, g_ref in enumerate((gq_ref, gk_ref, gv_ref)):
        parts = []
        for core, x_ref in enumerate((own_x, oth_x)):
            for mask in range(CHIPS):
                goal = slice((mask * CORES + core) * rows, (mask * CORES + core + 1) * rows)
                parts.append(dot_left(x_ref[mask * rows : (mask + 1) * rows, :], g_ref[goal, :]))
        full_ref[:, number * COLS : (number + 1) * COLS] = tree_sum(parts)
    total = tree_sum(ref[...].astype(f32) for ref in outs)
    for place in range(n_shard):
        for core in range(CORES):
            low = (place * CORES + core) * half
            full_ref[low : low + half, QKV:] = total[
                place * half : (place + 1) * half, core * COLS : (core + 1) * COLS
            ]
    for place in range(n_shard):
        goal = slice(place * half, (place + 1) * half)
        mine = pl.ds(pl.multiple_of((place * CORES + k) * half, half), half)
        theirs = pl.ds(pl.multiple_of((place * CORES + 1 - k) * half, half), half)
        own_ref[goal, :] = full_ref[mine, :]
        send_ref[goal, :] = full_ref[theirs, :].astype(bf16)
    lane = lax.broadcasted_iota(jnp.int32, (1, 2 * COLS), 1)
    stats = jnp.zeros((1, 2 * COLS), f32)
    for number, row in enumerate(
        (loss_sums[3:4, :], branch_sums[0:1, :], loss_sums[4:5, :], loss_sums[5:6, :])
    ):
        stats = stats + jnp.where(lane == number, jnp.sum(row, axis=1, keepdims=True), 0.0)
    table = jnp.concatenate(
        [
            res_sums[0:1, :],
            loss_sums[0:1, :],
            res_sums[1:3, :],
            loss_sums[1:3, :],
            tree_sum(ref[0:1, :] for ref in b1_sums),
            jnp.concatenate([qv_sums[0:1, :], qv_sums[1:2, :], stats], axis=1),
        ]
    )
    high, low = split_hi_lo(table)
    base = n_shard * half
    send_ref[base : base + VEC_ROWS, :] = high
    send_ref[base + VEC_ROWS : base + 2 * VEC_ROWS, :] = low
    vec_ref[...] = high.astype(f32) + low.astype(f32)


def early_split_kernel(n_shard, ids_ref, own_ref, vec_ref, got_ref, *outs):
    z = ids_ref[IZ]
    half = D // n_shard // CORES
    base = n_shard * half
    table = vec_ref[...] + (
        got_ref[base : base + VEC_ROWS, :].astype(f32)
        + got_ref[base + VEC_ROWS : base + 2 * VEC_ROWS, :].astype(f32)
    )
    high, low = split_hi_lo(table)
    for mask in range(n_shard):
        rows = aligned((z ^ mask) * half, half)
        kind = outs[mask].dtype
        outs[mask][0:half, :] = (own_ref[rows, :] + got_ref[rows, :].astype(f32)).astype(kind)
        outs[mask][half : half + VEC_ROWS, :] = high.astype(kind)
        outs[mask][half + VEC_ROWS : half + 2 * VEC_ROWS, :] = low.astype(kind)


def early_sum_kernel(*refs):
    ins, out_ref = refs[:-1], refs[-1]
    half = out_ref.shape[0] - 2 * VEC_ROWS
    out_ref[0:half, :] = tree_sum(ref[0:half, :].astype(f32) for ref in ins).astype(bf16)
    table = tree_sum(
        ref[half : half + VEC_ROWS, :].astype(f32)
        + ref[half + VEC_ROWS : half + 2 * VEC_ROWS, :].astype(f32)
        for ref in ins
    )
    high, low = split_hi_lo(table)
    out_ref[half : half + VEC_ROWS, :] = high
    out_ref[half + VEC_ROWS : half + 2 * VEC_ROWS, :] = low


def early_final_kernel(n_shard, ids_ref, lengths_ref, *refs):
    k, j = ids_ref[IK], ids_ref[IJ]
    pieces = refs[:GROUP]
    latent_ref, attn_ref, vec_ref, query_ref, stats_ref, all_ref, rows_ref, flat_ref = refs[GROUP:]
    half = D // n_shard // CORES
    few = FF // n_shard // GROUP
    units = FF // n_shard
    for core in range(CORES):
        for mask in range(CHIPS):
            ref = pieces[core * CHIPS + mask]
            all_ref[(j ^ mask) * CORES + (k ^ core)] = ref[0:half, :]
    for chip in range(CHIPS):
        for core in range(CORES):
            for number in range(4):
                lanes = slice(chip * COLS, (chip + 1) * COLS)
                rows = slice(core * half, (core + 1) * half)
                grad = all_ref[
                    chip * CORES + core, :, number * COLS : (number + 1) * COLS
                ].astype(f32)
                keep = jnp.abs(latent_ref[number, rows, lanes]) <= 1.0
                attn_ref[number, rows, lanes] = jnp.where(keep, grad, 0.0)
    tables = [
        pieces[mask][half : half + VEC_ROWS, :].astype(f32)
        + pieces[mask][half + VEC_ROWS : half + 2 * VEC_ROWS, :].astype(f32)
        for mask in range(CHIPS)
    ]
    total = tree_sum(tables)
    for mask in range(CHIPS):
        rows_ref[j ^ mask] = tables[mask]
    count = lengths_ref[0]
    for number in range(1, lengths_ref.shape[0]):
        count = count + lengths_ref[number]
    scale = count.astype(f32) * D
    stats = total[ROW_QV : ROW_QV + 1, 2 * COLS : 2 * COLS + 128] / scale
    lane = lax.broadcasted_iota(jnp.int32, (1, 128), 1)
    stats_ref[...] = jnp.where(lane == 0, stats, jnp.sqrt(stats))
    vec_ref[1:7, :] = total[0:6, :]
    for chip in range(CHIPS):
        lanes = slice(chip * COLS, (chip + 1) * COLS)
        query_ref[:, lanes] = rows_ref[chip, ROW_QV : ROW_QV + 1, 0:COLS]
        vec_ref[0:1, lanes] = rows_ref[chip, ROW_QV : ROW_QV + 1, COLS : 2 * COLS]
        for core in range(CORES):
            for place in range(n_shard):
                start = place * units + (chip * CORES + core) * few
                row, lane = 7 + start // D, start % D
                vec_ref[row : row + 1, lane : lane + few] = rows_ref[
                    chip, ROW_B1 : ROW_B1 + 1, core * HALF + place * few : core * HALF + (place + 1) * few
                ]


def owners_kernel(ids_ref, here_ref, there_ref, out_ref):
    k = ids_ref[IK]
    out_ref[k] = here_ref[...]
    out_ref[1 - k] = there_ref[...]


def body(
    hidden_in,
    block_of,
    lengths,
    attn_latent,
    ffn_in_latent,
    ffn_out_latent,
    student_vec,
    teacher_attn,
    teacher_ffn_in,
    teacher_ffn_out,
    teacher_vec,
):
    seqs, rows, _ = hidden_in.shape
    rest = lax.axis_size("rest")
    n_shard = lax.axis_size("shard")
    own = seqs * rows
    tokens = CHIPS * own
    keys = rest * tokens
    ids = jnp.stack([lax.axis_index(name) for name in ("shard", "core", "chip", "rest")])
    half = D // n_shard // CORES
    few = FF // n_shard // GROUP
    rows_z = D // n_shard
    each = rows_z + 2 * few
    line = Line(ids.astype(jnp.int32))

    def flip(piece, axis, mask):
        size = lax.axis_size(axis)
        return lax.ppermute(piece, axis, [(a, a ^ mask) for a in range(size)])

    def gather(piece, axis):
        return [piece] + [flip(piece, axis, m) for m in range(1, lax.axis_size(axis))]

    def exchange(pieces, axis):
        return [pieces[0]] + [flip(pieces[m], axis, m) for m in range(1, len(pieces))]

    def swap(piece):
        return flip(piece, "core", 1)

    def near_rows(piece):
        return [piece, flip(piece, "chip", 1), flip(piece, "chip", 2)]

    def all_rows(near):
        near = [near[0], *line.behind(*near[1:])]
        half = near[0].shape[0] // 2
        far = (flip(near[2][:half], "chip", 1), flip(near[1][half:], "chip", 2))
        return [(near[0],), (near[1],), (near[2],), far]

    def spread_z(piece):
        bits = n_shard.bit_length() - 1
        own = piece[None]
        for bit in range(bits):
            got = flip(own, "shard", 1 << bit)
            if bit == bits - 1:
                return own, got
            own = line(
                functools.partial(merge_kernel, bit),
                "merge",
                shape((2 * own.shape[0], *own.shape[1:])),
                (),
                (own, got),
                limit=6,
            )

    near = near_rows(hidden_in)
    t_early = early_pieces(line, False, teacher_attn)
    s_early = early_pieces(line, True, attn_latent)
    outs = [shape((own, 1), f32)]
    if rest > 1:
        outs += [shape((1, tokens), jnp.int32), shape((keys, 1), jnp.int32)]
    valid, *positions = line(
        functools.partial(places_kernel, rest, seqs=seqs, rows=rows),
        "places",
        tuple(outs),
        (block_of, lengths),
        (),
    )
    t_qkv_half, t_out_half = line(
        functools.partial(early_kernel, n_shard, 0),
        "early_weights",
        (shape((n_shard * half, QKV)), shape((n_shard * half // 2, 2 * COLS))),
        (),
        gather(t_early, "shard"),
    )
    pieces = [piece for group in all_rows(near) for piece in group]
    t_late = late_pieces(line, n_shard, False, teacher_ffn_in, teacher_ffn_out)
    s_late = late_pieces(line, n_shard, True, ffn_in_latent, ffn_out_latent)
    pieces = pieces[:3] + [piece[0] for piece in pieces[3:]]
    x_own, x_send = line(
        input_kernel,
        "input",
        (shape((tokens // CORES, D)), shape((tokens // CORES, D))),
        (),
        pieces,
    )
    x_oth = swap(x_send)
    def rest_gather(values):
        if rest == 1:
            return values
        return jnp.concatenate(gather(values, "rest"), axis=1)

    def rest_scatter(partial):
        if rest == 1:
            return partial
        view = partial.reshape(rest, tokens, COLS)
        return tree_sum(
            [view[0]]
            + [flip(view[m].astype(bf16), "rest", m).astype(f32) for m in range(1, rest)]
        ).astype(bf16)

    def project(qkv_half, vector):
        heads = shape((HEADS_HERE, tokens, HEAD_DIM))
        query, key, value, w_qkv = line(
            functools.partial(qkv_kernel, n_shard, rest),
            "qkv",
            (heads, heads, heads, shape((D, QKV))),
            (block_of,),
            [x_own, x_oth, qkv_half, swap(qkv_half), vector],
        )
        return query, rest_gather(key), rest_gather(value), w_qkv

    def attend(query, key, value):
        outs = tuple([shape((own, COLS))] * CHIPS + [shape((HEADS_HERE, 1, tokens), f32)])
        scratch = (pltpu.VMEM((HEADS_HERE, tokens, HEAD_DIM), bf16),)
        if rest == 1:
            *heads, lse = line(
                functools.partial(causal_kernel, tile=own),
                "attend",
                outs,
                (block_of,),
                (query, key, value),
                scratch,
            )
        else:
            *heads, lse = line(
                functools.partial(attend_kernel, tile=own),
                "attend",
                outs,
                (),
                (query, key, value, *positions),
                scratch,
                limit=48,
                bare=True,
            )
        return exchange(heads, "chip"), lse

    def branch(student, heads, w_out, vector):
        outs = [shape((own, D), f32), shape((own, D))]
        if student:
            outs += [shape((own, D), f32), shape((8, D), f32)]
        return line(
            functools.partial(branch_kernel, student),
            "branch",
            tuple(outs),
            (),
            (*heads, w_out, x_own, x_oth, vector, valid),
        )

    def late_weights(student, near_far, vector):
        return line(
            functools.partial(late_kernel, n_shard, student),
            "late_weights",
            (shape((D, UNITS)), shape((UNITS, D)), shape((8, UNITS), f32)),
            (),
            [*near_far, *[swap(piece) for piece in near_far], vector],
        )

    def feed(student, pieces, mask, late):
        outs = [shape((own, D), f32 if mask == 0 else bf16)]
        if student:
            outs += [shape((own, UNITS), f32), shape((own, UNITS))]
        return line(
            functools.partial(feed_kernel, student, len(pieces)),
            "feed",
            tuple(outs),
            (),
            (*pieces, *late),
            bare=True,
        )

    t_query, t_key, t_value, _ = project(t_qkv_half, teacher_vec)
    (s_late,) = line.behind(s_late)
    s_qkv_half, out_half = line(
        functools.partial(early_kernel, n_shard, 1),
        "early_weights",
        (shape((n_shard * half, QKV)), shape((n_shard * half, 2 * COLS))),
        (),
        gather(s_early, "shard") + [t_out_half],
    )
    t_late = spread_z(t_late)
    t_heads, _ = attend(t_query, t_key, t_value)
    out_all = gather(out_half, "chip")
    query, key, value, w_qkv = project(s_qkv_half, student_vec)
    s_late = spread_z(s_late)
    t_out, s_out = line(
        functools.partial(out_weight_kernel, n_shard),
        "out_weights",
        (shape((CHIPS, D, COLS)), shape((CHIPS, D, COLS))),
        (),
        out_all + [swap(piece) for piece in out_all],
    )
    t_first, t_sent = branch(False, t_heads, t_out, teacher_vec)
    t_near = near_rows(t_sent)
    t_late = line.behind(*t_late)
    heads, lse = attend(query, key, value)
    t_late = late_weights(False, t_late, teacher_vec)
    t_parts = [feed(False, (t_sent,), 0, t_late)[0]]
    t_firsts = all_rows(t_near)
    first, sent, residual, branch_sums = branch(True, heads, s_out, student_vec)
    near = near_rows(sent)
    for m in (1, 2):
        t_parts.append(feed(False, t_firsts[m], m, t_late)[0])
    s_late = late_weights(True, line.behind(*s_late), student_vec)
    w_in, w_down, _ = s_late
    fed = [feed(True, (sent,), 0, s_late)]
    firsts = all_rows(near)
    t_parts.append(feed(False, t_firsts[3], 3, t_late)[0])
    t_parts = exchange(t_parts, "chip")
    fed += [feed(True, firsts[m], m, s_late) for m in range(1, CHIPS)]
    parts, inners, acts = ([f[i] for f in fed] for i in range(3))
    target = line(
        target_kernel,
        "target",
        shape((own, D), f32),
        (),
        (*t_parts, t_first, teacher_vec),
        bare=True,
    )
    out, grad_second, sent, loss_sums = line(
        loss_kernel,
        "loss",
        (shape((own, D)), shape((own, D), f32), shape((own, D)), shape((8, D), f32)),
        (lengths,),
        (*exchange(parts, "chip"), first, student_vec, target, valid),
    )

    near = near_rows(sent)

    def to_owners(here, there):
        return line(
            owners_kernel,
            "owners",
            shape((CORES, *here.shape), here.dtype),
            (),
            (here, swap(there)),
        )

    def feed_back(pieces, m):
        return line(
            functools.partial(feed_back_kernel, len(pieces)),
            "feed_back",
            (
                shape((own, D), f32 if m == 0 else bf16),
                shape((own, UNITS)),
                shape((8, UNITS), f32),
            ),
            (),
            (*pieces, inners[m], w_in, w_down),
            bare=True,
        )

    backs = [feed_back((sent,), 0)]
    feeds = all_rows(near)
    backs += [feed_back(feeds[m], m) for m in range(1, CHIPS)]
    output = to_owners(out[:rows], out[rows:])
    parts, grad_inners, b1_sums = ([b[i] for b in backs] for i in range(3))
    groups = [(act,) for act in acts] + feeds + firsts + [(inner,) for inner in grad_inners]
    keep, send = line(
        functools.partial(late_grad_kernel, n_shard, [len(group) for group in groups]),
        "late_grad",
        (shape((n_shard, each, HALF), f32), shape((n_shard, each, HALF))),
        (),
        [piece for group in groups for piece in group],
        (pltpu.VMEM((UNITS, D), f32), pltpu.VMEM((D, UNITS), f32)),
        limit=24,
    )
    grad_res, grad_branch, *rest_outs = line(
        branch_back_kernel,
        "branch_back",
        tuple(
            [shape((own, D), f32), shape((own, D))]
            + [shape((own, COLS))] * CHIPS
            + [shape((8, D), f32)]
        ),
        (),
        (*exchange(parts, "chip"), grad_second, residual, student_vec, s_out),
    )
    grad_heads, res_sums = exchange(rest_outs[:CHIPS], "chip"), rest_outs[CHIPS]
    late_pieces_out = line(
        functools.partial(late_split_kernel, n_shard),
        "late_split",
        tuple(shape((each, HALF), f32 if m == 0 else bf16) for m in range(n_shard)),
        (),
        (keep, swap(*line.behind(send))),
    )
    late_got = [late_pieces_out[0]]

    def late_exchange(*masks):
        for m in masks:
            if m < n_shard:
                late_got.append(flip(*line.behind(late_pieces_out[m]), "shard", m))

    late_exchange(1)
    out_parts = line(
        functools.partial(out_grad_kernel, n_shard),
        "out_grad",
        tuple(
            shape((n_shard * half, 2 * COLS), f32 if m == 0 else bf16) for m in range(CHIPS)
        ),
        (),
        (*heads, grad_branch),
        (pltpu.VMEM((CHIPS, own, COLS), bf16), pltpu.VMEM((D, COLS), f32)),
    )
    line.wait(*grad_heads)
    out_parts = list(line.behind(*out_parts))
    late_exchange(2)
    outs = (
        shape((tokens, COLS)),
        shape((keys, COLS), bf16 if rest == 1 else f32),
        shape((keys, COLS), bf16 if rest == 1 else f32),
        shape((8, COLS), f32),
    )
    scratch = (
        pltpu.VMEM((HEADS_HERE, tokens, HEAD_DIM), bf16),
        pltpu.VMEM((HEADS_HERE, tokens, HEAD_DIM), f32),
        pltpu.VMEM((HEADS_HERE, keys, HEAD_DIM), f32),
        pltpu.VMEM((HEADS_HERE, keys, HEAD_DIM), f32),
    )
    if rest == 1:
        grad_query, grad_key, grad_value, qv_sums = line(
            functools.partial(causal_back_kernel, tile=own),
            "attend_back",
            outs,
            (block_of,),
            (query, key, value, *grad_heads, lse),
            scratch,
            limit=28,
        )
    else:
        grad_query, grad_key, grad_value, qv_sums = line(
            functools.partial(attend_back_kernel, tile=own),
            "attend_back",
            outs,
            (),
            (query, key, value, *grad_heads, lse, *positions),
            scratch,
            limit=56,
            bare=True,
        )
    grad_key, grad_value = rest_scatter(grad_key), rest_scatter(grad_value)
    line.wait(late_got[-1])
    mine, table, send = line(
        functools.partial(early_grad_kernel, n_shard),
        "early_grad",
        (
            shape((n_shard * half, D), f32),
            shape((VEC_ROWS, D), f32),
            shape((n_shard * half + 2 * VEC_ROWS, D)),
        ),
        (),
        (
            x_own,
            x_oth,
            grad_query,
            grad_key,
            grad_value,
            *exchange(out_parts, "chip"),
            branch_sums,
            loss_sums,
            res_sums,
            *b1_sums,
            qv_sums,
        ),
        (pltpu.VMEM((D, D), f32),),
        limit=20,
    )
    parts = line(
        qkv_back_kernel,
        "qkv_back",
        tuple(shape((own, D), f32 if m == 0 else bf16) for m in range(CHIPS)),
        (),
        (grad_query, grad_key, grad_value, w_qkv),
        bare=True,
    )
    pieces = line(
        functools.partial(early_split_kernel, n_shard),
        "early_split",
        tuple(
            shape((half + 2 * VEC_ROWS, D), f32 if m == 0 else bf16) for m in range(n_shard)
        ),
        (),
        (mine, table, swap(send)),
    )
    late_exchange(*range(3, n_shard))
    parts = line.behind(*parts)
    early = line(
        early_sum_kernel,
        "early_sum",
        shape((half + 2 * VEC_ROWS, D)),
        (),
        exchange(pieces, "shard"),
        bare=True,
    )
    if rest > 1:
        early = line(
            early_sum_kernel, "rest_sum", shape(early.shape), (), gather(early, "rest"), bare=True
        )
    here, there = line(
        hidden_kernel,
        "hidden",
        (shape((rows, D), f32), shape((rows, D), f32)),
        (),
        (grad_res, *exchange(parts, "chip")),
        bare=True,
    )
    late = line(sum_kernel, "late_sum", shape((each, HALF)), (), late_got, bare=True)
    if rest > 1:
        late = line(sum_kernel, "rest_sum", shape(late.shape), (), gather(late, "rest"), bare=True)
    late = gather(late, "chip")
    grad_hidden = to_owners(here, there)
    early = gather(early, "chip")
    attn_grad, vec_grad, query_grad, stats = line(
        functools.partial(early_final_kernel, n_shard),
        "early_final",
        (
            shape(attn_latent.shape, f32),
            shape((7 + FF // D, D), f32),
            shape((1, D), f32),
            shape((1, 128), f32),
        ),
        (lengths,),
        (*early, *[swap(piece) for piece in early], attn_latent),
        (
            pltpu.VMEM((GROUP, half, D), bf16),
            pltpu.VMEM((CHIPS, VEC_ROWS, D), f32),
            pltpu.VMEM((8, D), f32),
        ),
    )
    in_grad, down_grad = line(
        functools.partial(late_final_kernel, n_shard),
        "late_final",
        (shape(ffn_in_latent.shape, f32), shape(ffn_out_latent.shape, f32)),
        (),
        (*late, *[swap(piece) for piece in late], ffn_in_latent, ffn_out_latent),
        (pltpu.VMEM((GROUP, each, HALF), bf16),),
    )
    return (
        output,
        stats[0, :4],
        grad_hidden,
        attn_grad,
        in_grad,
        down_grad,
        vec_grad,
        query_grad[0],
    )


def solution(mesh):
    n_ctx, n_shard = mesh.shape["ctx"], mesh.shape["shard"]
    places = mesh.devices.reshape(n_ctx // GROUP, CHIPS, CORES, n_shard)
    inner = Mesh(places, ("rest", "chip", "core", "shard"))
    ctx = ("rest", "chip", "core")
    in_specs = (
        P("shard", ctx, None),
        P(),
        P(),
        P(None, "shard", None),
        P("shard", None),
        P("shard", None),
        P(),
        P(None, "shard", None),
        P("shard", None),
        P("shard", None),
        P(),
    )
    out_specs = (
        P("shard", ctx, None),
        P(),
        P("shard", ctx, None),
        P(None, "shard", None),
        P("shard", None),
        P("shard", None),
        P(),
        P(),
    )
    return jax.shard_map(
        body, mesh=inner, in_specs=in_specs, out_specs=out_specs, check_vma=False
    )
```
